32 devices in a mesh: seq: 4 (over z), expert: 8 (over y, x, core).
Axes of the slice: x: 2, y: 2, z: 4, core: 2. Of those that a mesh axis runs over, the one named last changes fastest.
Arguments:
- residual: bfloat16 [8, 512, 2048], P('expert', 'seq'), may hold values from -6 to 6
- queries: bfloat16 [8, 512, 2048], P('expert', 'seq'), may hold values from -400 to 400
- key_input: bfloat16 [8, 512, 512], P('expert', 'seq'), may hold values from -4 to 4
- value_input: bfloat16 [8, 512, 512], P('expert', 'seq'), may hold values from -6 to 6
- routes: int32 [8, 512, 6], P('expert', 'seq'), may hold values from 0 to 15, all different within a row; in each aligned block of 128 rows (0 to 127, 128 to 255, ..., all dimensions but the last counted through in order) at most 60 rows name the same one
- mix_weights: float32 [8, 512, 6], P('expert', 'seq'), may hold values from 0.1 to 1
- gate_weight: bfloat16 [16, 2048, 704], P('expert'), may hold values from -0.125 to 0.125
- up_weight: bfloat16 [16, 2048, 704], P('expert'), may hold values from -0.125 to 0.125
- down_weight: bfloat16 [16, 704, 2048], P('expert'), may hold values from -0.21875 to 0.21875
- grad_out: bfloat16 [8, 512, 2048], P('expert', 'seq'), may hold values from -6 to 6
Outputs:
- layer_out: bfloat16 [8, 512, 2048], P('expert', 'seq')
- residual_grad: bfloat16 [8, 512, 2048], P('expert', 'seq')
- query_grad: bfloat16 [8, 512, 2048], P('expert', 'seq')
- key_grad: bfloat16 [8, 512, 512], P('expert', 'seq')
- value_grad: bfloat16 [8, 512, 512], P('expert', 'seq')
- mix_grad: float32 [8, 512, 6], P('expert', 'seq')
- gate_weight_grad: bfloat16 [16, 2048, 704], P('expert', 'seq')
- up_weight_grad: bfloat16 [16, 2048, 704], P('expert', 'seq')
- down_weight_grad: bfloat16 [16, 704, 2048], P('expert', None, 'seq')
The draws below stay inside these ranges and needn't reach their ends.
Inputs may be any that keep to these rules, and one draw needn't show every extreme that they name: `routes`: each row names 6 different experts. Among the rows of one device no expert is named by more than 60 rows, and in every draw some expert is named by exactly 60 rows of some device.
All inputs are finite; a program needn't handle non-finite values.
Results may differ from the reference program's by a relative error of at most 0.04.
Values may be sent and summed in bfloat16 or wider, within the bound.
A program may use at most 192 MiB of HBM per device.

```python
import math
import jax
import jax.numpy as jnp
import numpy as np
from jax import lax

D = 2048
HQ = 16
HK = 4
DH = 128
F = 704
TOPK = 6
TOK_DEV = 128
EXPERTS = 16
SEQS = 8
SEQ_LEN = 512
CAP = 60
N_SEQ = 4


def paired_draws(key):
    key_base = jax.random.fold_in(key, 101)
    query_base = jax.random.fold_in(key, 202)
    key_vectors = jnp.clip(jax.random.normal(key_base, (SEQS, SEQ_LEN, HK, DH), jnp.float32), -4.0, 4.0)
    query_vectors = jnp.clip(jax.random.normal(query_base, (SEQS, SEQ_LEN, HQ, DH), jnp.float32), -4.0, 4.0)
    query_out = query_vectors.reshape(SEQS, SEQ_LEN, HQ * DH).astype(jnp.bfloat16)
    key_out = key_vectors.reshape(SEQS, SEQ_LEN, HK * DH).astype(jnp.bfloat16)
    return (query_out, key_out)


def draw_queries(key, part):
    return paired_draws(key)[0]


def draw_key_input(key, part):
    return paired_draws(key)[1]


def shard_levels(stream_key, shape, pieces, low, largest):
    gain = 1.0
    for axis_at, blocks in pieces:
        steps = jax.random.uniform(jax.random.fold_in(jax.random.fold_in(stream_key, 6), axis_at), (blocks,), jnp.float32, low / len(pieces), largest / len(pieces))
        gain = gain * jnp.repeat(jnp.exp(steps), shape[axis_at] // blocks).reshape((-1,) + (1,) * (len(shape) - 1 - axis_at))
    return gain


def routed_block(own_key, own, number, rows, count, top, bound, lean):
    ranking = jax.random.permutation(own_key, count)
    heavy_load, ordinary = portions_of(count, rows * top, bound, lean, True), portions_of(count, rows * top, bound, lean, False)
    places = jnp.arange(count)

    def named(sizes, turn):
        used = int((sizes > 0).sum())
        fixed = max(1, used // 4)
        moved = fixed + (places - fixed + turn * (used - fixed)) % max(1, count - fixed)
        return jnp.zeros((count,), jnp.int32).at[ranking[jnp.where(places < fixed, places, moved)]].set(jnp.asarray(sizes, jnp.int32))

    sizes = jnp.where(number % 4 == 0, named(heavy_load, number // 4), named(ordinary, number - number // 4 - 1))
    mixed = jax.random.permutation(jax.random.fold_in(own, 3), count)
    giver, sink = mixed[0:count // 2 * 2:2], mixed[1:count // 2 * 2:2]
    margin = jnp.minimum(sizes[giver] - 1, bound - sizes[sink]) // 2
    margin = jnp.where((giver == ranking[0]) | (sink == ranking[0]) | (sizes[sink] == 0), 0, jnp.maximum(margin, 0))
    moved = jax.random.randint(jax.random.fold_in(own, 4), (count // 2,), 0, 1 << 20) % (margin + 1)
    sizes = sizes.at[giver].add(-moved).at[sink].add(moved)
    members = jnp.searchsorted(jnp.cumsum(sizes), jnp.arange(rows * top), side="right").astype(jnp.int32)
    grid = members.reshape(top, rows).T
    grid = grid[jax.random.permutation(jax.random.fold_in(own, 1), rows)]
    turn = jax.random.randint(jax.random.fold_in(own, 2), (rows, 1), 0, top)
    return jnp.take_along_axis(grid, (jnp.arange(top)[None, :] + turn) % top, axis=1)


def portions_of(amount, total, most, slope, full):
    portions = [(1 << 20) // math.isqrt(standing ** slope) + 1 for standing in range(1, amount + 1)]
    largest = most if full else min(most, max(-(-total // amount), total * portions[0] // sum(portions)))
    least = 1 if total - largest >= amount - 1 else 0
    given, surplus = [largest] + [least] * (amount - 1), total - largest - least * (amount - 1)
    while surplus > 0:
        candidates = [i for i in range(1, amount) if given[i] < largest] or [i for i in range(1, amount) if given[i] < most]
        whole, left = sum([portions[i] for i in candidates]), surplus
        for i in candidates:
            more = min(most - given[i], max(1, left * portions[i] // whole), surplus)
            given[i] = given[i] + more
            surplus = surplus - more
    return np.array(given)


def centred(stream_key, dims, deviation, bound, split=(), held_as=jnp.bfloat16):
    values = deviation * jax.random.normal(stream_key, dims, jnp.float32)
    if split:
        values = values * shard_levels(stream_key, dims, split, -0.22, 0.18)
    return jnp.clip(values, -bound, bound).astype(held_as)


def setup_inputs(seed: int = 0) -> dict:
    splits = jax.random.split(jax.random.key(seed), 11)
    residual = centred(splits[0], (SEQS, SEQ_LEN, D), 1.0, 6.0, ((0, 8), (1, 4)))
    queries = draw_queries(jax.random.fold_in(splits[10], 71), 0)
    key_input = draw_key_input(jax.random.fold_in(splits[10], 71), 0)
    value_input = centred(splits[3], (SEQS, SEQ_LEN, HK * DH), 1.0, 6.0, ((0, 8), (1, 4)))
    routes_keys = jax.random.split(jax.random.fold_in(splits[4], 1), SEQS * SEQ_LEN // TOK_DEV)
    routes_turns = jax.random.permutation(jax.random.fold_in(splits[4], 3), SEQS * SEQ_LEN // TOK_DEV)
    routes = jax.vmap(lambda own, number: routed_block(jax.random.fold_in(splits[4], 2), own, number, TOK_DEV, EXPERTS, TOPK, CAP, 2))(routes_keys, routes_turns).reshape((SEQS, SEQ_LEN, TOPK))
    mix_weights = jnp.clip(jnp.exp(math.log(1.0) - 2.3025851 * jax.random.uniform(splits[5], (SEQS, SEQ_LEN, TOPK), jnp.float32) ** shard_levels(splits[5], (SEQS, SEQ_LEN, TOPK), ((0, 8), (1, 4)), -0.2, 0.2)), 0.1, 1.0)
    gate_weight = centred(splits[6], (EXPERTS, D, F), D ** -0.5, 0.125, ((0, 8),))
    up_weight = centred(splits[7], (EXPERTS, D, F), D ** -0.5, 0.125, ((0, 8),))
    down_weight = centred(splits[8], (EXPERTS, F, D), F ** -0.5, 0.21875, ((0, 8),))
    grad_out = centred(splits[9], (SEQS, SEQ_LEN, D), 1.0, 6.0, ((0, 8), (1, 4)))
    return dict(residual=residual, queries=queries, key_input=key_input, value_input=value_input, routes=routes, mix_weights=mix_weights, gate_weight=gate_weight, up_weight=up_weight, down_weight=down_weight, grad_out=grad_out)


neg_big = -1e+30
norm_eps = 1e-06
highest = lax.Precision.HIGHEST

def round_trip(values):
    return lax.optimization_barrier(values.astype(jnp.bfloat16)).astype(jnp.float32)

def causal_scores(query_seq, key_seq):
    length = query_seq.shape[0]
    group_size = HQ // HK
    query_heads = query_seq.astype(jnp.float32).reshape(length, HK, group_size, DH)
    key_heads = key_seq.astype(jnp.float32).reshape(length, HK, DH)
    scores = jnp.einsum('tkgd,jkd->tkgj', query_heads, key_heads, precision=highest) * (1.0 / math.sqrt(DH))
    positions = jnp.arange(length, dtype=jnp.int32)
    visible = (positions[None, :] <= positions[:, None])[:, None, None, :]
    return (query_heads, key_heads, scores, visible)

def attend_forward(operands):
    query_seq, key_seq, value_seq = operands
    length = query_seq.shape[0]
    query_heads, key_heads, scores, visible = causal_scores(query_seq, key_seq)
    value_heads = value_seq.astype(jnp.float32).reshape(length, HK, DH)
    masked = jnp.where(visible, scores, neg_big)
    row_max = lax.optimization_barrier(jnp.max(masked, axis=3))
    weights = jnp.where(visible, jnp.exp(masked - row_max[..., None]), 0.0)
    row_sum = lax.optimization_barrier(jnp.sum(weights, axis=3))
    mixed = jnp.einsum('tkgj,jkd->tkgd', round_trip(weights), value_heads, precision=highest)
    attention = (mixed / row_sum[..., None]).reshape(length, HQ * DH).astype(jnp.bfloat16)
    return (attention, row_max + jnp.log(row_sum))

def attend_backward(operands):
    query_seq, key_seq, value_seq, attention_seq, total_seq, out_grad_seq = operands
    length = query_seq.shape[0]
    group_size = HQ // HK
    inv_scale = 1.0 / math.sqrt(DH)
    query_heads, key_heads, scores, visible = causal_scores(query_seq, key_seq)
    value_heads = value_seq.astype(jnp.float32).reshape(length, HK, DH)
    probabilities = jnp.where(visible, jnp.exp(scores - total_seq[..., None]), 0.0)
    out_grad = out_grad_seq.astype(jnp.float32).reshape(length, HK, group_size, DH)
    attention_heads = attention_seq.astype(jnp.float32).reshape(length, HK, group_size, DH)
    row_delta = lax.optimization_barrier(jnp.sum(out_grad * attention_heads, axis=3))
    prob_grad = jnp.einsum('tkgd,jkd->tkgj', out_grad, value_heads, precision=highest)
    score_grad = round_trip(probabilities * (prob_grad - row_delta[..., None]))
    query_grad = jnp.einsum('tkgj,jkd->tkgd', score_grad, key_heads, precision=highest) * inv_scale
    blocks_shape = (N_SEQ, TOK_DEV, HK, group_size)
    key_part = jnp.einsum('stkgj,stkgd->sjkd', score_grad.reshape(blocks_shape + (length,)), query_heads.reshape(blocks_shape + (DH,)), precision=highest) * inv_scale
    value_part = jnp.einsum('stkgj,stkgd->sjkd', round_trip(probabilities).reshape(blocks_shape + (length,)), out_grad.reshape(blocks_shape + (DH,)), precision=highest)
    key_grad = lax.optimization_barrier(jnp.sum(round_trip(key_part), axis=0)).reshape(length, HK * DH).astype(jnp.bfloat16)
    value_grad = lax.optimization_barrier(jnp.sum(round_trip(value_part), axis=0)).reshape(length, HK * DH).astype(jnp.bfloat16)
    return (query_grad.reshape(length, HQ * DH).astype(jnp.bfloat16), key_grad, value_grad)

def reference(residual, queries, key_input, value_input, routes, mix_weights, gate_weight, up_weight, down_weight, grad_out):
    attention, log_total = lax.map(attend_forward, (queries, key_input, value_input))
    tokens_all = SEQS * SEQ_LEN
    hidden_flat = (residual.astype(jnp.float32) + attention.astype(jnp.float32)).reshape(tokens_all, D)
    inv_rms = lax.rsqrt(lax.optimization_barrier(jnp.mean(hidden_flat * hidden_flat, axis=1, keepdims=True)) + norm_eps)
    normed = hidden_flat * inv_rms
    normed_bf = normed.astype(jnp.bfloat16)
    blocks = tokens_all // TOK_DEV
    route_blocks = routes.reshape(blocks, TOK_DEV, TOPK)
    onehot = (route_blocks[..., None] == jnp.arange(EXPERTS, dtype=jnp.int32)).astype(jnp.int32)
    per_token = lax.optimization_barrier(jnp.sum(onehot, axis=2))
    earlier = jnp.cumsum(per_token, axis=1) - per_token
    slot_rank = lax.optimization_barrier(jnp.sum(onehot * earlier[:, :, None, :], axis=3))
    position = jnp.arange(blocks, dtype=jnp.int32)[:, None, None] * CAP + slot_rank
    pair_ids = jnp.arange(tokens_all * TOPK, dtype=jnp.int32)
    table = jnp.zeros((EXPERTS, blocks * CAP), jnp.int32).at[route_blocks.reshape(-1), position.reshape(-1)].set(pair_ids)
    alive_table = jnp.zeros((EXPERTS, blocks * CAP), jnp.bool_).at[route_blocks.reshape(-1), position.reshape(-1)].set(True)
    mix_flat = mix_weights.reshape(-1)
    grad_flat = grad_out.reshape(tokens_all, D)

    def forward_step(carried, operands):
        combined, mix_grad = carried
        gate_matrix, up_matrix, down_matrix, pairs, alive = operands
        token_ids = pairs // TOPK
        rows = jnp.where(alive[:, None], normed_bf[token_ids], jnp.zeros((), jnp.bfloat16))
        gate_pre = jnp.dot(rows, gate_matrix, preferred_element_type=jnp.float32)
        up_pre = jnp.dot(rows, up_matrix, preferred_element_type=jnp.float32)
        activation = (jax.nn.silu(gate_pre) * up_pre).astype(jnp.bfloat16)
        output = jnp.dot(activation, down_matrix, preferred_element_type=jnp.float32).astype(jnp.bfloat16)
        weight = jnp.where(alive, mix_flat[pairs], 0.0)
        combined = combined.at[token_ids].add(weight[:, None] * output.astype(jnp.float32))
        inner = lax.optimization_barrier(jnp.sum(grad_flat[token_ids].astype(jnp.float32) * output.astype(jnp.float32), axis=1))
        mix_grad = mix_grad.at[pairs].add(jnp.where(alive, inner, 0.0))
        return ((combined, mix_grad), None)
    (combined, mix_grad), ignored = lax.scan(forward_step, (hidden_flat, jnp.zeros((tokens_all * TOPK,), jnp.float32)), (gate_weight, up_weight, down_weight, table, alive_table))

    def backward_step(normed_grad, operands):
        gate_matrix, up_matrix, down_matrix, pairs, alive = operands
        token_ids = pairs // TOPK
        rows = jnp.where(alive[:, None], normed_bf[token_ids], jnp.zeros((), jnp.bfloat16))
        gate_pre = jnp.dot(rows, gate_matrix, preferred_element_type=jnp.float32)
        up_pre = jnp.dot(rows, up_matrix, preferred_element_type=jnp.float32)
        activation = (jax.nn.silu(gate_pre) * up_pre).astype(jnp.bfloat16)
        weight = jnp.where(alive, mix_flat[pairs], 0.0)
        grad_rows = (weight[:, None] * grad_flat[token_ids].astype(jnp.float32)).astype(jnp.bfloat16)
        act_grad = jnp.dot(grad_rows, down_matrix.T, preferred_element_type=jnp.float32)
        sigmoid = jax.nn.sigmoid(gate_pre)
        gate_grad = (act_grad * up_pre * sigmoid * (1.0 + gate_pre * (1.0 - sigmoid))).astype(jnp.bfloat16)
        up_grad = (act_grad * gate_pre * sigmoid).astype(jnp.bfloat16)
        input_grad = (jnp.dot(gate_grad, gate_matrix.T, preferred_element_type=jnp.float32) + jnp.dot(up_grad, up_matrix.T, preferred_element_type=jnp.float32)).astype(jnp.bfloat16)
        normed_grad = normed_grad.at[token_ids].add(jnp.where(alive[:, None], input_grad.astype(jnp.float32), 0.0))
        rows_split = rows.astype(jnp.float32).reshape(SEQS, N_SEQ, CAP, D)
        gate_split = gate_grad.astype(jnp.float32).reshape(SEQS, N_SEQ, CAP, F)
        up_split = up_grad.astype(jnp.float32).reshape(SEQS, N_SEQ, CAP, F)
        act_split = activation.astype(jnp.float32).reshape(SEQS, N_SEQ, CAP, F)
        grad_split = grad_rows.astype(jnp.float32).reshape(SEQS, N_SEQ, CAP, D)
        gate_part = jnp.einsum('jscd,jscf->sdf', rows_split, gate_split, precision=highest)
        up_part = jnp.einsum('jscd,jscf->sdf', rows_split, up_split, precision=highest)
        down_part = jnp.einsum('jscf,jscd->sfd', act_split, grad_split, precision=highest)
        sums = (lax.optimization_barrier(jnp.sum(round_trip(gate_part), axis=0)).astype(jnp.bfloat16), lax.optimization_barrier(jnp.sum(round_trip(up_part), axis=0)).astype(jnp.bfloat16), lax.optimization_barrier(jnp.sum(round_trip(down_part), axis=0)).astype(jnp.bfloat16))
        return (normed_grad, sums)
    normed_grad, weight_sums = lax.scan(backward_step, jnp.zeros((tokens_all, D), jnp.float32), (gate_weight, up_weight, down_weight, table, alive_table))
    dot_mean = lax.optimization_barrier(jnp.mean(normed_grad * normed, axis=1, keepdims=True))
    hidden_grad = grad_flat.astype(jnp.float32) + inv_rms * (normed_grad - normed * dot_mean)
    residual_grad = hidden_grad.astype(jnp.bfloat16).reshape(SEQS, SEQ_LEN, D)
    query_grad, key_grad, value_grad = lax.map(attend_backward, (queries, key_input, value_input, attention, log_total, residual_grad))
    layer_out = combined.astype(jnp.bfloat16).reshape(SEQS, SEQ_LEN, D)
    return (layer_out, residual_grad, query_grad, key_grad, value_grad, mix_grad.reshape(SEQS, SEQ_LEN, TOPK), weight_sums[0], weight_sums[1], weight_sums[2])
```

```python
import functools
import math

import jax
import jax.numpy as jnp
from jax import lax
from jax.experimental import pallas as pl
from jax.experimental.pallas import tpu as pltpu
from jax.sharding import PartitionSpec as P

DH = 128
neg_big = -1e30
norm_eps = 1e-06
BF = jnp.bfloat16
F32 = jnp.float32
GATHER_BYTES = 32 * 1024 * 1024
MESH = pl.DeviceIdType.MESH
VMEM_LIMIT = 56 * 1024 * 1024


def dot(a, b, ca, cb):
    return lax.dot_general(a, b, (((ca,), (cb,)), ((), ())), preferred_element_type=F32)


def vm():
    return pl.BlockSpec(memory_space=pltpu.VMEM)


def heads_of(ref, first, count):
    return jnp.concatenate(
        [ref[:, (first + g) * DH : (first + g + 1) * DH] for g in range(count)], axis=0
    )


def visible_mask(tokens, group, full, seq_index):
    shape = (group, tokens, full)
    pos = lax.broadcasted_iota(jnp.int32, shape, 1) + seq_index * tokens
    key = lax.broadcasted_iota(jnp.int32, shape, 2)
    return (key <= pos).reshape(group * tokens, full)


def attend_kernel(group, residual, q, kv, att, log_total, inv_rms, normed):
    tokens = q.shape[0]
    full = kv.shape[0]
    kv_heads = kv.shape[1] // (2 * DH)
    visible = visible_mask(tokens, group, full, lax.axis_index("seq"))
    scale = 1.0 / math.sqrt(DH)
    for k in range(kv_heads):
        qh = heads_of(q, k * group, group)
        kh = kv[:, k * DH : (k + 1) * DH]
        vh = kv[:, (kv_heads + k) * DH : (kv_heads + k + 1) * DH]
        scores = jnp.where(visible, dot(qh, kh, 1, 1) * scale, neg_big)
        top = jnp.max(scores, axis=1, keepdims=True)
        weights = jnp.exp(scores - top)
        total = jnp.sum(weights, axis=1, keepdims=True)
        out = (dot(weights.astype(BF), vh, 1, 0) / total).astype(BF)
        logs = top + jnp.log(total)
        for g in range(group):
            h = k * group + g
            att[:, h * DH : (h + 1) * DH] = out[g * tokens : (g + 1) * tokens]
            log_total[:, h : h + 1] = logs[g * tokens : (g + 1) * tokens]
    hidden = residual[...].astype(F32) + att[...].astype(F32)
    inv = lax.rsqrt(jnp.mean(hidden * hidden, axis=1, keepdims=True) + norm_eps)
    inv_rms[...] = inv
    normed[...] = (hidden * inv).astype(BF)


def attend(residual, q, kv, group):
    tokens, width = q.shape
    heads = width // DH
    return pl.pallas_call(
        functools.partial(attend_kernel, group),
        out_shape=(
            jax.ShapeDtypeStruct((tokens, width), BF),
            jax.ShapeDtypeStruct((tokens, heads), F32),
            jax.ShapeDtypeStruct((tokens, 1), F32),
            jax.ShapeDtypeStruct((tokens, width), BF),
        ),
        in_specs=[vm()] * 3,
        out_specs=(vm(),) * 4,
        compiler_params=pltpu.CompilerParams(vmem_limit_bytes=VMEM_LIMIT),
        cost_estimate=pl.CostEstimate(
            flops=4 * tokens * kv.shape[0] * width,
            bytes_accessed=8 * tokens * width + 2 * kv.size,
            transcendentals=heads * tokens * kv.shape[0],
        ),
        name="attend",
    )(residual, q, kv)


def attend_rows(group, residual, q, kv, att, log_total, inv_rms, normed):
    tokens = q.shape[0]
    full = kv.shape[0]
    kv_heads = kv.shape[1] // (2 * DH)
    visible = visible_mask(tokens, group, full, lax.axis_index("seq"))
    scale = 1.0 / math.sqrt(DH)
    for k in range(kv_heads):
        qh = heads_of(q, k * group, group)
        kh = kv[:, k * DH : (k + 1) * DH]
        vh = kv[:, (kv_heads + k) * DH : (kv_heads + k + 1) * DH]
        scores = jnp.where(visible, dot(qh, kh, 1, 1) * scale, neg_big)
        top = jnp.max(scores, axis=1, keepdims=True)
        weights = jnp.exp(scores - top)
        total = jnp.sum(weights, axis=1, keepdims=True)
        out = (dot(weights.astype(BF), vh, 1, 0) / total).astype(BF)
        logs = top + jnp.log(total)
        for g in range(group):
            h = k * group + g
            att[:, h * DH : (h + 1) * DH] = out[g * tokens : (g + 1) * tokens]
            log_total[:, h : h + 1] = logs[g * tokens : (g + 1) * tokens]
    hidden = residual[...].astype(F32) + att[...].astype(F32)
    inv = lax.rsqrt(jnp.mean(hidden * hidden, axis=1, keepdims=True) + norm_eps)
    inv_rms[...] = inv
    normed[...] = (hidden * inv).astype(BF)


def front_kernel(
    group,
    seqs,
    residual,
    q,
    kv_mine,
    table,
    grads,
    att,
    log_total,
    inv_rms,
    kv_all,
    grads_all,
    normed_all,
    tables,
    kv,
    normed,
    local_sem,
    kv_sem,
    line_sem,
    plane_sem,
    table_line_sem,
    table_plane_sem,
):
    z = lax.axis_index("seq")
    e = lax.axis_index("expert")
    c, x, y = lax.rem(e, 2), lax.rem(e // 2, 2), e // 4
    tokens = q.shape[0]
    half = tokens // 2
    sibling = {"expert": e + 1 - 2 * c}
    across_x = {"expert": e + 2 - 4 * x}
    across_y = {"expert": e + 4 - 8 * y}
    above, below = {"seq": z + 1}, {"seq": z - 1}
    top = seqs - 1
    arrays = (grads_all, normed_all)
    sends = []

    def copy_of(view, sems, device):
        return pltpu.make_async_remote_copy(
            src_ref=view,
            dst_ref=view,
            send_sem=sems.at[0],
            recv_sem=sems.at[1],
            device_id=device,
            device_id_type=MESH,
        )

    def send(guard, view, sems, device):
        copy_of(view(), sems(), device).start()
        sends.append((guard, lambda: copy_of(view(), sems(), device).wait_send()))

    def arrived(view, sems):
        copy_of(view, sems, sibling).wait_recv()

    def under(guard, body):
        if guard is True:
            body()
        else:
            pl.when(guard)(body)

    def plane(k):
        d = (k + 1) // 2
        return z if k == 0 else (z - d if k % 2 else z + d)

    def present(k):
        d = (k + 1) // 2
        return True if k == 0 else (z >= d if k % 2 else z + d <= top)

    def forwarded(k):
        d = (k + 1) // 2
        return z + 1 <= top if k % 2 else z >= 1

    def both(a, b):
        return b if a is True else (a if b is True else jnp.logical_and(a, b))

    def line_start(ref, sems, k):
        guard = both(present(k - 2) if k > 2 else True, forwarded(k))

        def block():
            return ref.at[plane(k - 2) if k > 2 else z, y, x, c]

        under(guard, lambda: send(guard, block, lambda: sems(k), above if k % 2 else below))

    def first(a, k):
        ref = arrays[a]

        def sems(i):
            return plane_sem.at[a, k, i]

        if k:

            def take():
                arrived(ref.at[plane(k), y, x, c], line_sem.at[a, k])
                if a == 0:
                    arrived(tables.at[plane(k), y, x, c], table_line_sem.at[k])

            under(present(k), take)
            if k + 2 <= 2 * top:
                line_start(ref, lambda j: line_sem.at[a, j], k + 2)
                if a == 0:
                    line_start(tables, lambda j: table_line_sem.at[j], k + 2)

        def start():
            send(k, lambda: ref.at[plane(k), y, x, c, :half], lambda: sems(0), across_x)
            send(k, lambda: ref.at[plane(k), y, x, c, half:], lambda: sems(1), across_y)
            if a == 0:
                send(
                    k,
                    lambda: tables.at[plane(k), y, x, c],
                    lambda: table_plane_sem.at[k, 0],
                    across_x,
                )

        under(present(k), start)

    def second(a, k):
        ref = arrays[a]

        def sems(i):
            return plane_sem.at[a, k, i]

        def step():
            p = plane(k)
            arrived(ref.at[p, y, 1 - x, c, :half], sems(0))
            send(k, lambda: ref.at[plane(k), y, :, c, :half], lambda: sems(2), across_y)
            arrived(ref.at[p, 1 - y, x, c, half:], sems(1))
            send(k, lambda: ref.at[plane(k), :, x, c, half:], lambda: sems(3), across_x)
            if a == 0:
                arrived(tables.at[p, y, 1 - x, c], table_plane_sem.at[k, 0])
                send(
                    k,
                    lambda: tables.at[plane(k), y, :, c],
                    lambda: table_plane_sem.at[k, 1],
                    across_y,
                )

        under(present(k), step)

    def third(a, k):
        ref = arrays[a]

        def sems(i):
            return plane_sem.at[a, k, i]

        def step():
            p = plane(k)
            arrived(ref.at[p, 1 - y, :, c, :half], sems(2))
            arrived(ref.at[p, :, 1 - x, c, half:], sems(3))
            send(k, lambda: ref.at[plane(k), :, :, c], lambda: sems(4), sibling)
            if a == 0:
                arrived(tables.at[p, 1 - y, :, c], table_plane_sem.at[k, 1])
                send(
                    k,
                    lambda: tables.at[plane(k), :, :, c],
                    lambda: table_plane_sem.at[k, 2],
                    sibling,
                )

        under(present(k), step)

    def fourth(a, k):
        def step():
            p = plane(k)
            arrived(arrays[a].at[p, :, :, 1 - c], plane_sem.at[a, k, 4])
            if a == 0:
                arrived(tables.at[p, :, :, 1 - c], table_plane_sem.at[k, 2])

        under(present(k), step)

    copies = [
        pltpu.make_async_copy(grads, grads_all.at[z, y, x, c], local_sem.at[0]),
        pltpu.make_async_copy(table, tables.at[z, y, x, c], local_sem.at[1]),
        pltpu.make_async_copy(kv_mine, kv.at[z], local_sem.at[2]),
    ]
    for copy in copies:
        copy.start()
    for j in range(1, seqs):

        @pl.when(j > z)
        def _():
            kv[j] = jnp.zeros(kv.shape[1:], BF)

    barrier = pltpu.get_barrier_semaphore()
    for device in (sibling, across_x, across_y):
        pl.semaphore_signal(barrier, inc=1, device_id=device, device_id_type=MESH)

    @pl.when(z < top)
    def _():
        pl.semaphore_signal(barrier, inc=1, device_id=above, device_id_type=MESH)

    @pl.when(z > 0)
    def _():
        pl.semaphore_signal(barrier, inc=1, device_id=below, device_id_type=MESH)

    pl.semaphore_wait(barrier, 3 + (z < top).astype(jnp.int32) + (z > 0).astype(jnp.int32))
    for copy in copies:
        copy.wait()

    def kv_start(d):
        guard = both(z >= d if d else True, z < top)
        under(guard, lambda: send(guard, lambda: kv.at[z - d], lambda: kv_sem.at[d + 1], above))

    def kv_take(d):
        @pl.when(z >= d)
        def _():
            arrived(kv.at[z - d], kv_sem.at[d])

    kv_start(0)
    line_start(grads_all, lambda j: line_sem.at[0, j], 2)
    line_start(tables, lambda j: table_line_sem.at[j], 2)
    line_start(tables, lambda j: table_line_sem.at[j], 1)
    first(0, 0)
    for d in range(1, seqs):
        kv_take(d)
        if d < top:
            kv_start(d)
        if d == 1:
            second(0, 0)
        if d == 2:
            third(0, 0)
    line_start(grads_all, lambda j: line_sem.at[0, j], 1)
    keys = kv[...].reshape(seqs * tokens, kv.shape[2])
    attend_rows(group, residual, q, keys, att, log_total, inv_rms, normed)
    keep = [
        pltpu.make_async_copy(normed, normed_all.at[z, y, x, c], local_sem.at[3]),
        pltpu.make_async_copy(kv, kv_all, local_sem.at[4]),
    ]
    for copy in keep:
        copy.start()
    keep[0].wait()
    line_start(normed_all, lambda j: line_sem.at[1, j], 1)
    line_start(normed_all, lambda j: line_sem.at[1, j], 2)
    order = [(1, 0)]
    for d in range(1, seqs):
        for a in range(2):
            order += [(a, 2 * d - 1), (a, 2 * d)]
    for i in range(len(order) + 4):
        if i < len(order):
            first(*order[i])
        if 0 <= i - 2 < len(order):
            second(*order[i - 2])
        if 0 <= i - 4 < len(order):
            third(*order[i - 4])
    keep[1].wait()
    for a, k in [(0, 0)] + order:
        fourth(a, k)
    for guard, finish in sends:
        under(present(guard) if isinstance(guard, int) else guard, finish)


def front(residual, q, kv_mine, table, grads, group, seqs):
    tokens, width = q.shape
    heads = width // DH
    slots = 2 * seqs - 1
    any_space = pl.BlockSpec(memory_space=pl.ANY)
    dma = pltpu.SemaphoreType.DMA
    return pl.pallas_call(
        functools.partial(front_kernel, group, seqs),
        out_shape=(
            jax.ShapeDtypeStruct((tokens, width), BF),
            jax.ShapeDtypeStruct((tokens, heads), F32),
            jax.ShapeDtypeStruct((tokens, 1), F32),
            jax.ShapeDtypeStruct((seqs,) + kv_mine.shape, BF),
            jax.ShapeDtypeStruct((seqs, 2, 2, 2, tokens, width), BF),
            jax.ShapeDtypeStruct((seqs, 2, 2, 2, tokens, width), BF),
            jax.ShapeDtypeStruct((seqs, 2, 2, 2) + table.shape, F32),
        ),
        in_specs=[vm()] * 5,
        out_specs=(vm(),) * 3 + (any_space,) * 4,
        scratch_shapes=[
            pltpu.VMEM((seqs,) + kv_mine.shape, BF),
            pltpu.VMEM((tokens, width), BF),
            dma((5,)),
            dma((seqs, 2)),
            dma((2, slots, 2)),
            dma((2, slots, 5, 2)),
            dma((slots, 2)),
            dma((slots, 3, 2)),
        ],
        compiler_params=pltpu.CompilerParams(
            collective_id=0, has_side_effects=True, vmem_limit_bytes=VMEM_LIMIT
        ),
        cost_estimate=pl.CostEstimate(
            flops=4 * tokens * seqs * tokens * width,
            bytes_accessed=32 * seqs * tokens * width,
            transcendentals=heads * tokens * seqs * tokens,
        ),
        name="front",
    )(residual, q, kv_mine, table, grads)


def attend_back_kernel(
    group, residual, q, kv, att, log_total, inv_rms, grad_out, normed_grad, res_grad, q_grad, kv_part
):
    tokens = q.shape[0]
    full = kv.shape[0]
    kv_heads = kv.shape[1] // (2 * DH)
    scale = 1.0 / math.sqrt(DH)
    inv = inv_rms[...]
    normed = (residual[...].astype(F32) + att[...].astype(F32)) * inv
    ngrad = normed_grad[...].astype(F32)
    dot_mean = jnp.mean(ngrad * normed, axis=1, keepdims=True)
    res_grad[...] = (grad_out[...].astype(F32) + inv * (ngrad - normed * dot_mean)).astype(BF)
    visible = visible_mask(tokens, group, full, lax.axis_index("seq"))
    for k in range(kv_heads):
        qh = heads_of(q, k * group, group)
        oh = heads_of(att, k * group, group)
        gh = heads_of(res_grad, k * group, group)
        logs = jnp.concatenate(
            [log_total[:, k * group + g : k * group + g + 1] for g in range(group)], axis=0
        )
        kh = kv[:, k * DH : (k + 1) * DH]
        vh = kv[:, (kv_heads + k) * DH : (kv_heads + k + 1) * DH]
        scores = jnp.where(visible, dot(qh, kh, 1, 1) * scale, neg_big)
        probs = jnp.exp(scores - logs)
        delta = jnp.sum(gh.astype(F32) * oh.astype(F32), axis=1, keepdims=True)
        pgrad = dot(gh, vh, 1, 1)
        sgrad = (probs * (pgrad - delta)).astype(BF)
        dq = (dot(sgrad, kh, 1, 0) * scale).astype(BF)
        for g in range(group):
            h = k * group + g
            q_grad[:, h * DH : (h + 1) * DH] = dq[g * tokens : (g + 1) * tokens]
        kv_part[:, k * DH : (k + 1) * DH] = (dot(sgrad, qh, 0, 0) * scale).astype(BF)
        kv_part[:, (kv_heads + k) * DH : (kv_heads + k + 1) * DH] = dot(
            probs.astype(BF), gh, 0, 0
        ).astype(BF)


def attend_back(group, residual, q, kv, att, log_total, inv_rms, grad_out, normed_grad):
    tokens, width = q.shape
    return pl.pallas_call(
        functools.partial(attend_back_kernel, group),
        out_shape=(
            jax.ShapeDtypeStruct((tokens, width), BF),
            jax.ShapeDtypeStruct((tokens, width), BF),
            jax.ShapeDtypeStruct(kv.shape, BF),
        ),
        in_specs=[vm()] * 8,
        out_specs=(vm(),) * 3,
        compiler_params=pltpu.CompilerParams(vmem_limit_bytes=VMEM_LIMIT),
        cost_estimate=pl.CostEstimate(
            flops=10 * tokens * kv.shape[0] * width,
            bytes_accessed=14 * tokens * width + 4 * kv.size,
            transcendentals=tokens * kv.shape[0] * (width // DH),
        ),
        name="attend_back",
    )(residual, q, kv, att, log_total, inv_rms, grad_out, normed_grad)


def pick_kernel(seq_index, slot, rows, picked):
    local = slot.shape[2]
    depth = picked.shape[1]
    tokens = rows.shape[2]
    row = lax.broadcasted_iota(jnp.int32, (depth, tokens), 0)
    for e in range(local):
        chosen = (slot[0, 0, e : e + 1, :] == row).astype(F32).astype(BF)
        picked[e] = dot(chosen, rows[0, 0], 1, 0).astype(BF)


def pick_rows(gathered, slot, seq_index, first, planes, depth):
    seqs, ranks, tokens, width = gathered.shape
    local = slot.shape[2]
    count = planes * ranks

    def source(i, s):
        return (lax.rem(s[0] + first + i // ranks, seqs), lax.rem(i, ranks), 0, 0)

    return pl.pallas_call(
        pick_kernel,
        out_shape=jax.ShapeDtypeStruct((local, count * depth, width), BF),
        grid_spec=pltpu.PrefetchScalarGridSpec(
            num_scalar_prefetch=1,
            grid=(count,),
            in_specs=[
                pl.BlockSpec((1, 1, local, tokens), source),
                pl.BlockSpec((1, 1, tokens, width), source),
            ],
            out_specs=pl.BlockSpec((local, depth, width), lambda i, s: (0, i, 0)),
        ),
        compiler_params=pltpu.CompilerParams(vmem_limit_bytes=16 * 1024 * 1024),
        cost_estimate=pl.CostEstimate(
            flops=2 * local * count * depth * tokens * width,
            bytes_accessed=2 * count * (tokens + local * depth) * width,
            transcendentals=0,
        ),
        name="pick_rows",
    )(seq_index, slot, gathered)


def spread_kernel(slot, rows, out):
    ranks, local, tokens = slot.shape
    depth = rows.shape[1]
    row = lax.broadcasted_iota(jnp.int32, (depth, tokens), 0)
    total = None
    for e in range(local):
        chosen = (slot[0, e : e + 1, :] == row).astype(F32).astype(BF)
        part = dot(chosen, rows[e], 0, 0)
        total = part if total is None else total + part
    out[0] = total.astype(BF)


def spread_rows(rows, slot):
    ranks, local, tokens = slot.shape
    width = rows.shape[2]
    depth = rows.shape[1] // ranks
    return pl.pallas_call(
        spread_kernel,
        out_shape=jax.ShapeDtypeStruct((ranks, tokens, width), BF),
        grid=(ranks,),
        in_specs=[
            pl.BlockSpec((1, local, tokens), lambda i: (i, 0, 0)),
            pl.BlockSpec((local, depth, width), lambda i: (0, i, 0)),
        ],
        out_specs=pl.BlockSpec((1, tokens, width), lambda i: (i, 0, 0)),
        compiler_params=pltpu.CompilerParams(vmem_limit_bytes=16 * 1024 * 1024),
        cost_estimate=pl.CostEstimate(
            flops=2 * local * ranks * depth * tokens * width,
            bytes_accessed=2 * ranks * (tokens + local * depth) * width,
            transcendentals=0,
        ),
        name="spread_rows",
    )(slot, rows)


def hidden_units(rows, grads, mix, gate_weight, up_weight, down_weight):
    gate_pre = jnp.einsum("erd,edf->erf", rows, gate_weight, preferred_element_type=F32)
    up_pre = jnp.einsum("erd,edf->erf", rows, up_weight, preferred_element_type=F32)
    raw = jnp.einsum("erd,efd->erf", grads, down_weight, preferred_element_type=F32)
    sigmoid = jax.nn.sigmoid(gate_pre)
    silu = gate_pre * sigmoid
    act = silu * up_pre
    act_grad = raw * mix[:, :, None]
    gate_grad = (act_grad * up_pre * sigmoid * (1.0 + gate_pre * (1.0 - sigmoid))).astype(BF)
    up_grad = (act_grad * silu).astype(BF)
    mixed = (act * mix[:, :, None]).astype(BF)
    return (gate_grad, up_grad, mixed, act, raw)


def on_device(
    residual,
    queries,
    key_input,
    value_input,
    routes,
    mix_weights,
    gate_weight,
    up_weight,
    down_weight,
    grad_out,
):
    tokens = residual.shape[1]
    width = residual.shape[2]
    kv_width = key_input.shape[2]
    group = queries.shape[2] // kv_width
    local = gate_weight.shape[0]
    ranks = lax.axis_size("expert")
    seqs = lax.axis_size("seq")
    experts = local * ranks
    top_count = routes.shape[2]
    capacity = tokens * top_count * 5 // (4 * experts)
    depth = -(-capacity // 16) * 16
    both = ("seq", "expert")
    both_size = seqs * ranks
    seq_index = lax.axis_index("seq")
    rank_index = lax.axis_index("expert")
    seq_array = seq_index.astype(jnp.int32).reshape(1)

    kv_mine = jnp.concatenate(
        [key_input.reshape(tokens, kv_width), value_input.reshape(tokens, kv_width)], axis=1
    )
    expert_ids = jnp.arange(experts, dtype=jnp.int32)
    picked = routes.reshape(tokens, top_count)
    mix_rows = mix_weights.reshape(tokens, top_count)
    hit = picked[None, :, :] == expert_ids[:, None, None]
    table = jnp.sum(jnp.where(hit, mix_rows[None], 0.0), axis=2) - (
        1.0 - jnp.sum(hit.astype(F32), axis=2)
    )
    grad_rows = grad_out.reshape(tokens, width)
    q = queries.reshape(tokens, width)
    res = residual.reshape(tokens, width)
    paired = ranks == 8 and 2 * both_size * grad_rows.size <= GATHER_BYTES
    if paired:
        att, log_total, inv_rms, kv, grads_all, normed_all, tables = front(
            res, q, kv_mine, table, grad_rows, group, seqs
        )
        kv = kv.reshape(seqs * tokens, 2 * kv_width)
        grads_all = grads_all.reshape(seqs, ranks, tokens, width)
        normed_all = normed_all.reshape(seqs, ranks, tokens, width)
        tables = tables.reshape(seqs * ranks, experts, tokens)
    else:
        kv = lax.all_gather(kv_mine, "seq", axis=0, tiled=True)
        tables = lax.all_gather(table, both, axis=0, tiled=False)
        grads_all = lax.all_gather(grad_rows, both, axis=0, tiled=True)
        grads_all = grads_all.reshape(seqs, ranks, tokens, width)
        att, log_total, inv_rms, normed_bf = attend(res, q, kv, group)
    mine = lax.dynamic_slice_in_dim(tables, rank_index * local, local, axis=1)
    routed = mine >= 0.0
    before = jnp.triu(jnp.ones((tokens, tokens), BF), 1)
    rank = jnp.einsum("bet,tu->beu", routed.astype(BF), before, preferred_element_type=F32)
    slot = jnp.where(routed, rank.astype(jnp.int32), -1)
    slot = slot.reshape(seqs, ranks, local, tokens)
    mine = mine.reshape(seqs, ranks, local, tokens)

    grads_own = pick_rows(grads_all, slot, seq_array, 0, 1, depth)
    grads_far = pick_rows(grads_all, slot, seq_array, 1, seqs - 1, depth)
    if not paired:
        normed_bf, grads_own, grads_far = lax.optimization_barrier(
            (normed_bf, grads_own, grads_far)
        )
        normed_all = lax.all_gather(normed_bf, both, axis=0, tiled=True)
        normed_all = normed_all.reshape(seqs, ranks, tokens, width)

    slot_turned = jnp.roll(slot, -seq_index, axis=0)
    mix_turned = jnp.roll(mine, -seq_index, axis=0)
    here = slot_turned[..., None, :] == jnp.arange(depth, dtype=jnp.int32)[:, None]
    mix_slot = jnp.sum(jnp.where(here, mix_turned[..., None, :], 0.0), axis=4)
    mix_slot = jnp.transpose(mix_slot, (2, 0, 1, 3)).reshape(local, seqs * ranks * depth)
    own = ranks * depth

    rows_own = pick_rows(normed_all, slot, seq_array, 0, 1, depth)
    rows_far = pick_rows(normed_all, slot, seq_array, 1, seqs - 1, depth)
    weights = (gate_weight, up_weight, down_weight)
    gate_own, up_own, mixed_own, act_own, raw_own = hidden_units(
        rows_own, grads_own, mix_slot[:, :own], *weights
    )
    input_grad = (
        jnp.einsum("erf,edf->erd", gate_own, gate_weight, preferred_element_type=F32)
        + jnp.einsum("erf,edf->erd", up_own, up_weight, preferred_element_type=F32)
    ).astype(BF)
    slot_own = slot_turned[0]
    input_part = spread_rows(input_grad, slot_own).reshape(ranks * tokens, width)
    normed_grad = lax.psum_scatter(input_part, "expert", scatter_dimension=0, tiled=True)

    expert_out = jnp.einsum(
        "erf,efd->erd", mixed_own, down_weight, preferred_element_type=F32
    ).astype(BF)
    out_part = spread_rows(expert_out, slot_own).reshape(ranks * tokens, width)
    routed_out = lax.psum_scatter(out_part, "expert", scatter_dimension=0, tiled=True)
    hidden = res.astype(F32) + att.astype(F32)
    layer_out = (hidden + routed_out.astype(F32)).astype(BF)

    pair_dot = jnp.sum(act_own.astype(BF).astype(F32) * raw_own, axis=2)
    pair_dot = pair_dot.reshape(local, ranks, depth)
    token_dot = jnp.sum(
        jnp.where(here[0], jnp.transpose(pair_dot, (1, 0, 2))[..., None], 0.0), axis=2
    )
    dots = lax.all_to_all(token_dot, "expert", split_axis=0, concat_axis=0, tiled=True)
    dots = dots.reshape(experts, tokens)
    mix_grad = jnp.sum(jnp.where(hit, dots[:, :, None], 0.0), axis=0)

    gate_far, up_far, mixed_far, _, _ = hidden_units(
        rows_far, grads_far, mix_slot[:, own:], *weights
    )
    share = width // seqs

    def columns(array):
        return lax.dynamic_slice_in_dim(array, seq_index * share, share, axis=2)

    def outer(a_own, a_far, b_own, b_far):
        return (
            jnp.einsum("erm,ern->emn", a_own, b_own, preferred_element_type=F32)
            + jnp.einsum("erm,ern->emn", a_far, b_far, preferred_element_type=F32)
        ).astype(BF)

    cols_own, cols_far = columns(rows_own), columns(rows_far)
    gate_share = outer(cols_own, cols_far, gate_own, gate_far)
    up_share = outer(cols_own, cols_far, up_own, up_far)
    down_share = outer(mixed_own, mixed_far, columns(grads_own), columns(grads_far))

    res_grad, q_grad, kv_part = attend_back(
        group, res, q, kv, att, log_total, inv_rms, grad_rows, normed_grad
    )
    kv_share = lax.psum_scatter(kv_part, "seq", scatter_dimension=0, tiled=True)
    return (
        layer_out.reshape(1, tokens, width),
        res_grad.reshape(1, tokens, width),
        q_grad.reshape(1, tokens, width),
        kv_share[:, :kv_width].reshape(1, tokens, kv_width),
        kv_share[:, kv_width:].reshape(1, tokens, kv_width),
        mix_grad.reshape(1, tokens, top_count),
        gate_share,
        up_share,
        down_share,
    )


def solution(mesh):
    rows = P("expert", "seq", None)
    weight = P("expert", None, None)
    return jax.shard_map(
        on_device,
        mesh=mesh,
        in_specs=(rows,) * 6 + (weight,) * 3 + (rows,),
        out_specs=(rows,) * 8 + (P("expert", None, "seq"),),
        check_vma=False,
    )
```

```python
import functools
import math

import jax
import jax.numpy as jnp
from jax import lax
from jax.experimental import pallas as pl
from jax.experimental.pallas import tpu as pltpu
from jax.sharding import PartitionSpec as P

DH = 128
neg_big = -1e30
norm_eps = 1e-06
BF = jnp.bfloat16
F32 = jnp.float32
GATHER_BYTES = 32 * 1024 * 1024
FRONT_LIMIT = 62 * 1024 * 1024
MESH = pl.DeviceIdType.MESH
VMEM_LIMIT = 56 * 1024 * 1024


def dot(a, b, ca, cb):
    return lax.dot_general(a, b, (((ca,), (cb,)), ((), ())), preferred_element_type=F32)


def vm():
    return pl.BlockSpec(memory_space=pltpu.VMEM)


def heads_of(ref, first, count):
    return jnp.concatenate(
        [ref[:, (first + g) * DH : (first + g + 1) * DH] for g in range(count)], axis=0
    )


def visible_mask(tokens, group, full, seq_index):
    shape = (group, tokens, full)
    pos = lax.broadcasted_iota(jnp.int32, shape, 1) + seq_index * tokens
    key = lax.broadcasted_iota(jnp.int32, shape, 2)
    return (key <= pos).reshape(group * tokens, full)


def attend_kernel(group, residual, q, kv, att, log_total, inv_rms, normed):
    tokens = q.shape[0]
    full = kv.shape[0]
    kv_heads = kv.shape[1] // (2 * DH)
    visible = visible_mask(tokens, group, full, lax.axis_index("seq"))
    scale = 1.0 / math.sqrt(DH)
    for k in range(kv_heads):
        qh = heads_of(q, k * group, group)
        kh = kv[:, k * DH : (k + 1) * DH]
        vh = kv[:, (kv_heads + k) * DH : (kv_heads + k + 1) * DH]
        scores = jnp.where(visible, dot(qh, kh, 1, 1) * scale, neg_big)
        top = jnp.max(scores, axis=1, keepdims=True)
        weights = jnp.exp(scores - top)
        total = jnp.sum(weights, axis=1, keepdims=True)
        out = (dot(weights.astype(BF), vh, 1, 0) / total).astype(BF)
        logs = top + jnp.log(total)
        for g in range(group):
            h = k * group + g
            att[:, h * DH : (h + 1) * DH] = out[g * tokens : (g + 1) * tokens]
            log_total[:, h : h + 1] = logs[g * tokens : (g + 1) * tokens]
    hidden = residual[...].astype(F32) + att[...].astype(F32)
    inv = lax.rsqrt(jnp.mean(hidden * hidden, axis=1, keepdims=True) + norm_eps)
    inv_rms[...] = inv
    normed[...] = (hidden * inv).astype(BF)


def attend(residual, q, kv, group):
    tokens, width = q.shape
    heads = width // DH
    return pl.pallas_call(
        functools.partial(attend_kernel, group),
        out_shape=(
            jax.ShapeDtypeStruct((tokens, width), BF),
            jax.ShapeDtypeStruct((tokens, heads), F32),
            jax.ShapeDtypeStruct((tokens, 1), F32),
            jax.ShapeDtypeStruct((tokens, width), BF),
        ),
        in_specs=[vm()] * 3,
        out_specs=(vm(),) * 4,
        compiler_params=pltpu.CompilerParams(vmem_limit_bytes=VMEM_LIMIT),
        cost_estimate=pl.CostEstimate(
            flops=4 * tokens * kv.shape[0] * width,
            bytes_accessed=8 * tokens * width + 2 * kv.size,
            transcendentals=heads * tokens * kv.shape[0],
        ),
        name="attend",
    )(residual, q, kv)


def attend_rows(group, residual, q, kv, att, log_total, inv_rms, normed):
    tokens = q.shape[0]
    full = kv.shape[0]
    kv_heads = kv.shape[1] // (2 * DH)
    visible = visible_mask(tokens, group, full, lax.axis_index("seq"))
    scale = 1.0 / math.sqrt(DH)
    for k in range(kv_heads):
        qh = heads_of(q, k * group, group)
        kh = kv[:, k * DH : (k + 1) * DH]
        vh = kv[:, (kv_heads + k) * DH : (kv_heads + k + 1) * DH]
        scores = jnp.where(visible, dot(qh, kh, 1, 1) * scale, neg_big)
        top = jnp.max(scores, axis=1, keepdims=True)
        weights = jnp.exp(scores - top)
        total = jnp.sum(weights, axis=1, keepdims=True)
        out = (dot(weights.astype(BF), vh, 1, 0) / total).astype(BF)
        logs = top + jnp.log(total)
        for g in range(group):
            h = k * group + g
            att[:, h * DH : (h + 1) * DH] = out[g * tokens : (g + 1) * tokens]
            log_total[:, h : h + 1] = logs[g * tokens : (g + 1) * tokens]
    hidden = residual[...].astype(F32) + att[...].astype(F32)
    inv = lax.rsqrt(jnp.mean(hidden * hidden, axis=1, keepdims=True) + norm_eps)
    inv_rms[...] = inv
    normed[...] = (hidden * inv).astype(BF)


def front_kernel(
    group,
    seqs,
    residual,
    q,
    kv_mine,
    table,
    grads,
    gate_weight,
    up_weight,
    down_weight,
    att,
    log_total,
    inv_rms,
    token_dot,
    kv_all,
    grads_all,
    normed_all,
    tables,
    rows_own,
    grads_own,
    gate_own,
    up_own,
    mixed_own,
    input_part,
    out_part,
    kv,
    normed,
    gate_w,
    up_w,
    down_w,
    tabs,
    mix,
    slot,
    held,
    rows,
    pulls,
    raw,
    gate_pre,
    up_pre,
    gate_grad,
    up_grad,
    mixed,
    local_sem,
    weight_sem,
    out_sem,
    kv_sem,
    line_sem,
    plane_sem,
    table_line_sem,
    table_plane_sem,
):
    z = lax.axis_index("seq")
    e = lax.axis_index("expert")
    c, x, y = lax.rem(e, 2), lax.rem(e // 2, 2), e // 4
    tokens = q.shape[0]
    half = tokens // 2
    sibling = {"expert": e + 1 - 2 * c}
    across_x = {"expert": e + 2 - 4 * x}
    across_y = {"expert": e + 4 - 8 * y}
    above, below = {"seq": z + 1}, {"seq": z - 1}
    top = seqs - 1
    arrays = (grads_all, normed_all)
    sends = []

    def copy_of(view, sems, device):
        return pltpu.make_async_remote_copy(
            src_ref=view,
            dst_ref=view,
            send_sem=sems.at[0],
            recv_sem=sems.at[1],
            device_id=device,
            device_id_type=MESH,
        )

    def send(guard, view, sems, device):
        copy_of(view(), sems(), device).start()
        sends.append((guard, lambda: copy_of(view(), sems(), device).wait_send()))

    def arrived(view, sems):
        copy_of(view, sems, sibling).wait_recv()

    def under(guard, body):
        if guard is True:
            body()
        else:
            pl.when(guard)(body)

    def plane(k):
        d = (k + 1) // 2
        return z if k == 0 else (z - d if k % 2 else z + d)

    def present(k):
        d = (k + 1) // 2
        return True if k == 0 else (z >= d if k % 2 else z + d <= top)

    def forwarded(k):
        d = (k + 1) // 2
        return z + 1 <= top if k % 2 else z >= 1

    def both(a, b):
        return b if a is True else (a if b is True else jnp.logical_and(a, b))

    def line_start(ref, sems, k):
        guard = both(present(k - 2) if k > 2 else True, forwarded(k))

        def block():
            return ref.at[plane(k - 2) if k > 2 else z, y, x, c]

        under(guard, lambda: send(guard, block, lambda: sems(k), above if k % 2 else below))

    def first(a, k):
        ref = arrays[a]

        def sems(i):
            return plane_sem.at[a, k, i]

        if k:

            def take():
                arrived(ref.at[plane(k), y, x, c], line_sem.at[a, k])
                if a == 0:
                    arrived(tables.at[plane(k), y, x, c], table_line_sem.at[k])

            under(present(k), take)
            if k + 2 <= 2 * top:
                line_start(ref, lambda j: line_sem.at[a, j], k + 2)
                if a == 0:
                    line_start(tables, lambda j: table_line_sem.at[j], k + 2)

        def start():
            send(k, lambda: ref.at[plane(k), y, x, c, :half], lambda: sems(0), across_x)
            send(k, lambda: ref.at[plane(k), y, x, c, half:], lambda: sems(1), across_y)
            if a == 0:
                send(
                    k,
                    lambda: tables.at[plane(k), y, x, c],
                    lambda: table_plane_sem.at[k, 0],
                    across_x,
                )

        under(present(k), start)

    def second(a, k):
        ref = arrays[a]

        def sems(i):
            return plane_sem.at[a, k, i]

        def step():
            p = plane(k)
            arrived(ref.at[p, y, 1 - x, c, :half], sems(0))
            send(k, lambda: ref.at[plane(k), y, :, c, :half], lambda: sems(2), across_y)
            arrived(ref.at[p, 1 - y, x, c, half:], sems(1))
            send(k, lambda: ref.at[plane(k), :, x, c, half:], lambda: sems(3), across_x)
            if a == 0:
                arrived(tables.at[p, y, 1 - x, c], table_plane_sem.at[k, 0])
                send(
                    k,
                    lambda: tables.at[plane(k), y, :, c],
                    lambda: table_plane_sem.at[k, 1],
                    across_y,
                )

        under(present(k), step)

    def third(a, k):
        ref = arrays[a]

        def sems(i):
            return plane_sem.at[a, k, i]

        def step():
            p = plane(k)
            arrived(ref.at[p, 1 - y, :, c, :half], sems(2))
            arrived(ref.at[p, :, 1 - x, c, half:], sems(3))
            send(k, lambda: ref.at[plane(k), :, :, c], lambda: sems(4), sibling)
            if a == 0:
                arrived(tables.at[p, 1 - y, :, c], table_plane_sem.at[k, 1])
                send(
                    k,
                    lambda: tables.at[plane(k), :, :, c],
                    lambda: table_plane_sem.at[k, 2],
                    sibling,
                )

        under(present(k), step)

    def fourth(a, k):
        def step():
            p = plane(k)
            arrived(arrays[a].at[p, :, :, 1 - c], plane_sem.at[a, k, 4])
            if a == 0:
                arrived(tables.at[p, :, :, 1 - c], table_plane_sem.at[k, 2])

        under(present(k), step)

    copies = [
        pltpu.make_async_copy(grads, grads_all.at[z, y, x, c], local_sem.at[0]),
        pltpu.make_async_copy(table, tables.at[z, y, x, c], local_sem.at[1]),
        pltpu.make_async_copy(kv_mine, kv.at[z], local_sem.at[2]),
    ]
    for copy in copies:
        copy.start()
    weights = [
        pltpu.make_async_copy(down_weight, down_w, weight_sem.at[0]),
        pltpu.make_async_copy(gate_weight, gate_w, weight_sem.at[1]),
        pltpu.make_async_copy(up_weight, up_w, weight_sem.at[2]),
    ]
    for copy in weights:
        copy.start()
    for j in range(1, seqs):

        @pl.when(j > z)
        def _():
            kv[j] = jnp.zeros(kv.shape[1:], BF)

    barrier = pltpu.get_barrier_semaphore()
    for device in (sibling, across_x, across_y):
        pl.semaphore_signal(barrier, inc=1, device_id=device, device_id_type=MESH)

    @pl.when(z < top)
    def _():
        pl.semaphore_signal(barrier, inc=1, device_id=above, device_id_type=MESH)

    @pl.when(z > 0)
    def _():
        pl.semaphore_signal(barrier, inc=1, device_id=below, device_id_type=MESH)

    pl.semaphore_wait(barrier, 3 + (z < top).astype(jnp.int32) + (z > 0).astype(jnp.int32))
    for copy in copies:
        copy.wait()

    def kv_start(d):
        guard = both(z >= d if d else True, z < top)
        under(guard, lambda: send(guard, lambda: kv.at[z - d], lambda: kv_sem.at[d + 1], above))

    def kv_take(d):
        @pl.when(z >= d)
        def _():
            arrived(kv.at[z - d], kv_sem.at[d])

    kv_start(0)
    line_start(grads_all, lambda j: line_sem.at[0, j], 2)
    line_start(tables, lambda j: table_line_sem.at[j], 2)
    line_start(tables, lambda j: table_line_sem.at[j], 1)
    first(0, 0)
    for d in range(1, seqs):
        kv_take(d)
        if d < top:
            kv_start(d)
        if d == 1:
            second(0, 0)
        if d == 2:
            third(0, 0)
    line_start(grads_all, lambda j: line_sem.at[0, j], 1)
    keys = kv[...].reshape(seqs * tokens, kv.shape[2])
    attend_rows(group, residual, q, keys, att, log_total, inv_rms, normed)
    keep = [
        pltpu.make_async_copy(normed, normed_all.at[z, y, x, c], local_sem.at[3]),
        pltpu.make_async_copy(kv, kv_all, local_sem.at[4]),
    ]
    for copy in keep:
        copy.start()
    keep[0].wait()
    line_start(normed_all, lambda j: line_sem.at[1, j], 1)
    line_start(normed_all, lambda j: line_sem.at[1, j], 2)
    first(1, 0)

    local = slot.shape[0]
    ranks = slot.shape[1]
    depth = rows.shape[1] // ranks

    def chosen(i, r):
        row = lax.broadcasted_iota(jnp.int32, (depth, tokens), 0)
        return slot[i, pl.ds(r, 1), :] == row

    def span(r):
        return pl.ds(pl.multiple_of(r * depth, depth), depth)

    def each_rank(body):
        lax.fori_loop(0, ranks, lambda r, carry: (body(r), carry)[1], 0)

    def place(r):
        return (r // 4, lax.rem(r // 2, 2), lax.rem(r, 2))

    def find_slots():
        before = (
            lax.broadcasted_iota(jnp.int32, (tokens, tokens), 0)
            < lax.broadcasted_iota(jnp.int32, (tokens, tokens), 1)
        ).astype(F32).astype(BF)
        for i in range(local):
            mine = jnp.concatenate(
                [tabs[r // 4, r // 2 % 2, r % 2, pl.ds(e * local + i, 1), :] for r in range(ranks)],
                axis=0,
            )
            routed = mine >= 0.0
            rank = dot(routed.astype(F32).astype(BF), before, 1, 0)
            mix[i] = mine
            slot[i] = jnp.where(routed, rank.astype(jnp.int32), -1)

    def pick_into(target):
        def body(r):
            block = held[place(r)]
            for i in range(local):
                target[i, span(r), :] = dot(
                    chosen(i, r).astype(F32).astype(BF), block, 1, 0
                ).astype(BF)

        each_rank(body)

    def blend(i):
        def body(r):
            at = span(r)
            hit = chosen(i, r)
            share = jnp.sum(jnp.where(hit, mix[i, pl.ds(r, 1), :], 0.0), axis=1, keepdims=True)
            g, u, w = gate_pre[at, :], up_pre[at, :], raw[i, at, :]
            sigmoid = jax.nn.sigmoid(g)
            silu = g * sigmoid
            act = silu * u
            act_grad = w * share
            gate_grad[i, at, :] = (act_grad * u * sigmoid * (1.0 + g * (1.0 - sigmoid))).astype(BF)
            up_grad[i, at, :] = (act_grad * silu).astype(BF)
            mixed[i, at, :] = (act * share).astype(BF)
            total = jnp.sum(act.astype(BF).astype(F32) * w, axis=1, keepdims=True)
            token_dot[r, i : i + 1, :] = jnp.sum(jnp.where(hit, total, 0.0), axis=0, keepdims=True)

        each_rank(body)

    def spread(source):
        def body(r):
            total = None
            for i in range(local):
                part = dot(chosen(i, r).astype(F32).astype(BF), source[i, span(r), :], 0, 0)
                total = part if total is None else total + part
            held[place(r)] = total.astype(BF)

        each_rank(body)

    def hold(ref):
        copy = pltpu.make_async_copy(ref.at[z], held, local_sem.at[0])
        copy.start()
        copy.wait()

    outs = [
        pltpu.make_async_copy(pulls, grads_own, out_sem.at[0]),
        pltpu.make_async_copy(rows, rows_own, out_sem.at[1]),
        pltpu.make_async_copy(gate_grad, gate_own, out_sem.at[2]),
        pltpu.make_async_copy(up_grad, up_own, out_sem.at[3]),
        pltpu.make_async_copy(mixed, mixed_own, out_sem.at[4]),
        pltpu.make_async_copy(held, input_part, out_sem.at[5]),
        pltpu.make_async_copy(held, out_part, out_sem.at[6]),
    ]

    def task_grads():
        fourth(0, 0)
        table_copy = pltpu.make_async_copy(tables.at[z], tabs, local_sem.at[1])
        table_copy.start()
        table_copy.wait()
        find_slots()
        hold(grads_all)
        pick_into(pulls)
        outs[0].start()

    def task_raw(i):
        if i == 0:
            weights[0].wait()
        raw[i] = dot(pulls[i], down_w[i], 1, 1)

    def task_rows():
        fourth(1, 0)
        hold(normed_all)
        pick_into(rows)
        outs[1].start()
        weights[1].wait()
        weights[2].wait()

    def task_gate(i):
        gate_pre[...] = dot(rows[i], gate_w[i], 1, 0)

    def task_up(i):
        up_pre[...] = dot(rows[i], up_w[i], 1, 0)

    def task_input(i):
        if i == 0:
            outs[0].wait()
            outs[1].wait()
        rows[i] = (dot(gate_grad[i], gate_w[i], 1, 1) + dot(up_grad[i], up_w[i], 1, 1)).astype(BF)

    def task_out(i):
        pulls[i] = dot(mixed[i], down_w[i], 1, 0).astype(BF)

    def task_spread_input():
        for copy in outs[2:5]:
            copy.start()
        spread(rows)
        outs[5].start()

    def task_spread_out():
        outs[5].wait()
        spread(pulls)
        outs[6].start()

    task_grads()
    task_raw(0)
    second(1, 0)
    order = []
    for d in range(1, seqs):
        for a in range(2):
            order += [(a, 2 * d - 1), (a, 2 * d)]
    tasks = [functools.partial(task_raw, i) for i in range(1, local)]
    tasks += [lambda: third(1, 0), task_rows]
    for i in range(local):
        tasks += [
            functools.partial(task, i) for task in (task_gate, task_up, blend, task_input, task_out)
        ]
    tasks += [task_spread_input, task_spread_out]
    for i in range(max(len(order) + 4, len(tasks))):
        if i < len(order):
            first(*order[i])
        if 0 <= i - 2 < len(order):
            second(*order[i - 2])
        if 0 <= i - 4 < len(order):
            third(*order[i - 4])
        if i < len(tasks):
            tasks[i]()
    for copy in outs[2:5] + outs[6:]:
        copy.wait()
    keep[1].wait()
    for a, k in order:
        fourth(a, k)
    for guard, finish in sends:
        under(present(guard) if isinstance(guard, int) else guard, finish)


def front(residual, q, kv_mine, table, grads, weights, group, seqs, ranks, depth):
    tokens, width = q.shape
    heads = width // DH
    slots = 2 * seqs - 1
    local, _, hidden = weights[0].shape
    any_space = pl.BlockSpec(memory_space=pl.ANY)
    dma = pltpu.SemaphoreType.DMA
    picked = (local, ranks * depth, width)
    units = (local, ranks * depth, hidden)
    plane = (2, 2, 2, tokens, width)
    return pl.pallas_call(
        functools.partial(front_kernel, group, seqs),
        out_shape=(
            jax.ShapeDtypeStruct((tokens, width), BF),
            jax.ShapeDtypeStruct((tokens, heads), F32),
            jax.ShapeDtypeStruct((tokens, 1), F32),
            jax.ShapeDtypeStruct((ranks, local, tokens), F32),
            jax.ShapeDtypeStruct((seqs,) + kv_mine.shape, BF),
            jax.ShapeDtypeStruct((seqs,) + plane, BF),
            jax.ShapeDtypeStruct((seqs,) + plane, BF),
            jax.ShapeDtypeStruct((seqs, 2, 2, 2) + table.shape, F32),
            jax.ShapeDtypeStruct(picked, BF),
            jax.ShapeDtypeStruct(picked, BF),
            jax.ShapeDtypeStruct(units, BF),
            jax.ShapeDtypeStruct(units, BF),
            jax.ShapeDtypeStruct(units, BF),
            jax.ShapeDtypeStruct(plane, BF),
            jax.ShapeDtypeStruct(plane, BF),
        ),
        in_specs=[vm()] * 5 + [any_space] * 3,
        out_specs=(vm(),) * 4 + (any_space,) * 11,
        scratch_shapes=[
            pltpu.VMEM((seqs,) + kv_mine.shape, BF),
            pltpu.VMEM((tokens, width), BF),
            pltpu.VMEM(weights[0].shape, BF),
            pltpu.VMEM(weights[1].shape, BF),
            pltpu.VMEM(weights[2].shape, BF),
            pltpu.VMEM((2, 2, 2) + table.shape, F32),
            pltpu.VMEM((local, ranks, tokens), F32),
            pltpu.VMEM((local, ranks, tokens), jnp.int32),
            pltpu.VMEM(plane, BF),
            pltpu.VMEM(picked, BF),
            pltpu.VMEM(picked, BF),
            pltpu.VMEM(units, F32),
            pltpu.VMEM(units[1:], F32),
            pltpu.VMEM(units[1:], F32),
            pltpu.VMEM(units, BF),
            pltpu.VMEM(units, BF),
            pltpu.VMEM(units, BF),
            dma((5,)),
            dma((3,)),
            dma((7,)),
            dma((seqs, 2)),
            dma((2, slots, 2)),
            dma((2, slots, 5, 2)),
            dma((slots, 2)),
            dma((slots, 3, 2)),
        ],
        compiler_params=pltpu.CompilerParams(
            collective_id=0, has_side_effects=True, vmem_limit_bytes=FRONT_LIMIT
        ),
        cost_estimate=pl.CostEstimate(
            flops=4 * tokens * seqs * tokens * width + 12 * local * ranks * depth * width * hidden,
            bytes_accessed=32 * seqs * tokens * width,
            transcendentals=heads * tokens * seqs * tokens,
        ),
        name="front",
    )(residual, q, kv_mine, table, grads, *weights)


def attend_back_kernel(
    group, residual, q, kv, att, log_total, inv_rms, grad_out, normed_grad, res_grad, q_grad, kv_part
):
    tokens = q.shape[0]
    full = kv.shape[0]
    kv_heads = kv.shape[1] // (2 * DH)
    scale = 1.0 / math.sqrt(DH)
    inv = inv_rms[...]
    normed = (residual[...].astype(F32) + att[...].astype(F32)) * inv
    ngrad = normed_grad[...].astype(F32)
    dot_mean = jnp.mean(ngrad * normed, axis=1, keepdims=True)
    res_grad[...] = (grad_out[...].astype(F32) + inv * (ngrad - normed * dot_mean)).astype(BF)
    visible = visible_mask(tokens, group, full, lax.axis_index("seq"))
    for k in range(kv_heads):
        qh = heads_of(q, k * group, group)
        oh = heads_of(att, k * group, group)
        gh = heads_of(res_grad, k * group, group)
        logs = jnp.concatenate(
            [log_total[:, k * group + g : k * group + g + 1] for g in range(group)], axis=0
        )
        kh = kv[:, k * DH : (k + 1) * DH]
        vh = kv[:, (kv_heads + k) * DH : (kv_heads + k + 1) * DH]
        scores = jnp.where(visible, dot(qh, kh, 1, 1) * scale, neg_big)
        probs = jnp.exp(scores - logs)
        delta = jnp.sum(gh.astype(F32) * oh.astype(F32), axis=1, keepdims=True)
        pgrad = dot(gh, vh, 1, 1)
        sgrad = (probs * (pgrad - delta)).astype(BF)
        dq = (dot(sgrad, kh, 1, 0) * scale).astype(BF)
        for g in range(group):
            h = k * group + g
            q_grad[:, h * DH : (h + 1) * DH] = dq[g * tokens : (g + 1) * tokens]
        kv_part[:, k * DH : (k + 1) * DH] = (dot(sgrad, qh, 0, 0) * scale).astype(BF)
        kv_part[:, (kv_heads + k) * DH : (kv_heads + k + 1) * DH] = dot(
            probs.astype(BF), gh, 0, 0
        ).astype(BF)


def attend_back(group, residual, q, kv, att, log_total, inv_rms, grad_out, normed_grad):
    tokens, width = q.shape
    return pl.pallas_call(
        functools.partial(attend_back_kernel, group),
        out_shape=(
            jax.ShapeDtypeStruct((tokens, width), BF),
            jax.ShapeDtypeStruct((tokens, width), BF),
            jax.ShapeDtypeStruct(kv.shape, BF),
        ),
        in_specs=[vm()] * 8,
        out_specs=(vm(),) * 3,
        compiler_params=pltpu.CompilerParams(vmem_limit_bytes=VMEM_LIMIT),
        cost_estimate=pl.CostEstimate(
            flops=10 * tokens * kv.shape[0] * width,
            bytes_accessed=14 * tokens * width + 4 * kv.size,
            transcendentals=tokens * kv.shape[0] * (width // DH),
        ),
        name="attend_back",
    )(residual, q, kv, att, log_total, inv_rms, grad_out, normed_grad)


def pick_kernel(seq_index, slot, rows, picked):
    local = slot.shape[2]
    depth = picked.shape[1]
    tokens = rows.shape[2]
    row = lax.broadcasted_iota(jnp.int32, (depth, tokens), 0)
    for e in range(local):
        chosen = (slot[0, 0, e : e + 1, :] == row).astype(F32).astype(BF)
        picked[e] = dot(chosen, rows[0, 0], 1, 0).astype(BF)


def pick_rows(gathered, slot, seq_index, first, planes, depth):
    seqs, ranks, tokens, width = gathered.shape
    local = slot.shape[2]
    count = planes * ranks

    def source(i, s):
        return (lax.rem(s[0] + first + i // ranks, seqs), lax.rem(i, ranks), 0, 0)

    return pl.pallas_call(
        pick_kernel,
        out_shape=jax.ShapeDtypeStruct((local, count * depth, width), BF),
        grid_spec=pltpu.PrefetchScalarGridSpec(
            num_scalar_prefetch=1,
            grid=(count,),
            in_specs=[
                pl.BlockSpec((1, 1, local, tokens), source),
                pl.BlockSpec((1, 1, tokens, width), source),
            ],
            out_specs=pl.BlockSpec((local, depth, width), lambda i, s: (0, i, 0)),
        ),
        compiler_params=pltpu.CompilerParams(vmem_limit_bytes=16 * 1024 * 1024),
        cost_estimate=pl.CostEstimate(
            flops=2 * local * count * depth * tokens * width,
            bytes_accessed=2 * count * (tokens + local * depth) * width,
            transcendentals=0,
        ),
        name="pick_rows",
    )(seq_index, slot, gathered)


def spread_kernel(slot, rows, out):
    ranks, local, tokens = slot.shape
    depth = rows.shape[1]
    row = lax.broadcasted_iota(jnp.int32, (depth, tokens), 0)
    total = None
    for e in range(local):
        chosen = (slot[0, e : e + 1, :] == row).astype(F32).astype(BF)
        part = dot(chosen, rows[e], 0, 0)
        total = part if total is None else total + part
    out[0] = total.astype(BF)


def spread_rows(rows, slot):
    ranks, local, tokens = slot.shape
    width = rows.shape[2]
    depth = rows.shape[1] // ranks
    return pl.pallas_call(
        spread_kernel,
        out_shape=jax.ShapeDtypeStruct((ranks, tokens, width), BF),
        grid=(ranks,),
        in_specs=[
            pl.BlockSpec((1, local, tokens), lambda i: (i, 0, 0)),
            pl.BlockSpec((local, depth, width), lambda i: (0, i, 0)),
        ],
        out_specs=pl.BlockSpec((1, tokens, width), lambda i: (i, 0, 0)),
        compiler_params=pltpu.CompilerParams(vmem_limit_bytes=16 * 1024 * 1024),
        cost_estimate=pl.CostEstimate(
            flops=2 * local * ranks * depth * tokens * width,
            bytes_accessed=2 * ranks * (tokens + local * depth) * width,
            transcendentals=0,
        ),
        name="spread_rows",
    )(slot, rows)


def hidden_units(rows, grads, mix, gate_weight, up_weight, down_weight):
    gate_pre = jnp.einsum("erd,edf->erf", rows, gate_weight, preferred_element_type=F32)
    up_pre = jnp.einsum("erd,edf->erf", rows, up_weight, preferred_element_type=F32)
    raw = jnp.einsum("erd,efd->erf", grads, down_weight, preferred_element_type=F32)
    sigmoid = jax.nn.sigmoid(gate_pre)
    silu = gate_pre * sigmoid
    act = silu * up_pre
    act_grad = raw * mix[:, :, None]
    gate_grad = (act_grad * up_pre * sigmoid * (1.0 + gate_pre * (1.0 - sigmoid))).astype(BF)
    up_grad = (act_grad * silu).astype(BF)
    mixed = (act * mix[:, :, None]).astype(BF)
    return (gate_grad, up_grad, mixed, act, raw)


def on_device(
    residual,
    queries,
    key_input,
    value_input,
    routes,
    mix_weights,
    gate_weight,
    up_weight,
    down_weight,
    grad_out,
):
    tokens = residual.shape[1]
    width = residual.shape[2]
    kv_width = key_input.shape[2]
    group = queries.shape[2] // kv_width
    local = gate_weight.shape[0]
    ranks = lax.axis_size("expert")
    seqs = lax.axis_size("seq")
    experts = local * ranks
    top_count = routes.shape[2]
    capacity = tokens * top_count * 5 // (4 * experts)
    depth = -(-capacity // 16) * 16
    both = ("seq", "expert")
    both_size = seqs * ranks
    seq_index = lax.axis_index("seq")
    rank_index = lax.axis_index("expert")
    seq_array = seq_index.astype(jnp.int32).reshape(1)

    kv_mine = jnp.concatenate(
        [key_input.reshape(tokens, kv_width), value_input.reshape(tokens, kv_width)], axis=1
    )
    expert_ids = jnp.arange(experts, dtype=jnp.int32)
    picked = routes.reshape(tokens, top_count)
    mix_rows = mix_weights.reshape(tokens, top_count)
    hit = picked[None, :, :] == expert_ids[:, None, None]
    table = jnp.sum(jnp.where(hit, mix_rows[None], 0.0), axis=2) - (
        1.0 - jnp.sum(hit.astype(F32), axis=2)
    )
    grad_rows = grad_out.reshape(tokens, width)
    q = queries.reshape(tokens, width)
    res = residual.reshape(tokens, width)
    weights = (gate_weight, up_weight, down_weight)
    paired = ranks == 8 and 2 * both_size * grad_rows.size <= GATHER_BYTES
    if paired:
        (
            att,
            log_total,
            inv_rms,
            token_dot,
            kv,
            grads_all,
            normed_all,
            tables,
            rows_own,
            grads_own,
            gate_own,
            up_own,
            mixed_own,
            input_part,
            out_part,
        ) = front(
            res, q, kv_mine, table, grad_rows, weights, group, seqs, ranks, depth
        )
        input_part = input_part.reshape(ranks * tokens, width)
        out_part = out_part.reshape(ranks * tokens, width)
        kv = kv.reshape(seqs * tokens, 2 * kv_width)
        grads_all = grads_all.reshape(seqs, ranks, tokens, width)
        normed_all = normed_all.reshape(seqs, ranks, tokens, width)
        tables = tables.reshape(seqs * ranks, experts, tokens)
    else:
        kv = lax.all_gather(kv_mine, "seq", axis=0, tiled=True)
        tables = lax.all_gather(table, both, axis=0, tiled=False)
        grads_all = lax.all_gather(grad_rows, both, axis=0, tiled=True)
        grads_all = grads_all.reshape(seqs, ranks, tokens, width)
        att, log_total, inv_rms, normed_bf = attend(res, q, kv, group)
    mine = lax.dynamic_slice_in_dim(tables, rank_index * local, local, axis=1)
    routed = mine >= 0.0
    before = jnp.triu(jnp.ones((tokens, tokens), BF), 1)
    rank = jnp.einsum("bet,tu->beu", routed.astype(BF), before, preferred_element_type=F32)
    slot = jnp.where(routed, rank.astype(jnp.int32), -1)
    slot = slot.reshape(seqs, ranks, local, tokens)
    mine = mine.reshape(seqs, ranks, local, tokens)

    grads_far = pick_rows(grads_all, slot, seq_array, 1, seqs - 1, depth)
    if not paired:
        grads_own = pick_rows(grads_all, slot, seq_array, 0, 1, depth)
        normed_bf, grads_own, grads_far = lax.optimization_barrier(
            (normed_bf, grads_own, grads_far)
        )
        normed_all = lax.all_gather(normed_bf, both, axis=0, tiled=True)
        normed_all = normed_all.reshape(seqs, ranks, tokens, width)

    slot_turned = jnp.roll(slot, -seq_index, axis=0)
    mix_turned = jnp.roll(mine, -seq_index, axis=0)
    here = slot_turned[..., None, :] == jnp.arange(depth, dtype=jnp.int32)[:, None]
    mix_slot = jnp.sum(jnp.where(here, mix_turned[..., None, :], 0.0), axis=4)
    mix_slot = jnp.transpose(mix_slot, (2, 0, 1, 3)).reshape(local, seqs * ranks * depth)
    own = ranks * depth

    rows_far = pick_rows(normed_all, slot, seq_array, 1, seqs - 1, depth)
    if not paired:
        rows_own = pick_rows(normed_all, slot, seq_array, 0, 1, depth)
        gate_own, up_own, mixed_own, act_own, raw_own = hidden_units(
            rows_own, grads_own, mix_slot[:, :own], *weights
        )
        input_grad = (
            jnp.einsum("erf,edf->erd", gate_own, gate_weight, preferred_element_type=F32)
            + jnp.einsum("erf,edf->erd", up_own, up_weight, preferred_element_type=F32)
        ).astype(BF)
        slot_own = slot_turned[0]
        input_part = spread_rows(input_grad, slot_own).reshape(ranks * tokens, width)
        expert_out = jnp.einsum(
            "erf,efd->erd", mixed_own, down_weight, preferred_element_type=F32
        ).astype(BF)
        out_part = spread_rows(expert_out, slot_own).reshape(ranks * tokens, width)
        pair_dot = jnp.sum(act_own.astype(BF).astype(F32) * raw_own, axis=2)
        pair_dot = pair_dot.reshape(local, ranks, depth)
        token_dot = jnp.sum(
            jnp.where(here[0], jnp.transpose(pair_dot, (1, 0, 2))[..., None], 0.0), axis=2
        )
    normed_grad = lax.psum_scatter(input_part, "expert", scatter_dimension=0, tiled=True)
    routed_out = lax.psum_scatter(out_part, "expert", scatter_dimension=0, tiled=True)
    hidden = res.astype(F32) + att.astype(F32)
    layer_out = (hidden + routed_out.astype(F32)).astype(BF)

    dots = lax.all_to_all(token_dot, "expert", split_axis=0, concat_axis=0, tiled=True)
    dots = dots.reshape(experts, tokens)
    mix_grad = jnp.sum(jnp.where(hit, dots[:, :, None], 0.0), axis=0)

    gate_far, up_far, mixed_far, _, _ = hidden_units(
        rows_far, grads_far, mix_slot[:, own:], *weights
    )
    share = width // seqs

    def columns(array):
        return lax.dynamic_slice_in_dim(array, seq_index * share, share, axis=2)

    def outer(a_own, a_far, b_own, b_far):
        return (
            jnp.einsum("erm,ern->emn", a_own, b_own, preferred_element_type=F32)
            + jnp.einsum("erm,ern->emn", a_far, b_far, preferred_element_type=F32)
        ).astype(BF)

    cols_own, cols_far = columns(rows_own), columns(rows_far)
    gate_share = outer(cols_own, cols_far, gate_own, gate_far)
    up_share = outer(cols_own, cols_far, up_own, up_far)
    down_share = outer(mixed_own, mixed_far, columns(grads_own), columns(grads_far))

    res_grad, q_grad, kv_part = attend_back(
        group, res, q, kv, att, log_total, inv_rms, grad_rows, normed_grad
    )
    kv_share = lax.psum_scatter(kv_part, "seq", scatter_dimension=0, tiled=True)
    return (
        layer_out.reshape(1, tokens, width),
        res_grad.reshape(1, tokens, width),
        q_grad.reshape(1, tokens, width),
        kv_share[:, :kv_width].reshape(1, tokens, kv_width),
        kv_share[:, kv_width:].reshape(1, tokens, kv_width),
        mix_grad.reshape(1, tokens, top_count),
        gate_share,
        up_share,
        down_share,
    )


def solution(mesh):
    rows = P("expert", "seq", None)
    weight = P("expert", None, None)
    return jax.shard_map(
        on_device,
        mesh=mesh,
        in_specs=(rows,) * 6 + (weight,) * 3 + (rows,),
        out_specs=(rows,) * 8 + (P("expert", None, "seq"),),
        check_vma=False,
    )
```

```python
import functools
import math

import jax
import jax.numpy as jnp
from jax import lax
from jax.experimental import pallas as pl
from jax.experimental.pallas import tpu as pltpu
from jax.sharding import PartitionSpec as P

DH = 128
neg_big = -1e30
norm_eps = 1e-06
BF = jnp.bfloat16
F32 = jnp.float32
GATHER_BYTES = 32 * 1024 * 1024
FRONT_LIMIT = 62 * 1024 * 1024
MESH = pl.DeviceIdType.MESH
VMEM_LIMIT = 56 * 1024 * 1024


def dot(a, b, ca, cb):
    return lax.dot_general(a, b, (((ca,), (cb,)), ((), ())), preferred_element_type=F32)


def vm():
    return pl.BlockSpec(memory_space=pltpu.VMEM)


def heads_of(ref, first, count):
    return jnp.concatenate(
        [ref[:, (first + g) * DH : (first + g + 1) * DH] for g in range(count)], axis=0
    )


def visible_mask(tokens, group, full, seq_index):
    shape = (group, tokens, full)
    pos = lax.broadcasted_iota(jnp.int32, shape, 1) + seq_index * tokens
    key = lax.broadcasted_iota(jnp.int32, shape, 2)
    return (key <= pos).reshape(group * tokens, full)


def attend_kernel(group, residual, q, kv, att, log_total, inv_rms, normed):
    tokens = q.shape[0]
    full = kv.shape[0]
    kv_heads = kv.shape[1] // (2 * DH)
    visible = visible_mask(tokens, group, full, lax.axis_index("seq"))
    scale = 1.0 / math.sqrt(DH)
    for k in range(kv_heads):
        qh = heads_of(q, k * group, group)
        kh = kv[:, k * DH : (k + 1) * DH]
        vh = kv[:, (kv_heads + k) * DH : (kv_heads + k + 1) * DH]
        scores = jnp.where(visible, dot(qh, kh, 1, 1) * scale, neg_big)
        top = jnp.max(scores, axis=1, keepdims=True)
        weights = jnp.exp(scores - top)
        total = jnp.sum(weights, axis=1, keepdims=True)
        out = (dot(weights.astype(BF), vh, 1, 0) / total).astype(BF)
        logs = top + jnp.log(total)
        for g in range(group):
            h = k * group + g
            att[:, h * DH : (h + 1) * DH] = out[g * tokens : (g + 1) * tokens]
            log_total[:, h : h + 1] = logs[g * tokens : (g + 1) * tokens]
    hidden = residual[...].astype(F32) + att[...].astype(F32)
    inv = lax.rsqrt(jnp.mean(hidden * hidden, axis=1, keepdims=True) + norm_eps)
    inv_rms[...] = inv
    normed[...] = (hidden * inv).astype(BF)


def attend(residual, q, kv, group):
    tokens, width = q.shape
    heads = width // DH
    return pl.pallas_call(
        functools.partial(attend_kernel, group),
        out_shape=(
            jax.ShapeDtypeStruct((tokens, width), BF),
            jax.ShapeDtypeStruct((tokens, heads), F32),
            jax.ShapeDtypeStruct((tokens, 1), F32),
            jax.ShapeDtypeStruct((tokens, width), BF),
        ),
        in_specs=[vm()] * 3,
        out_specs=(vm(),) * 4,
        compiler_params=pltpu.CompilerParams(vmem_limit_bytes=VMEM_LIMIT),
        cost_estimate=pl.CostEstimate(
            flops=4 * tokens * kv.shape[0] * width,
            bytes_accessed=8 * tokens * width + 2 * kv.size,
            transcendentals=heads * tokens * kv.shape[0],
        ),
        name="attend",
    )(residual, q, kv)


def attend_rows(group, residual, q, kv, att, log_total, inv_rms, normed):
    tokens = q.shape[0]
    full = kv.shape[0]
    kv_heads = kv.shape[1] // (2 * DH)
    visible = visible_mask(tokens, group, full, lax.axis_index("seq"))
    scale = 1.0 / math.sqrt(DH)
    for k in range(kv_heads):
        qh = heads_of(q, k * group, group)
        kh = kv[:, k * DH : (k + 1) * DH]
        vh = kv[:, (kv_heads + k) * DH : (kv_heads + k + 1) * DH]
        scores = jnp.where(visible, dot(qh, kh, 1, 1) * scale, neg_big)
        top = jnp.max(scores, axis=1, keepdims=True)
        weights = jnp.exp(scores - top)
        total = jnp.sum(weights, axis=1, keepdims=True)
        out = (dot(weights.astype(BF), vh, 1, 0) / total).astype(BF)
        logs = top + jnp.log(total)
        for g in range(group):
            h = k * group + g
            att[:, h * DH : (h + 1) * DH] = out[g * tokens : (g + 1) * tokens]
            log_total[:, h : h + 1] = logs[g * tokens : (g + 1) * tokens]
    hidden = residual[...].astype(F32) + att[...].astype(F32)
    inv = lax.rsqrt(jnp.mean(hidden * hidden, axis=1, keepdims=True) + norm_eps)
    inv_rms[...] = inv
    normed[...] = (hidden * inv).astype(BF)


def front_kernel(
    group,
    seqs,
    residual,
    q,
    kv_mine,
    table,
    grads,
    gate_weight,
    up_weight,
    down_weight,
    att,
    log_total,
    inv_rms,
    token_dot,
    input_sum,
    out_sum,
    kv_all,
    grads_all,
    normed_all,
    tables,
    rows_own,
    grads_own,
    gate_own,
    up_own,
    mixed_own,
    input_part,
    out_part,
    kv,
    normed,
    gate_w,
    up_w,
    down_w,
    tabs,
    mix,
    slot,
    held,
    spare,
    pair_sum,
    line_sum,
    last_sum,
    rows,
    pulls,
    raw,
    gate_pre,
    up_pre,
    gate_grad,
    up_grad,
    mixed,
    local_sem,
    weight_sem,
    out_sem,
    sum_sem,
    kv_sem,
    line_sem,
    plane_sem,
    table_line_sem,
    table_plane_sem,
):
    z = lax.axis_index("seq")
    e = lax.axis_index("expert")
    c, x, y = lax.rem(e, 2), lax.rem(e // 2, 2), e // 4
    tokens = q.shape[0]
    half = tokens // 2
    sibling = {"expert": e + 1 - 2 * c}
    across_x = {"expert": e + 2 - 4 * x}
    across_y = {"expert": e + 4 - 8 * y}
    above, below = {"seq": z + 1}, {"seq": z - 1}
    top = seqs - 1
    arrays = (grads_all, normed_all)
    sends = []

    def copy_of(view, sems, device):
        return pltpu.make_async_remote_copy(
            src_ref=view,
            dst_ref=view,
            send_sem=sems.at[0],
            recv_sem=sems.at[1],
            device_id=device,
            device_id_type=MESH,
        )

    def send(guard, view, sems, device):
        copy_of(view(), sems(), device).start()
        sends.append((guard, lambda: copy_of(view(), sems(), device).wait_send()))

    def arrived(view, sems):
        copy_of(view, sems, sibling).wait_recv()

    def under(guard, body):
        if guard is True:
            body()
        else:
            pl.when(guard)(body)

    def plane(k):
        d = (k + 1) // 2
        return z if k == 0 else (z - d if k % 2 else z + d)

    def present(k):
        d = (k + 1) // 2
        return True if k == 0 else (z >= d if k % 2 else z + d <= top)

    def forwarded(k):
        d = (k + 1) // 2
        return z + 1 <= top if k % 2 else z >= 1

    def both(a, b):
        return b if a is True else (a if b is True else jnp.logical_and(a, b))

    def line_start(ref, sems, k):
        guard = both(present(k - 2) if k > 2 else True, forwarded(k))

        def block():
            return ref.at[plane(k - 2) if k > 2 else z, y, x, c]

        under(guard, lambda: send(guard, block, lambda: sems(k), above if k % 2 else below))

    def first(a, k):
        ref = arrays[a]

        def sems(i):
            return plane_sem.at[a, k, i]

        if k:

            def take():
                arrived(ref.at[plane(k), y, x, c], line_sem.at[a, k])
                if a == 0:
                    arrived(tables.at[plane(k), y, x, c], table_line_sem.at[k])

            under(present(k), take)
            if k + 2 <= 2 * top:
                line_start(ref, lambda j: line_sem.at[a, j], k + 2)
                if a == 0:
                    line_start(tables, lambda j: table_line_sem.at[j], k + 2)

        def start():
            send(k, lambda: ref.at[plane(k), y, x, c, :half], lambda: sems(0), across_x)
            send(k, lambda: ref.at[plane(k), y, x, c, half:], lambda: sems(1), across_y)
            if a == 0:
                send(
                    k,
                    lambda: tables.at[plane(k), y, x, c],
                    lambda: table_plane_sem.at[k, 0],
                    across_x,
                )

        under(present(k), start)

    def second(a, k):
        ref = arrays[a]

        def sems(i):
            return plane_sem.at[a, k, i]

        def step():
            p = plane(k)
            arrived(ref.at[p, y, 1 - x, c, :half], sems(0))
            send(k, lambda: ref.at[plane(k), y, :, c, :half], lambda: sems(2), across_y)
            arrived(ref.at[p, 1 - y, x, c, half:], sems(1))
            send(k, lambda: ref.at[plane(k), :, x, c, half:], lambda: sems(3), across_x)
            if a == 0:
                arrived(tables.at[p, y, 1 - x, c], table_plane_sem.at[k, 0])
                send(
                    k,
                    lambda: tables.at[plane(k), y, :, c],
                    lambda: table_plane_sem.at[k, 1],
                    across_y,
                )

        under(present(k), step)

    def third(a, k):
        ref = arrays[a]

        def sems(i):
            return plane_sem.at[a, k, i]

        def step():
            p = plane(k)
            arrived(ref.at[p, 1 - y, :, c, :half], sems(2))
            arrived(ref.at[p, :, 1 - x, c, half:], sems(3))
            send(k, lambda: ref.at[plane(k), :, :, c], lambda: sems(4), sibling)
            if a == 0:
                arrived(tables.at[p, 1 - y, :, c], table_plane_sem.at[k, 1])
                send(
                    k,
                    lambda: tables.at[plane(k), :, :, c],
                    lambda: table_plane_sem.at[k, 2],
                    sibling,
                )

        under(present(k), step)

    def fourth(a, k):
        def step():
            p = plane(k)
            arrived(arrays[a].at[p, :, :, 1 - c], plane_sem.at[a, k, 4])
            if a == 0:
                arrived(tables.at[p, :, :, 1 - c], table_plane_sem.at[k, 2])

        under(present(k), step)

    copies = [
        pltpu.make_async_copy(grads, grads_all.at[z, y, x, c], local_sem.at[0]),
        pltpu.make_async_copy(table, tables.at[z, y, x, c], local_sem.at[1]),
        pltpu.make_async_copy(kv_mine, kv.at[z], local_sem.at[2]),
    ]
    for copy in copies:
        copy.start()
    weights = [
        pltpu.make_async_copy(down_weight, down_w, weight_sem.at[0]),
        pltpu.make_async_copy(gate_weight, gate_w, weight_sem.at[1]),
        pltpu.make_async_copy(up_weight, up_w, weight_sem.at[2]),
    ]
    for copy in weights:
        copy.start()
    for j in range(1, seqs):

        @pl.when(j > z)
        def _():
            kv[j] = jnp.zeros(kv.shape[1:], BF)

    barrier = pltpu.get_barrier_semaphore()
    for device in (sibling, across_x, across_y):
        pl.semaphore_signal(barrier, inc=1, device_id=device, device_id_type=MESH)

    @pl.when(z < top)
    def _():
        pl.semaphore_signal(barrier, inc=1, device_id=above, device_id_type=MESH)

    @pl.when(z > 0)
    def _():
        pl.semaphore_signal(barrier, inc=1, device_id=below, device_id_type=MESH)

    pl.semaphore_wait(barrier, 3 + (z < top).astype(jnp.int32) + (z > 0).astype(jnp.int32))
    for copy in copies:
        copy.wait()

    def kv_start(d):
        guard = both(z >= d if d else True, z < top)
        under(guard, lambda: send(guard, lambda: kv.at[z - d], lambda: kv_sem.at[d + 1], above))

    def kv_take(d):
        @pl.when(z >= d)
        def _():
            arrived(kv.at[z - d], kv_sem.at[d])

    kv_start(0)
    line_start(grads_all, lambda j: line_sem.at[0, j], 2)
    line_start(tables, lambda j: table_line_sem.at[j], 2)
    line_start(tables, lambda j: table_line_sem.at[j], 1)
    first(0, 0)
    for d in range(1, seqs):
        kv_take(d)
        if d < top:
            kv_start(d)
        if d == 1:
            second(0, 0)
        if d == 2:
            third(0, 0)
    line_start(grads_all, lambda j: line_sem.at[0, j], 1)
    keys = kv[...].reshape(seqs * tokens, kv.shape[2])
    attend_rows(group, residual, q, keys, att, log_total, inv_rms, normed)
    keep = [
        pltpu.make_async_copy(normed, normed_all.at[z, y, x, c], local_sem.at[3]),
        pltpu.make_async_copy(kv, kv_all, local_sem.at[4]),
    ]
    for copy in keep:
        copy.start()
    keep[0].wait()
    line_start(normed_all, lambda j: line_sem.at[1, j], 1)
    line_start(normed_all, lambda j: line_sem.at[1, j], 2)
    first(1, 0)

    local = slot.shape[0]
    ranks = slot.shape[1]
    depth = rows.shape[1] // ranks

    def chosen(i, r):
        row = lax.broadcasted_iota(jnp.int32, (depth, tokens), 0)
        return slot[i, pl.ds(r, 1), :] == row

    def span(r):
        return pl.ds(pl.multiple_of(r * depth, depth), depth)

    def each_rank(body):
        lax.fori_loop(0, ranks, lambda r, carry: (body(r), carry)[1], 0)

    def place(r):
        return (r // 4, lax.rem(r // 2, 2), lax.rem(r, 2))

    def find_slots():
        before = (
            lax.broadcasted_iota(jnp.int32, (tokens, tokens), 0)
            < lax.broadcasted_iota(jnp.int32, (tokens, tokens), 1)
        ).astype(F32).astype(BF)
        for i in range(local):
            mine = jnp.concatenate(
                [tabs[r // 4, r // 2 % 2, r % 2, pl.ds(e * local + i, 1), :] for r in range(ranks)],
                axis=0,
            )
            routed = mine >= 0.0
            rank = dot(routed.astype(F32).astype(BF), before, 1, 0)
            mix[i] = mine
            slot[i] = jnp.where(routed, rank.astype(jnp.int32), -1)

    def pick_into(target):
        def body(r):
            block = held[place(r)]
            for i in range(local):
                target[i, span(r), :] = dot(
                    chosen(i, r).astype(F32).astype(BF), block, 1, 0
                ).astype(BF)

        each_rank(body)

    def blend(i):
        def body(r):
            at = span(r)
            hit = chosen(i, r)
            share = jnp.sum(jnp.where(hit, mix[i, pl.ds(r, 1), :], 0.0), axis=1, keepdims=True)
            g, u, w = gate_pre[at, :], up_pre[at, :], raw[i, at, :]
            sigmoid = jax.nn.sigmoid(g)
            silu = g * sigmoid
            act = silu * u
            act_grad = w * share
            gate_grad[i, at, :] = (act_grad * u * sigmoid * (1.0 + g * (1.0 - sigmoid))).astype(BF)
            up_grad[i, at, :] = (act_grad * silu).astype(BF)
            mixed[i, at, :] = (act * share).astype(BF)
            total = jnp.sum(act.astype(BF).astype(F32) * w, axis=1, keepdims=True)
            token_dot[r, i : i + 1, :] = jnp.sum(jnp.where(hit, total, 0.0), axis=0, keepdims=True)

        each_rank(body)

    def spread(source, target):
        def body(r):
            total = None
            for i in range(local):
                part = dot(chosen(i, r).astype(F32).astype(BF), source[i, span(r), :], 0, 0)
                total = part if total is None else total + part
            target[place(r)] = total.astype(BF)

        each_rank(body)

    def hold(ref):
        copy = pltpu.make_async_copy(ref.at[z], held, local_sem.at[0])
        copy.start()
        copy.wait()

    outs = [
        pltpu.make_async_copy(pulls, grads_own, out_sem.at[0]),
        pltpu.make_async_copy(rows, rows_own, out_sem.at[1]),
        pltpu.make_async_copy(gate_grad, gate_own, out_sem.at[2]),
        pltpu.make_async_copy(up_grad, up_own, out_sem.at[3]),
        pltpu.make_async_copy(mixed, mixed_own, out_sem.at[4]),
        pltpu.make_async_copy(held, input_part, out_sem.at[5]),
        pltpu.make_async_copy(spare, out_part, out_sem.at[6]),
    ]

    def task_grads():
        fourth(0, 0)
        table_copy = pltpu.make_async_copy(tables.at[z], tabs, local_sem.at[1])
        table_copy.start()
        table_copy.wait()
        find_slots()
        hold(grads_all)
        pick_into(pulls)
        outs[0].start()

    def task_raw(i):
        if i == 0:
            weights[0].wait()
        raw[i] = dot(pulls[i], down_w[i], 1, 1)

    def task_rows():
        fourth(1, 0)
        hold(normed_all)
        pick_into(rows)
        outs[1].start()
        weights[1].wait()
        weights[2].wait()

    def task_gate(i):
        gate_pre[...] = dot(rows[i], gate_w[i], 1, 1)

    def task_up(i):
        up_pre[...] = dot(rows[i], up_w[i], 1, 1)

    def task_input(i):
        if i == 0:
            outs[0].wait()
            outs[1].wait()
        rows[i] = (dot(gate_grad[i], gate_w[i], 1, 0) + dot(up_grad[i], up_w[i], 1, 0)).astype(BF)

    def task_out(i):
        pulls[i] = dot(mixed[i], down_w[i], 1, 0).astype(BF)

    def task_spread_input():
        for copy in outs[2:5]:
            copy.start()
        spread(rows, held)
        outs[5].start()

    def task_spread_out():
        spread(pulls, spare)
        outs[6].start()

    parts = ((held, input_part, input_sum), (spare, out_part, out_sum))
    pieces = 4

    def in_pieces(body):
        step = half // pieces

        def run(j, carry):
            body(pl.ds(pl.multiple_of(j * step, step), step), step)
            return carry

        lax.fori_loop(0, pieces, run, 0)

    def sum_pair_send(a):
        outs[5 + a].wait()
        view = parts[a][1]
        pltpu.make_async_remote_copy(
            src_ref=view.at[:, :, 1 - c],
            dst_ref=pair_sum.at[a],
            send_sem=sum_sem.at[a, 0, 0],
            recv_sem=sum_sem.at[a, 0, 1],
            device_id=sibling,
            device_id_type=MESH,
        ).start()

    def sum_pair_take(a):
        arrived(pair_sum.at[a], sum_sem.at[a, 0])
        for yy in range(2):
            for xx in range(2):

                def body(at, step):
                    mine = parts[a][0][yy, xx, c, at, :].astype(F32)
                    pair_sum[a, yy, xx, at, :] = (
                        mine + pair_sum[a, yy, xx, at, :].astype(F32)
                    ).astype(BF)

                def both_halves(at, step):
                    body(at, step)
                    low = pl.ds(pl.multiple_of(half + at.start, step), step)
                    body(low, step)

                in_pieces(both_halves)

    def half_copies(a):
        return (
            pltpu.make_async_remote_copy(
                src_ref=pair_sum.at[a, :, 1 - x, :half],
                dst_ref=line_sum.at[a, 0],
                send_sem=sum_sem.at[a, 1, 0],
                recv_sem=sum_sem.at[a, 1, 1],
                device_id=across_x,
                device_id_type=MESH,
            ),
            pltpu.make_async_remote_copy(
                src_ref=pair_sum.at[a, 1 - y, :, half:],
                dst_ref=line_sum.at[a, 1],
                send_sem=sum_sem.at[a, 2, 0],
                recv_sem=sum_sem.at[a, 2, 1],
                device_id=across_y,
                device_id_type=MESH,
            ),
        )

    def last_copies(a):
        return tuple(
            pltpu.make_async_remote_copy(
                src_ref=line_sum.at[a, i, 1 - (y, x)[i]],
                dst_ref=last_sum.at[a, i],
                send_sem=sum_sem.at[a, 3 + i, 0],
                recv_sem=sum_sem.at[a, 3 + i, 1],
                device_id=(across_y, across_x)[i],
                device_id_type=MESH,
            )
            for i in range(2)
        )

    def sum_line_send(a):
        for copy in half_copies(a):
            copy.start()

    def sum_line_take(a):
        for copy in half_copies(a):
            copy.wait_recv()
        for j in range(2):

            def body(at, step):
                low = pl.ds(pl.multiple_of(half + at.start, step), step)
                line_sum[a, 0, j, at, :] = (
                    line_sum[a, 0, j, at, :].astype(F32) + pair_sum[a, j, x, at, :].astype(F32)
                ).astype(BF)
                line_sum[a, 1, j, at, :] = (
                    line_sum[a, 1, j, at, :].astype(F32) + pair_sum[a, y, j, low, :].astype(F32)
                ).astype(BF)

            in_pieces(body)

    def sum_last_send(a):
        for copy in last_copies(a):
            copy.start()

    def sum_last_take(a):
        for copy in last_copies(a):
            copy.wait_recv()

        def body(at, step):
            low = pl.ds(pl.multiple_of(half + at.start, step), step)
            total = parts[a][2]
            total[at, :] = (
                line_sum[a, 0, y, at, :].astype(F32) + last_sum[a, 0, at, :].astype(F32)
            ).astype(BF)
            total[low, :] = (
                line_sum[a, 1, x, at, :].astype(F32) + last_sum[a, 1, at, :].astype(F32)
            ).astype(BF)

        in_pieces(body)

    def sum_end(a):
        view = parts[a][1].at[:, :, 1 - c]
        copy_of(view, sum_sem.at[a, 0], sibling).wait_send()
        for copy in half_copies(a) + last_copies(a):
            copy.wait_send()

    task_grads()
    task_raw(0)
    second(1, 0)
    order = []
    for d in range(1, seqs):
        for a in range(2):
            order += [(a, 2 * d - 1), (a, 2 * d)]
    tasks = [functools.partial(task_raw, i) for i in range(1, local)]
    tasks += [lambda: third(1, 0), task_rows]
    for i in range(local):
        tasks += [
            functools.partial(task, i) for task in (task_gate, task_up, blend, task_input, task_out)
        ]
    tasks += [task_spread_input, task_spread_out]
    for step in (
        sum_pair_send,
        sum_pair_take,
        sum_line_send,
        sum_line_take,
        sum_last_send,
        sum_last_take,
    ):
        tasks += [functools.partial(step, a) for a in range(2)]
    for i in range(max(len(order) + 4, len(tasks))):
        if i < len(order):
            first(*order[i])
        if 0 <= i - 2 < len(order):
            second(*order[i - 2])
        if 0 <= i - 4 < len(order):
            third(*order[i - 4])
        if i < len(tasks):
            tasks[i]()
    for copy in outs[2:5]:
        copy.wait()
    for a in range(2):
        sum_end(a)
    keep[1].wait()
    for a, k in order:
        fourth(a, k)
    for guard, finish in sends:
        under(present(guard) if isinstance(guard, int) else guard, finish)


def front(residual, q, kv_mine, table, grads, weights, group, seqs, ranks, depth):
    tokens, width = q.shape
    heads = width // DH
    slots = 2 * seqs - 1
    local, hidden, _ = weights[0].shape
    any_space = pl.BlockSpec(memory_space=pl.ANY)
    dma = pltpu.SemaphoreType.DMA
    picked = (local, ranks * depth, width)
    units = (local, ranks * depth, hidden)
    plane = (2, 2, 2, tokens, width)
    return pl.pallas_call(
        functools.partial(front_kernel, group, seqs),
        out_shape=(
            jax.ShapeDtypeStruct((tokens, width), BF),
            jax.ShapeDtypeStruct((tokens, heads), F32),
            jax.ShapeDtypeStruct((tokens, 1), F32),
            jax.ShapeDtypeStruct((ranks, local, tokens), F32),
            jax.ShapeDtypeStruct((tokens, width), BF),
            jax.ShapeDtypeStruct((tokens, width), BF),
            jax.ShapeDtypeStruct((seqs,) + kv_mine.shape, BF),
            jax.ShapeDtypeStruct((seqs,) + plane, BF),
            jax.ShapeDtypeStruct((seqs,) + plane, BF),
            jax.ShapeDtypeStruct((seqs, 2, 2, 2) + table.shape, F32),
            jax.ShapeDtypeStruct(picked, BF),
            jax.ShapeDtypeStruct(picked, BF),
            jax.ShapeDtypeStruct(units, BF),
            jax.ShapeDtypeStruct(units, BF),
            jax.ShapeDtypeStruct(units, BF),
            jax.ShapeDtypeStruct(plane, BF),
            jax.ShapeDtypeStruct(plane, BF),
        ),
        in_specs=[vm()] * 5 + [any_space] * 3,
        out_specs=(vm(),) * 6 + (any_space,) * 11,
        scratch_shapes=[
            pltpu.VMEM((seqs,) + kv_mine.shape, BF),
            pltpu.VMEM((tokens, width), BF),
            pltpu.VMEM(weights[0].shape, BF),
            pltpu.VMEM(weights[1].shape, BF),
            pltpu.VMEM(weights[2].shape, BF),
            pltpu.VMEM((2, 2, 2) + table.shape, F32),
            pltpu.VMEM((local, ranks, tokens), F32),
            pltpu.VMEM((local, ranks, tokens), jnp.int32),
            pltpu.VMEM(plane, BF),
            pltpu.VMEM(plane, BF),
            pltpu.VMEM((2, 2, 2, tokens, width), BF),
            pltpu.VMEM((2, 2, 2, tokens // 2, width), BF),
            pltpu.VMEM((2, 2, tokens // 2, width), BF),
            pltpu.VMEM(picked, BF),
            pltpu.VMEM(picked, BF),
            pltpu.VMEM(units, F32),
            pltpu.VMEM(units[1:], F32),
            pltpu.VMEM(units[1:], F32),
            pltpu.VMEM(units, BF),
            pltpu.VMEM(units, BF),
            pltpu.VMEM(units, BF),
            dma((5,)),
            dma((3,)),
            dma((7,)),
            dma((2, 5, 2)),
            dma((seqs, 2)),
            dma((2, slots, 2)),
            dma((2, slots, 5, 2)),
            dma((slots, 2)),
            dma((slots, 3, 2)),
        ],
        compiler_params=pltpu.CompilerParams(
            collective_id=0, has_side_effects=True, vmem_limit_bytes=FRONT_LIMIT
        ),
        cost_estimate=pl.CostEstimate(
            flops=4 * tokens * seqs * tokens * width + 12 * local * ranks * depth * width * hidden,
            bytes_accessed=32 * seqs * tokens * width,
            transcendentals=heads * tokens * seqs * tokens,
        ),
        name="front",
    )(residual, q, kv_mine, table, grads, *weights)


def attend_back_kernel(
    group, residual, q, kv, att, log_total, inv_rms, grad_out, normed_grad, res_grad, q_grad, kv_part
):
    tokens = q.shape[0]
    full = kv.shape[0]
    kv_heads = kv.shape[1] // (2 * DH)
    scale = 1.0 / math.sqrt(DH)
    inv = inv_rms[...]
    normed = (residual[...].astype(F32) + att[...].astype(F32)) * inv
    ngrad = normed_grad[...].astype(F32)
    dot_mean = jnp.mean(ngrad * normed, axis=1, keepdims=True)
    res_grad[...] = (grad_out[...].astype(F32) + inv * (ngrad - normed * dot_mean)).astype(BF)
    visible = visible_mask(tokens, group, full, lax.axis_index("seq"))
    for k in range(kv_heads):
        qh = heads_of(q, k * group, group)
        oh = heads_of(att, k * group, group)
        gh = heads_of(res_grad, k * group, group)
        logs = jnp.concatenate(
            [log_total[:, k * group + g : k * group + g + 1] for g in range(group)], axis=0
        )
        kh = kv[:, k * DH : (k + 1) * DH]
        vh = kv[:, (kv_heads + k) * DH : (kv_heads + k + 1) * DH]
        scores = jnp.where(visible, dot(qh, kh, 1, 1) * scale, neg_big)
        probs = jnp.exp(scores - logs)
        delta = jnp.sum(gh.astype(F32) * oh.astype(F32), axis=1, keepdims=True)
        pgrad = dot(gh, vh, 1, 1)
        sgrad = (probs * (pgrad - delta)).astype(BF)
        dq = (dot(sgrad, kh, 1, 0) * scale).astype(BF)
        for g in range(group):
            h = k * group + g
            q_grad[:, h * DH : (h + 1) * DH] = dq[g * tokens : (g + 1) * tokens]
        kv_part[:, k * DH : (k + 1) * DH] = (dot(sgrad, qh, 0, 0) * scale).astype(BF)
        kv_part[:, (kv_heads + k) * DH : (kv_heads + k + 1) * DH] = dot(
            probs.astype(BF), gh, 0, 0
        ).astype(BF)


def attend_back(group, residual, q, kv, att, log_total, inv_rms, grad_out, normed_grad):
    tokens, width = q.shape
    return pl.pallas_call(
        functools.partial(attend_back_kernel, group),
        out_shape=(
            jax.ShapeDtypeStruct((tokens, width), BF),
            jax.ShapeDtypeStruct((tokens, width), BF),
            jax.ShapeDtypeStruct(kv.shape, BF),
        ),
        in_specs=[vm()] * 8,
        out_specs=(vm(),) * 3,
        compiler_params=pltpu.CompilerParams(vmem_limit_bytes=VMEM_LIMIT),
        cost_estimate=pl.CostEstimate(
            flops=10 * tokens * kv.shape[0] * width,
            bytes_accessed=14 * tokens * width + 4 * kv.size,
            transcendentals=tokens * kv.shape[0] * (width // DH),
        ),
        name="attend_back",
    )(residual, q, kv, att, log_total, inv_rms, grad_out, normed_grad)


def pick_kernel(seq_index, slot, rows, picked):
    local = slot.shape[2]
    depth = picked.shape[1]
    tokens = rows.shape[2]
    row = lax.broadcasted_iota(jnp.int32, (depth, tokens), 0)
    for e in range(local):
        chosen = (slot[0, 0, e : e + 1, :] == row).astype(F32).astype(BF)
        picked[e] = dot(chosen, rows[0, 0], 1, 0).astype(BF)


def pick_rows(gathered, slot, seq_index, first, planes, depth):
    seqs, ranks, tokens, width = gathered.shape
    local = slot.shape[2]
    count = planes * ranks

    def source(i, s):
        return (lax.rem(s[0] + first + i // ranks, seqs), lax.rem(i, ranks), 0, 0)

    return pl.pallas_call(
        pick_kernel,
        out_shape=jax.ShapeDtypeStruct((local, count * depth, width), BF),
        grid_spec=pltpu.PrefetchScalarGridSpec(
            num_scalar_prefetch=1,
            grid=(count,),
            in_specs=[
                pl.BlockSpec((1, 1, local, tokens), source),
                pl.BlockSpec((1, 1, tokens, width), source),
            ],
            out_specs=pl.BlockSpec((local, depth, width), lambda i, s: (0, i, 0)),
        ),
        compiler_params=pltpu.CompilerParams(vmem_limit_bytes=16 * 1024 * 1024),
        cost_estimate=pl.CostEstimate(
            flops=2 * local * count * depth * tokens * width,
            bytes_accessed=2 * count * (tokens + local * depth) * width,
            transcendentals=0,
        ),
        name="pick_rows",
    )(seq_index, slot, gathered)


def spread_kernel(slot, rows, out):
    ranks, local, tokens = slot.shape
    depth = rows.shape[1]
    row = lax.broadcasted_iota(jnp.int32, (depth, tokens), 0)
    total = None
    for e in range(local):
        chosen = (slot[0, e : e + 1, :] == row).astype(F32).astype(BF)
        part = dot(chosen, rows[e], 0, 0)
        total = part if total is None else total + part
    out[0] = total.astype(BF)


def spread_rows(rows, slot):
    ranks, local, tokens = slot.shape
    width = rows.shape[2]
    depth = rows.shape[1] // ranks
    return pl.pallas_call(
        spread_kernel,
        out_shape=jax.ShapeDtypeStruct((ranks, tokens, width), BF),
        grid=(ranks,),
        in_specs=[
            pl.BlockSpec((1, local, tokens), lambda i: (i, 0, 0)),
            pl.BlockSpec((local, depth, width), lambda i: (0, i, 0)),
        ],
        out_specs=pl.BlockSpec((1, tokens, width), lambda i: (i, 0, 0)),
        compiler_params=pltpu.CompilerParams(vmem_limit_bytes=16 * 1024 * 1024),
        cost_estimate=pl.CostEstimate(
            flops=2 * local * ranks * depth * tokens * width,
            bytes_accessed=2 * ranks * (tokens + local * depth) * width,
            transcendentals=0,
        ),
        name="spread_rows",
    )(slot, rows)


def hidden_units(rows, grads, mix, gate_weight, up_weight, down_weight):
    gate_pre = jnp.einsum("erd,edf->erf", rows, gate_weight, preferred_element_type=F32)
    up_pre = jnp.einsum("erd,edf->erf", rows, up_weight, preferred_element_type=F32)
    raw = jnp.einsum("erd,efd->erf", grads, down_weight, preferred_element_type=F32)
    sigmoid = jax.nn.sigmoid(gate_pre)
    silu = gate_pre * sigmoid
    act = silu * up_pre
    act_grad = raw * mix[:, :, None]
    gate_grad = (act_grad * up_pre * sigmoid * (1.0 + gate_pre * (1.0 - sigmoid))).astype(BF)
    up_grad = (act_grad * silu).astype(BF)
    mixed = (act * mix[:, :, None]).astype(BF)
    return (gate_grad, up_grad, mixed, act, raw)


def on_device(
    residual,
    queries,
    key_input,
    value_input,
    routes,
    mix_weights,
    gate_weight,
    up_weight,
    down_weight,
    grad_out,
):
    tokens = residual.shape[1]
    width = residual.shape[2]
    kv_width = key_input.shape[2]
    group = queries.shape[2] // kv_width
    local = gate_weight.shape[0]
    ranks = lax.axis_size("expert")
    seqs = lax.axis_size("seq")
    experts = local * ranks
    top_count = routes.shape[2]
    capacity = tokens * top_count * 5 // (4 * experts)
    depth = -(-capacity // 16) * 16
    both = ("seq", "expert")
    both_size = seqs * ranks
    seq_index = lax.axis_index("seq")
    rank_index = lax.axis_index("expert")
    seq_array = seq_index.astype(jnp.int32).reshape(1)

    kv_mine = jnp.concatenate(
        [key_input.reshape(tokens, kv_width), value_input.reshape(tokens, kv_width)], axis=1
    )
    expert_ids = jnp.arange(experts, dtype=jnp.int32)
    picked = routes.reshape(tokens, top_count)
    mix_rows = mix_weights.reshape(tokens, top_count)
    hit = picked[None, :, :] == expert_ids[:, None, None]
    table = jnp.sum(jnp.where(hit, mix_rows[None], 0.0), axis=2) - (
        1.0 - jnp.sum(hit.astype(F32), axis=2)
    )
    grad_rows = grad_out.reshape(tokens, width)
    q = queries.reshape(tokens, width)
    res = residual.reshape(tokens, width)
    weights = (gate_weight, up_weight, down_weight)
    paired = ranks == 8 and 2 * both_size * grad_rows.size <= GATHER_BYTES
    if paired:
        (
            att,
            log_total,
            inv_rms,
            token_dot,
            normed_grad,
            routed_out,
            kv,
            grads_all,
            normed_all,
            tables,
            rows_own,
            grads_own,
            gate_own,
            up_own,
            mixed_own,
            _,
            _,
        ) = front(
            res,
            q,
            kv_mine,
            table,
            grad_rows,
            (jnp.swapaxes(gate_weight, 1, 2), jnp.swapaxes(up_weight, 1, 2), down_weight),
            group,
            seqs,
            ranks,
            depth,
        )
        kv = kv.reshape(seqs * tokens, 2 * kv_width)
        grads_all = grads_all.reshape(seqs, ranks, tokens, width)
        normed_all = normed_all.reshape(seqs, ranks, tokens, width)
        tables = tables.reshape(seqs * ranks, experts, tokens)
    else:
        kv = lax.all_gather(kv_mine, "seq", axis=0, tiled=True)
        tables = lax.all_gather(table, both, axis=0, tiled=False)
        grads_all = lax.all_gather(grad_rows, both, axis=0, tiled=True)
        grads_all = grads_all.reshape(seqs, ranks, tokens, width)
        att, log_total, inv_rms, normed_bf = attend(res, q, kv, group)
    mine = lax.dynamic_slice_in_dim(tables, rank_index * local, local, axis=1)
    routed = mine >= 0.0
    before = jnp.triu(jnp.ones((tokens, tokens), BF), 1)
    rank = jnp.einsum("bet,tu->beu", routed.astype(BF), before, preferred_element_type=F32)
    slot = jnp.where(routed, rank.astype(jnp.int32), -1)
    slot = slot.reshape(seqs, ranks, local, tokens)
    mine = mine.reshape(seqs, ranks, local, tokens)

    grads_far = pick_rows(grads_all, slot, seq_array, 1, seqs - 1, depth)
    if not paired:
        grads_own = pick_rows(grads_all, slot, seq_array, 0, 1, depth)
        normed_bf, grads_own, grads_far = lax.optimization_barrier(
            (normed_bf, grads_own, grads_far)
        )
        normed_all = lax.all_gather(normed_bf, both, axis=0, tiled=True)
        normed_all = normed_all.reshape(seqs, ranks, tokens, width)

    slot_turned = jnp.roll(slot, -seq_index, axis=0)
    mix_turned = jnp.roll(mine, -seq_index, axis=0)
    here = slot_turned[..., None, :] == jnp.arange(depth, dtype=jnp.int32)[:, None]
    mix_slot = jnp.sum(jnp.where(here, mix_turned[..., None, :], 0.0), axis=4)
    mix_slot = jnp.transpose(mix_slot, (2, 0, 1, 3)).reshape(local, seqs * ranks * depth)
    own = ranks * depth

    rows_far = pick_rows(normed_all, slot, seq_array, 1, seqs - 1, depth)
    if not paired:
        rows_own = pick_rows(normed_all, slot, seq_array, 0, 1, depth)
        gate_own, up_own, mixed_own, act_own, raw_own = hidden_units(
            rows_own, grads_own, mix_slot[:, :own], *weights
        )
        input_grad = (
            jnp.einsum("erf,edf->erd", gate_own, gate_weight, preferred_element_type=F32)
            + jnp.einsum("erf,edf->erd", up_own, up_weight, preferred_element_type=F32)
        ).astype(BF)
        slot_own = slot_turned[0]
        input_part = spread_rows(input_grad, slot_own).reshape(ranks * tokens, width)
        expert_out = jnp.einsum(
            "erf,efd->erd", mixed_own, down_weight, preferred_element_type=F32
        ).astype(BF)
        out_part = spread_rows(expert_out, slot_own).reshape(ranks * tokens, width)
        pair_dot = jnp.sum(act_own.astype(BF).astype(F32) * raw_own, axis=2)
        pair_dot = pair_dot.reshape(local, ranks, depth)
        token_dot = jnp.sum(
            jnp.where(here[0], jnp.transpose(pair_dot, (1, 0, 2))[..., None], 0.0), axis=2
        )
        normed_grad = lax.psum_scatter(input_part, "expert", scatter_dimension=0, tiled=True)
        routed_out = lax.psum_scatter(out_part, "expert", scatter_dimension=0, tiled=True)
    hidden = res.astype(F32) + att.astype(F32)
    layer_out = (hidden + routed_out.astype(F32)).astype(BF)

    dots = lax.all_to_all(token_dot, "expert", split_axis=0, concat_axis=0, tiled=True)
    dots = dots.reshape(experts, tokens)
    mix_grad = jnp.sum(jnp.where(hit, dots[:, :, None], 0.0), axis=0)

    gate_far, up_far, mixed_far, _, _ = hidden_units(
        rows_far, grads_far, mix_slot[:, own:], *weights
    )
    share = width // seqs

    def columns(array):
        return lax.dynamic_slice_in_dim(array, seq_index * share, share, axis=2)

    def outer(a_own, a_far, b_own, b_far):
        return (
            jnp.einsum("erm,ern->emn", a_own, b_own, preferred_element_type=F32)
            + jnp.einsum("erm,ern->emn", a_far, b_far, preferred_element_type=F32)
        ).astype(BF)

    cols_own, cols_far = columns(rows_own), columns(rows_far)
    gate_share = outer(cols_own, cols_far, gate_own, gate_far)
    up_share = outer(cols_own, cols_far, up_own, up_far)
    down_share = outer(mixed_own, mixed_far, columns(grads_own), columns(grads_far))

    res_grad, q_grad, kv_part = attend_back(
        group, res, q, kv, att, log_total, inv_rms, grad_rows, normed_grad
    )
    kv_share = lax.psum_scatter(kv_part, "seq", scatter_dimension=0, tiled=True)
    return (
        layer_out.reshape(1, tokens, width),
        res_grad.reshape(1, tokens, width),
        q_grad.reshape(1, tokens, width),
        kv_share[:, :kv_width].reshape(1, tokens, kv_width),
        kv_share[:, kv_width:].reshape(1, tokens, kv_width),
        mix_grad.reshape(1, tokens, top_count),
        gate_share,
        up_share,
        down_share,
    )


def solution(mesh):
    rows = P("expert", "seq", None)
    weight = P("expert", None, None)
    return jax.shard_map(
        on_device,
        mesh=mesh,
        in_specs=(rows,) * 6 + (weight,) * 3 + (rows,),
        out_specs=(rows,) * 8 + (P("expert", None, "seq"),),
        check_vma=False,
    )
```

```python
import functools
import math

import jax
import jax.numpy as jnp
from jax import lax
from jax.experimental import pallas as pl
from jax.experimental.pallas import tpu as pltpu
from jax.sharding import PartitionSpec as P

DH = 128
neg_big = -1e30
norm_eps = 1e-06
BF = jnp.bfloat16
F32 = jnp.float32
GATHER_BYTES = 32 * 1024 * 1024
FRONT_LIMIT = 62 * 1024 * 1024
TASKS = 3
MESH = pl.DeviceIdType.MESH
VMEM_LIMIT = 56 * 1024 * 1024


def dot(a, b, ca, cb):
    return lax.dot_general(a, b, (((ca,), (cb,)), ((), ())), preferred_element_type=F32)


def vm():
    return pl.BlockSpec(memory_space=pltpu.VMEM)


def heads_of(ref, first, count):
    return jnp.concatenate(
        [ref[:, (first + g) * DH : (first + g + 1) * DH] for g in range(count)], axis=0
    )


def visible_mask(tokens, group, full, seq_index):
    shape = (group, tokens, full)
    pos = lax.broadcasted_iota(jnp.int32, shape, 1) + seq_index * tokens
    key = lax.broadcasted_iota(jnp.int32, shape, 2)
    return (key <= pos).reshape(group * tokens, full)


def attend_kernel(group, residual, q, kv, att, log_total, inv_rms, normed):
    tokens = q.shape[0]
    full = kv.shape[0]
    kv_heads = kv.shape[1] // (2 * DH)
    visible = visible_mask(tokens, group, full, lax.axis_index("seq"))
    scale = 1.0 / math.sqrt(DH)
    for k in range(kv_heads):
        qh = heads_of(q, k * group, group)
        kh = kv[:, k * DH : (k + 1) * DH]
        vh = kv[:, (kv_heads + k) * DH : (kv_heads + k + 1) * DH]
        scores = jnp.where(visible, dot(qh, kh, 1, 1) * scale, neg_big)
        top = jnp.max(scores, axis=1, keepdims=True)
        weights = jnp.exp(scores - top)
        total = jnp.sum(weights, axis=1, keepdims=True)
        out = (dot(weights.astype(BF), vh, 1, 0) / total).astype(BF)
        logs = top + jnp.log(total)
        for g in range(group):
            h = k * group + g
            att[:, h * DH : (h + 1) * DH] = out[g * tokens : (g + 1) * tokens]
            log_total[:, h : h + 1] = logs[g * tokens : (g + 1) * tokens]
    hidden = residual[...].astype(F32) + att[...].astype(F32)
    inv = lax.rsqrt(jnp.mean(hidden * hidden, axis=1, keepdims=True) + norm_eps)
    inv_rms[...] = inv
    normed[...] = (hidden * inv).astype(BF)


def attend(residual, q, kv, group):
    tokens, width = q.shape
    heads = width // DH
    return pl.pallas_call(
        functools.partial(attend_kernel, group),
        out_shape=(
            jax.ShapeDtypeStruct((tokens, width), BF),
            jax.ShapeDtypeStruct((tokens, heads), F32),
            jax.ShapeDtypeStruct((tokens, 1), F32),
            jax.ShapeDtypeStruct((tokens, width), BF),
        ),
        in_specs=[vm()] * 3,
        out_specs=(vm(),) * 4,
        compiler_params=pltpu.CompilerParams(vmem_limit_bytes=VMEM_LIMIT),
        cost_estimate=pl.CostEstimate(
            flops=4 * tokens * kv.shape[0] * width,
            bytes_accessed=8 * tokens * width + 2 * kv.size,
            transcendentals=heads * tokens * kv.shape[0],
        ),
        name="attend",
    )(residual, q, kv)


def attend_rows(group, residual, q, kv, att, log_total, inv_rms, normed):
    tokens = q.shape[0]
    full = kv.shape[0]
    kv_heads = kv.shape[1] // (2 * DH)
    visible = visible_mask(tokens, group, full, lax.axis_index("seq"))
    scale = 1.0 / math.sqrt(DH)
    for k in range(kv_heads):
        qh = heads_of(q, k * group, group)
        kh = kv[:, k * DH : (k + 1) * DH]
        vh = kv[:, (kv_heads + k) * DH : (kv_heads + k + 1) * DH]
        scores = jnp.where(visible, dot(qh, kh, 1, 1) * scale, neg_big)
        top = jnp.max(scores, axis=1, keepdims=True)
        weights = jnp.exp(scores - top)
        total = jnp.sum(weights, axis=1, keepdims=True)
        out = (dot(weights.astype(BF), vh, 1, 0) / total).astype(BF)
        logs = top + jnp.log(total)
        for g in range(group):
            h = k * group + g
            att[:, h * DH : (h + 1) * DH] = out[g * tokens : (g + 1) * tokens]
            log_total[:, h : h + 1] = logs[g * tokens : (g + 1) * tokens]
    hidden = residual[...].astype(F32) + att[...].astype(F32)
    inv = lax.rsqrt(jnp.mean(hidden * hidden, axis=1, keepdims=True) + norm_eps)
    inv_rms[...] = inv
    normed[...] = (hidden * inv).astype(BF)


def front_kernel(
    group,
    seqs,
    residual,
    q,
    kv_mine,
    table,
    grads,
    gate_weight,
    up_weight,
    down_weight,
    att,
    log_total,
    inv_rms,
    token_dot,
    input_sum,
    out_sum,
    kv_all,
    grads_all,
    normed_all,
    tables,
    rows_cols,
    pulls_cols,
    gate_all,
    up_all,
    mixed_all,
    input_part,
    out_part,
    kv,
    normed,
    gate_w,
    up_w,
    down_w,
    tabs,
    mix,
    slot,
    held,
    spare,
    pair_sum,
    line_sum,
    last_sum,
    rows,
    pulls,
    raw,
    gate_pre,
    up_pre,
    gate_grad,
    up_grad,
    mixed,
    local_sem,
    weight_sem,
    out_sem,
    part_sem,
    sum_sem,
    kv_sem,
    line_sem,
    plane_sem,
    table_line_sem,
    table_plane_sem,
):
    z = lax.axis_index("seq")
    e = lax.axis_index("expert")
    c, x, y = lax.rem(e, 2), lax.rem(e // 2, 2), e // 4
    tokens = q.shape[0]
    half = tokens // 2
    sibling = {"expert": e + 1 - 2 * c}
    across_x = {"expert": e + 2 - 4 * x}
    across_y = {"expert": e + 4 - 8 * y}
    above, below = {"seq": z + 1}, {"seq": z - 1}
    top = seqs - 1
    arrays = (grads_all, normed_all)
    sends = []

    def copy_of(view, sems, device):
        return pltpu.make_async_remote_copy(
            src_ref=view,
            dst_ref=view,
            send_sem=sems.at[0],
            recv_sem=sems.at[1],
            device_id=device,
            device_id_type=MESH,
        )

    def send(guard, view, sems, device):
        copy_of(view(), sems(), device).start()
        sends.append((guard, lambda: copy_of(view(), sems(), device).wait_send()))

    def arrived(view, sems):
        copy_of(view, sems, sibling).wait_recv()

    def under(guard, body):
        if guard is True:
            body()
        else:
            pl.when(guard)(body)

    def plane(k):
        d = (k + 1) // 2
        return z if k == 0 else (z - d if k % 2 else z + d)

    def present(k):
        d = (k + 1) // 2
        return True if k == 0 else (z >= d if k % 2 else z + d <= top)

    def forwarded(k):
        d = (k + 1) // 2
        return z + 1 <= top if k % 2 else z >= 1

    def both(a, b):
        return b if a is True else (a if b is True else jnp.logical_and(a, b))

    def line_start(ref, sems, k):
        guard = both(present(k - 2) if k > 2 else True, forwarded(k))

        def block():
            return ref.at[plane(k - 2) if k > 2 else z, y, x, c]

        under(guard, lambda: send(guard, block, lambda: sems(k), above if k % 2 else below))

    def first(a, k):
        ref = arrays[a]

        def sems(i):
            return plane_sem.at[a, k, i]

        if k:

            def take():
                arrived(ref.at[plane(k), y, x, c], line_sem.at[a, k])
                if a == 0:
                    arrived(tables.at[plane(k), y, x, c], table_line_sem.at[k])

            under(present(k), take)
            if k + 2 <= 2 * top:
                line_start(ref, lambda j: line_sem.at[a, j], k + 2)
                if a == 0:
                    line_start(tables, lambda j: table_line_sem.at[j], k + 2)

        def start():
            send(k, lambda: ref.at[plane(k), y, x, c, :half], lambda: sems(0), across_x)
            send(k, lambda: ref.at[plane(k), y, x, c, half:], lambda: sems(1), across_y)
            if a == 0:
                send(
                    k,
                    lambda: tables.at[plane(k), y, x, c],
                    lambda: table_plane_sem.at[k, 0],
                    across_x,
                )

        under(present(k), start)

    def second(a, k):
        ref = arrays[a]

        def sems(i):
            return plane_sem.at[a, k, i]

        def step():
            p = plane(k)
            arrived(ref.at[p, y, 1 - x, c, :half], sems(0))
            send(k, lambda: ref.at[plane(k), y, :, c, :half], lambda: sems(2), across_y)
            arrived(ref.at[p, 1 - y, x, c, half:], sems(1))
            send(k, lambda: ref.at[plane(k), :, x, c, half:], lambda: sems(3), across_x)
            if a == 0:
                arrived(tables.at[p, y, 1 - x, c], table_plane_sem.at[k, 0])
                send(
                    k,
                    lambda: tables.at[plane(k), y, :, c],
                    lambda: table_plane_sem.at[k, 1],
                    across_y,
                )

        under(present(k), step)

    def third(a, k):
        ref = arrays[a]

        def sems(i):
            return plane_sem.at[a, k, i]

        def step():
            p = plane(k)
            arrived(ref.at[p, 1 - y, :, c, :half], sems(2))
            arrived(ref.at[p, :, 1 - x, c, half:], sems(3))
            send(k, lambda: ref.at[plane(k), :, :, c], lambda: sems(4), sibling)
            if a == 0:
                arrived(tables.at[p, 1 - y, :, c], table_plane_sem.at[k, 1])
                send(
                    k,
                    lambda: tables.at[plane(k), :, :, c],
                    lambda: table_plane_sem.at[k, 2],
                    sibling,
                )

        under(present(k), step)

    def fourth(a, k):
        def step():
            p = plane(k)
            arrived(arrays[a].at[p, :, :, 1 - c], plane_sem.at[a, k, 4])
            if a == 0:
                arrived(tables.at[p, :, :, 1 - c], table_plane_sem.at[k, 2])

        under(present(k), step)

    copies = [
        pltpu.make_async_copy(grads, grads_all.at[z, y, x, c], local_sem.at[0]),
        pltpu.make_async_copy(table, tables.at[z, y, x, c], local_sem.at[1]),
        pltpu.make_async_copy(kv_mine, kv.at[z], local_sem.at[2]),
    ]
    for copy in copies:
        copy.start()
    weights = [
        pltpu.make_async_copy(down_weight, down_w, weight_sem.at[0]),
        pltpu.make_async_copy(gate_weight, gate_w, weight_sem.at[1]),
        pltpu.make_async_copy(up_weight, up_w, weight_sem.at[2]),
    ]
    for copy in weights:
        copy.start()
    for j in range(1, seqs):

        @pl.when(j > z)
        def _():
            kv[j] = jnp.zeros(kv.shape[1:], BF)

    barrier = pltpu.get_barrier_semaphore()
    for device in (sibling, across_x, across_y):
        pl.semaphore_signal(barrier, inc=1, device_id=device, device_id_type=MESH)

    @pl.when(z < top)
    def _():
        pl.semaphore_signal(barrier, inc=1, device_id=above, device_id_type=MESH)

    @pl.when(z > 0)
    def _():
        pl.semaphore_signal(barrier, inc=1, device_id=below, device_id_type=MESH)

    pl.semaphore_wait(barrier, 3 + (z < top).astype(jnp.int32) + (z > 0).astype(jnp.int32))
    for copy in copies:
        copy.wait()

    def kv_start(d):
        guard = both(z >= d if d else True, z < top)
        under(guard, lambda: send(guard, lambda: kv.at[z - d], lambda: kv_sem.at[d + 1], above))

    def kv_take(d):
        @pl.when(z >= d)
        def _():
            arrived(kv.at[z - d], kv_sem.at[d])

    kv_start(0)
    line_start(grads_all, lambda j: line_sem.at[0, j], 2)
    line_start(tables, lambda j: table_line_sem.at[j], 2)
    line_start(tables, lambda j: table_line_sem.at[j], 1)
    first(0, 0)
    for d in range(1, seqs):
        kv_take(d)
        if d < top:
            kv_start(d)
        if d == 1:
            second(0, 0)
        if d == 2:
            third(0, 0)
    line_start(grads_all, lambda j: line_sem.at[0, j], 1)
    keys = kv[...].reshape(seqs * tokens, kv.shape[2])
    attend_rows(group, residual, q, keys, att, log_total, inv_rms, normed)
    keep = [
        pltpu.make_async_copy(normed, normed_all.at[z, y, x, c], local_sem.at[3]),
        pltpu.make_async_copy(kv, kv_all, local_sem.at[4]),
    ]
    for copy in keep:
        copy.start()
    keep[0].wait()
    line_start(normed_all, lambda j: line_sem.at[1, j], 1)
    line_start(normed_all, lambda j: line_sem.at[1, j], 2)
    first(1, 0)

    local = slot.shape[0]
    ranks = slot.shape[1]
    depth = rows.shape[1] // ranks

    def chosen(i, r):
        row = lax.broadcasted_iota(jnp.int32, (depth, tokens), 0)
        return slot[i, pl.ds(r, 1), :] == row

    def span(r):
        return pl.ds(pl.multiple_of(r * depth, depth), depth)

    def each_rank(body):
        lax.fori_loop(0, ranks, lambda r, carry: (body(r), carry)[1], 0)

    def place(r):
        return (r // 4, lax.rem(r // 2, 2), lax.rem(r, 2))

    def find_slots():
        before = (
            lax.broadcasted_iota(jnp.int32, (tokens, tokens), 0)
            < lax.broadcasted_iota(jnp.int32, (tokens, tokens), 1)
        ).astype(F32).astype(BF)
        for i in range(local):
            mine = jnp.concatenate(
                [tabs[r // 4, r // 2 % 2, r % 2, pl.ds(e * local + i, 1), :] for r in range(ranks)],
                axis=0,
            )
            routed = mine >= 0.0
            rank = dot(routed.astype(F32).astype(BF), before, 1, 0)
            mix[i] = mine
            slot[i] = jnp.where(routed, rank.astype(jnp.int32), -1)

    def pick_into(target, source):
        def body(r):
            block = source[place(r)]
            for i in range(local):
                target[i, span(r), :] = dot(
                    chosen(i, r).astype(F32).astype(BF), block, 1, 0
                ).astype(BF)

        each_rank(body)

    def blend(i, dots):
        def body(r):
            at = span(r)
            hit = chosen(i, r)
            share = jnp.sum(jnp.where(hit, mix[i, pl.ds(r, 1), :], 0.0), axis=1, keepdims=True)
            g, u, w = gate_pre[at, :], up_pre[at, :], raw[i, at, :]
            sigmoid = jax.nn.sigmoid(g)
            silu = g * sigmoid
            act = silu * u
            act_grad = w * share
            gate_grad[i, at, :] = (act_grad * u * sigmoid * (1.0 + g * (1.0 - sigmoid))).astype(BF)
            up_grad[i, at, :] = (act_grad * silu).astype(BF)
            mixed[i, at, :] = (act * share).astype(BF)
            if dots:
                total = jnp.sum(act.astype(BF).astype(F32) * w, axis=1, keepdims=True)
                token_dot[r, i : i + 1, :] = jnp.sum(
                    jnp.where(hit, total, 0.0), axis=0, keepdims=True
                )

        each_rank(body)

    def spread(source, target):
        def body(r):
            total = None
            for i in range(local):
                part = dot(chosen(i, r).astype(F32).astype(BF), source[i, span(r), :], 0, 0)
                total = part if total is None else total + part
            target[place(r)] = total.astype(BF)

        each_rank(body)

    share = rows_cols.shape[3]

    def kept(j):
        cols = pl.ds(pl.multiple_of(z * share, share), share)
        return [
            pltpu.make_async_copy(pulls.at[:, :, cols], pulls_cols.at[:, j], out_sem.at[j, 0]),
            pltpu.make_async_copy(rows.at[:, :, cols], rows_cols.at[:, j], out_sem.at[j, 1]),
            pltpu.make_async_copy(gate_grad, gate_all.at[:, j], out_sem.at[j, 2]),
            pltpu.make_async_copy(up_grad, up_all.at[:, j], out_sem.at[j, 3]),
            pltpu.make_async_copy(mixed, mixed_all.at[:, j], out_sem.at[j, 4]),
        ]

    part_outs = [
        pltpu.make_async_copy(held, input_part, part_sem.at[0]),
        pltpu.make_async_copy(spare, out_part, part_sem.at[1]),
    ]

    def hold(ref, target, sem):
        copy = pltpu.make_async_copy(ref, target, sem)
        copy.start()
        return copy

    def task_grads():
        fourth(0, 0)
        hold(tables.at[z], tabs, local_sem.at[1]).wait()
        copy = hold(grads_all.at[z], held, local_sem.at[0])
        find_slots()
        copy.wait()
        pick_into(pulls, held)
        kept(0)[0].start()

    def task_raw(i, ready):
        if ready:
            weights[0].wait()
        raw[i] = dot(pulls[i], down_w[i], 1, 1)

    def task_rows():
        fourth(1, 0)
        hold(normed_all.at[z], held, local_sem.at[0]).wait()
        pick_into(rows, held)
        kept(0)[1].start()
        weights[1].wait()
        weights[2].wait()

    def task_gate(i):
        gate_pre[...] = dot(rows[i], gate_w[i], 1, 1)

    def task_up(i):
        up_pre[...] = dot(rows[i], up_w[i], 1, 1)

    def task_input(i):
        if i == 0:
            kept(0)[0].wait()
            kept(0)[1].wait()
        rows[i] = (dot(gate_grad[i], gate_w[i], 1, 0) + dot(up_grad[i], up_w[i], 1, 0)).astype(BF)

    def task_out(i):
        pulls[i] = dot(mixed[i], down_w[i], 1, 0).astype(BF)

    def task_spread_input():
        for copy in kept(0)[2:]:
            copy.start()
        spread(rows, held)
        part_outs[0].start()

    def task_spread_out():
        spread(pulls, spare)
        part_outs[1].start()

    parts = ((held, input_part, input_sum), (spare, out_part, out_sum))
    pieces = 4

    def in_pieces(body):
        step = half // pieces

        def run(j, carry):
            body(pl.ds(pl.multiple_of(j * step, step), step), step)
            return carry

        lax.fori_loop(0, pieces, run, 0)

    def sum_pair_send(a):
        part_outs[a].wait()
        view = parts[a][1]
        pltpu.make_async_remote_copy(
            src_ref=view.at[:, :, 1 - c],
            dst_ref=pair_sum.at[a],
            send_sem=sum_sem.at[a, 0, 0],
            recv_sem=sum_sem.at[a, 0, 1],
            device_id=sibling,
            device_id_type=MESH,
        ).start()

    def sum_pair_take(a):
        arrived(pair_sum.at[a], sum_sem.at[a, 0])
        for yy in range(2):
            for xx in range(2):

                def body(at, step):
                    mine = parts[a][0][yy, xx, c, at, :].astype(F32)
                    pair_sum[a, yy, xx, at, :] = (
                        mine + pair_sum[a, yy, xx, at, :].astype(F32)
                    ).astype(BF)

                def both_halves(at, step):
                    body(at, step)
                    low = pl.ds(pl.multiple_of(half + at.start, step), step)
                    body(low, step)

                in_pieces(both_halves)

    def half_copies(a):
        return (
            pltpu.make_async_remote_copy(
                src_ref=pair_sum.at[a, :, 1 - x, :half],
                dst_ref=line_sum.at[a, 0],
                send_sem=sum_sem.at[a, 1, 0],
                recv_sem=sum_sem.at[a, 1, 1],
                device_id=across_x,
                device_id_type=MESH,
            ),
            pltpu.make_async_remote_copy(
                src_ref=pair_sum.at[a, 1 - y, :, half:],
                dst_ref=line_sum.at[a, 1],
                send_sem=sum_sem.at[a, 2, 0],
                recv_sem=sum_sem.at[a, 2, 1],
                device_id=across_y,
                device_id_type=MESH,
            ),
        )

    def last_copies(a):
        return tuple(
            pltpu.make_async_remote_copy(
                src_ref=line_sum.at[a, i, 1 - (y, x)[i]],
                dst_ref=last_sum.at[a, i],
                send_sem=sum_sem.at[a, 3 + i, 0],
                recv_sem=sum_sem.at[a, 3 + i, 1],
                device_id=(across_y, across_x)[i],
                device_id_type=MESH,
            )
            for i in range(2)
        )

    def sum_line_send(a):
        for copy in half_copies(a):
            copy.start()

    def sum_line_take(a):
        for copy in half_copies(a):
            copy.wait_recv()
        for j in range(2):

            def body(at, step):
                low = pl.ds(pl.multiple_of(half + at.start, step), step)
                line_sum[a, 0, j, at, :] = (
                    line_sum[a, 0, j, at, :].astype(F32) + pair_sum[a, j, x, at, :].astype(F32)
                ).astype(BF)
                line_sum[a, 1, j, at, :] = (
                    line_sum[a, 1, j, at, :].astype(F32) + pair_sum[a, y, j, low, :].astype(F32)
                ).astype(BF)

            in_pieces(body)

    def sum_last_send(a):
        for copy in last_copies(a):
            copy.start()

    def sum_last_take(a):
        for copy in last_copies(a):
            copy.wait_recv()

        def body(at, step):
            low = pl.ds(pl.multiple_of(half + at.start, step), step)
            total = parts[a][2]
            total[at, :] = (
                line_sum[a, 0, y, at, :].astype(F32) + last_sum[a, 0, at, :].astype(F32)
            ).astype(BF)
            total[low, :] = (
                line_sum[a, 1, x, at, :].astype(F32) + last_sum[a, 1, at, :].astype(F32)
            ).astype(BF)

        in_pieces(body)

    def sum_end(a):
        view = parts[a][1].at[:, :, 1 - c]
        copy_of(view, sum_sem.at[a, 0], sibling).wait_send()
        for copy in half_copies(a) + last_copies(a):
            copy.wait_send()

    far = []
    for j in range(1, seqs):
        at, seen = 0, 0
        for k in range(1, 2 * seqs - 1):
            here = present(k).astype(jnp.int32)
            at = at + k * here * jnp.equal(seen, j - 1).astype(jnp.int32)
            seen = seen + here
        far.append(at)

    def far_plane(j):
        k = far[j - 1]
        return k, z + (k + 1) // 2 * (1 - 2 * lax.rem(k, 2))

    def task_far(j):
        k, p = far_plane(j)
        arrived(arrays[0].at[p, :, :, 1 - c], plane_sem.at[0, k, 4])
        arrived(tables.at[p, :, :, 1 - c], table_plane_sem.at[k, 2])
        loads = [
            hold(tables.at[p], tabs, local_sem.at[1]),
            hold(grads_all.at[p], held, local_sem.at[0]),
        ]
        arrived(arrays[1].at[p, :, :, 1 - c], plane_sem.at[1, k, 4])
        loads.append(hold(normed_all.at[p], spare, local_sem.at[3]))
        loads[0].wait()
        find_slots()
        for copy in kept(j - 1)[2:] if j == 1 else kept(j - 1):
            copy.wait()
        loads[1].wait()
        pick_into(pulls, held)
        kept(j)[0].start()
        loads[2].wait()
        pick_into(rows, spare)
        kept(j)[1].start()

    def task_far_units(j, i):
        task_raw(i, False)
        task_gate(i)
        task_up(i)
        blend(i, False)
        if i == local - 1:
            for copy in kept(j)[2:]:
                copy.start()

    task_grads()
    task_raw(0, True)
    second(1, 0)
    order = []
    for d in range(1, seqs):
        for a in range(2):
            order += [(a, 2 * d - 1), (a, 2 * d)]
    tasks = [(0, functools.partial(task_raw, i, False)) for i in range(1, local)]
    tasks += [(0, lambda: third(1, 0)), (0, task_rows)]
    for i in range(local):
        tasks += [
            (0, functools.partial(task_gate, i)),
            (0, functools.partial(task_up, i)),
            (0, functools.partial(blend, i, True)),
            (0, functools.partial(task_input, i)),
            (0, functools.partial(task_out, i)),
        ]
    tasks += [(0, task_spread_input), (0, task_spread_out)]
    sums = []
    for group_of in (
        (sum_pair_send,),
        (sum_pair_take, sum_line_send),
        (sum_line_take, sum_last_send),
        (sum_last_take,),
    ):
        for a in range(2):
            sums.append([(0, functools.partial(step, a)) for step in group_of])
    tasks += sums[0] + sums[1] + sums[2] + sums[3]
    sums = sums[4:]
    for j in range(1, seqs):
        least = 4 * (2 * j) // 2 + 3
        tasks.append((least, functools.partial(task_far, j)))
        for i in range(local):
            tasks.append((least, functools.partial(task_far_units, j, i)))
            if sums:
                tasks += sums.pop(0)
    for rest in sums:
        tasks += rest
    i = 0
    while i < len(order) + 4 or tasks:
        if i < len(order):
            first(*order[i])
        if 0 <= i - 2 < len(order):
            second(*order[i - 2])
        if 0 <= i - 4 < len(order):
            third(*order[i - 4])
        for _ in range(TASKS):
            if tasks and tasks[0][0] <= i:
                tasks.pop(0)[1]()
        i += 1
    for copy in kept(seqs - 1):
        copy.wait()
    for a in range(2):
        sum_end(a)
    keep[1].wait()
    for guard, finish in sends:
        under(present(guard) if isinstance(guard, int) else guard, finish)


def front(residual, q, kv_mine, table, grads, weights, group, seqs, ranks, depth):
    tokens, width = q.shape
    heads = width // DH
    slots = 2 * seqs - 1
    local, hidden, _ = weights[0].shape
    any_space = pl.BlockSpec(memory_space=pl.ANY)
    dma = pltpu.SemaphoreType.DMA
    picked = (local, ranks * depth, width)
    units = (local, ranks * depth, hidden)
    plane = (2, 2, 2, tokens, width)
    return pl.pallas_call(
        functools.partial(front_kernel, group, seqs),
        out_shape=(
            jax.ShapeDtypeStruct((tokens, width), BF),
            jax.ShapeDtypeStruct((tokens, heads), F32),
            jax.ShapeDtypeStruct((tokens, 1), F32),
            jax.ShapeDtypeStruct((ranks, local, tokens), F32),
            jax.ShapeDtypeStruct((tokens, width), BF),
            jax.ShapeDtypeStruct((tokens, width), BF),
            jax.ShapeDtypeStruct((seqs,) + kv_mine.shape, BF),
            jax.ShapeDtypeStruct((seqs,) + plane, BF),
            jax.ShapeDtypeStruct((seqs,) + plane, BF),
            jax.ShapeDtypeStruct((seqs, 2, 2, 2) + table.shape, F32),
            jax.ShapeDtypeStruct((local, seqs, ranks * depth, width // seqs), BF),
            jax.ShapeDtypeStruct((local, seqs, ranks * depth, width // seqs), BF),
            jax.ShapeDtypeStruct((local, seqs) + units[1:], BF),
            jax.ShapeDtypeStruct((local, seqs) + units[1:], BF),
            jax.ShapeDtypeStruct((local, seqs) + units[1:], BF),
            jax.ShapeDtypeStruct(plane, BF),
            jax.ShapeDtypeStruct(plane, BF),
        ),
        in_specs=[vm()] * 5 + [any_space] * 3,
        out_specs=(vm(),) * 6 + (any_space,) * 11,
        scratch_shapes=[
            pltpu.VMEM((seqs,) + kv_mine.shape, BF),
            pltpu.VMEM((tokens, width), BF),
            pltpu.VMEM(weights[0].shape, BF),
            pltpu.VMEM(weights[1].shape, BF),
            pltpu.VMEM(weights[2].shape, BF),
            pltpu.VMEM((2, 2, 2) + table.shape, F32),
            pltpu.VMEM((local, ranks, tokens), F32),
            pltpu.VMEM((local, ranks, tokens), jnp.int32),
            pltpu.VMEM(plane, BF),
            pltpu.VMEM(plane, BF),
            pltpu.VMEM((2, 2, 2, tokens, width), BF),
            pltpu.VMEM((2, 2, 2, tokens // 2, width), BF),
            pltpu.VMEM((2, 2, tokens // 2, width), BF),
            pltpu.VMEM(picked, BF),
            pltpu.VMEM(picked, BF),
            pltpu.VMEM(units, F32),
            pltpu.VMEM(units[1:], F32),
            pltpu.VMEM(units[1:], F32),
            pltpu.VMEM(units, BF),
            pltpu.VMEM(units, BF),
            pltpu.VMEM(units, BF),
            dma((5,)),
            dma((3,)),
            dma((seqs, 5)),
            dma((2,)),
            dma((2, 5, 2)),
            dma((seqs, 2)),
            dma((2, slots, 2)),
            dma((2, slots, 5, 2)),
            dma((slots, 2)),
            dma((slots, 3, 2)),
        ],
        compiler_params=pltpu.CompilerParams(
            collective_id=0, has_side_effects=True, vmem_limit_bytes=FRONT_LIMIT
        ),
        cost_estimate=pl.CostEstimate(
            flops=4 * tokens * seqs * tokens * width + (6 * seqs + 6) * local * ranks * depth * width * hidden,
            bytes_accessed=32 * seqs * tokens * width,
            transcendentals=heads * tokens * seqs * tokens,
        ),
        name="front",
    )(residual, q, kv_mine, table, grads, *weights)


def attend_back_kernel(
    group, residual, q, kv, att, log_total, inv_rms, grad_out, normed_grad, res_grad, q_grad, kv_part
):
    tokens = q.shape[0]
    full = kv.shape[0]
    kv_heads = kv.shape[1] // (2 * DH)
    scale = 1.0 / math.sqrt(DH)
    inv = inv_rms[...]
    normed = (residual[...].astype(F32) + att[...].astype(F32)) * inv
    ngrad = normed_grad[...].astype(F32)
    dot_mean = jnp.mean(ngrad * normed, axis=1, keepdims=True)
    res_grad[...] = (grad_out[...].astype(F32) + inv * (ngrad - normed * dot_mean)).astype(BF)
    visible = visible_mask(tokens, group, full, lax.axis_index("seq"))
    for k in range(kv_heads):
        qh = heads_of(q, k * group, group)
        oh = heads_of(att, k * group, group)
        gh = heads_of(res_grad, k * group, group)
        logs = jnp.concatenate(
            [log_total[:, k * group + g : k * group + g + 1] for g in range(group)], axis=0
        )
        kh = kv[:, k * DH : (k + 1) * DH]
        vh = kv[:, (kv_heads + k) * DH : (kv_heads + k + 1) * DH]
        scores = jnp.where(visible, dot(qh, kh, 1, 1) * scale, neg_big)
        probs = jnp.exp(scores - logs)
        delta = jnp.sum(gh.astype(F32) * oh.astype(F32), axis=1, keepdims=True)
        pgrad = dot(gh, vh, 1, 1)
        sgrad = (probs * (pgrad - delta)).astype(BF)
        dq = (dot(sgrad, kh, 1, 0) * scale).astype(BF)
        for g in range(group):
            h = k * group + g
            q_grad[:, h * DH : (h + 1) * DH] = dq[g * tokens : (g + 1) * tokens]
        kv_part[:, k * DH : (k + 1) * DH] = (dot(sgrad, qh, 0, 0) * scale).astype(BF)
        kv_part[:, (kv_heads + k) * DH : (kv_heads + k + 1) * DH] = dot(
            probs.astype(BF), gh, 0, 0
        ).astype(BF)


def attend_back(group, residual, q, kv, att, log_total, inv_rms, grad_out, normed_grad):
    tokens, width = q.shape
    return pl.pallas_call(
        functools.partial(attend_back_kernel, group),
        out_shape=(
            jax.ShapeDtypeStruct((tokens, width), BF),
            jax.ShapeDtypeStruct((tokens, width), BF),
            jax.ShapeDtypeStruct(kv.shape, BF),
        ),
        in_specs=[vm()] * 8,
        out_specs=(vm(),) * 3,
        compiler_params=pltpu.CompilerParams(vmem_limit_bytes=VMEM_LIMIT),
        cost_estimate=pl.CostEstimate(
            flops=10 * tokens * kv.shape[0] * width,
            bytes_accessed=14 * tokens * width + 4 * kv.size,
            transcendentals=tokens * kv.shape[0] * (width // DH),
        ),
        name="attend_back",
    )(residual, q, kv, att, log_total, inv_rms, grad_out, normed_grad)


def pick_kernel(seq_index, slot, rows, picked):
    local = slot.shape[2]
    depth = picked.shape[1]
    tokens = rows.shape[2]
    row = lax.broadcasted_iota(jnp.int32, (depth, tokens), 0)
    for e in range(local):
        chosen = (slot[0, 0, e : e + 1, :] == row).astype(F32).astype(BF)
        picked[e] = dot(chosen, rows[0, 0], 1, 0).astype(BF)


def pick_rows(gathered, slot, seq_index, first, planes, depth):
    seqs, ranks, tokens, width = gathered.shape
    local = slot.shape[2]
    count = planes * ranks

    def source(i, s):
        return (lax.rem(s[0] + first + i // ranks, seqs), lax.rem(i, ranks), 0, 0)

    return pl.pallas_call(
        pick_kernel,
        out_shape=jax.ShapeDtypeStruct((local, count * depth, width), BF),
        grid_spec=pltpu.PrefetchScalarGridSpec(
            num_scalar_prefetch=1,
            grid=(count,),
            in_specs=[
                pl.BlockSpec((1, 1, local, tokens), source),
                pl.BlockSpec((1, 1, tokens, width), source),
            ],
            out_specs=pl.BlockSpec((local, depth, width), lambda i, s: (0, i, 0)),
        ),
        compiler_params=pltpu.CompilerParams(vmem_limit_bytes=16 * 1024 * 1024),
        cost_estimate=pl.CostEstimate(
            flops=2 * local * count * depth * tokens * width,
            bytes_accessed=2 * count * (tokens + local * depth) * width,
            transcendentals=0,
        ),
        name="pick_rows",
    )(seq_index, slot, gathered)


def spread_kernel(slot, rows, out):
    ranks, local, tokens = slot.shape
    depth = rows.shape[1]
    row = lax.broadcasted_iota(jnp.int32, (depth, tokens), 0)
    total = None
    for e in range(local):
        chosen = (slot[0, e : e + 1, :] == row).astype(F32).astype(BF)
        part = dot(chosen, rows[e], 0, 0)
        total = part if total is None else total + part
    out[0] = total.astype(BF)


def spread_rows(rows, slot):
    ranks, local, tokens = slot.shape
    width = rows.shape[2]
    depth = rows.shape[1] // ranks
    return pl.pallas_call(
        spread_kernel,
        out_shape=jax.ShapeDtypeStruct((ranks, tokens, width), BF),
        grid=(ranks,),
        in_specs=[
            pl.BlockSpec((1, local, tokens), lambda i: (i, 0, 0)),
            pl.BlockSpec((local, depth, width), lambda i: (0, i, 0)),
        ],
        out_specs=pl.BlockSpec((1, tokens, width), lambda i: (i, 0, 0)),
        compiler_params=pltpu.CompilerParams(vmem_limit_bytes=16 * 1024 * 1024),
        cost_estimate=pl.CostEstimate(
            flops=2 * local * ranks * depth * tokens * width,
            bytes_accessed=2 * ranks * (tokens + local * depth) * width,
            transcendentals=0,
        ),
        name="spread_rows",
    )(slot, rows)


def hidden_units(rows, grads, mix, gate_weight, up_weight, down_weight):
    gate_pre = jnp.einsum("erd,edf->erf", rows, gate_weight, preferred_element_type=F32)
    up_pre = jnp.einsum("erd,edf->erf", rows, up_weight, preferred_element_type=F32)
    raw = jnp.einsum("erd,efd->erf", grads, down_weight, preferred_element_type=F32)
    sigmoid = jax.nn.sigmoid(gate_pre)
    silu = gate_pre * sigmoid
    act = silu * up_pre
    act_grad = raw * mix[:, :, None]
    gate_grad = (act_grad * up_pre * sigmoid * (1.0 + gate_pre * (1.0 - sigmoid))).astype(BF)
    up_grad = (act_grad * silu).astype(BF)
    mixed = (act * mix[:, :, None]).astype(BF)
    return (gate_grad, up_grad, mixed, act, raw)


def on_device(
    residual,
    queries,
    key_input,
    value_input,
    routes,
    mix_weights,
    gate_weight,
    up_weight,
    down_weight,
    grad_out,
):
    tokens = residual.shape[1]
    width = residual.shape[2]
    kv_width = key_input.shape[2]
    group = queries.shape[2] // kv_width
    local = gate_weight.shape[0]
    ranks = lax.axis_size("expert")
    seqs = lax.axis_size("seq")
    experts = local * ranks
    top_count = routes.shape[2]
    capacity = tokens * top_count * 5 // (4 * experts)
    depth = -(-capacity // 16) * 16
    both = ("seq", "expert")
    both_size = seqs * ranks
    seq_index = lax.axis_index("seq")
    rank_index = lax.axis_index("expert")
    seq_array = seq_index.astype(jnp.int32).reshape(1)

    kv_mine = jnp.concatenate(
        [key_input.reshape(tokens, kv_width), value_input.reshape(tokens, kv_width)], axis=1
    )
    expert_ids = jnp.arange(experts, dtype=jnp.int32)
    picked = routes.reshape(tokens, top_count)
    mix_rows = mix_weights.reshape(tokens, top_count)
    hit = picked[None, :, :] == expert_ids[:, None, None]
    table = jnp.sum(jnp.where(hit, mix_rows[None], 0.0), axis=2) - (
        1.0 - jnp.sum(hit.astype(F32), axis=2)
    )
    grad_rows = grad_out.reshape(tokens, width)
    q = queries.reshape(tokens, width)
    res = residual.reshape(tokens, width)
    weights = (gate_weight, up_weight, down_weight)
    paired = ranks == 8 and 2 * both_size * grad_rows.size <= GATHER_BYTES
    if paired:
        (
            att,
            log_total,
            inv_rms,
            token_dot,
            normed_grad,
            routed_out,
            kv,
            _,
            _,
            _,
            rows_cols,
            grads_cols,
            gate_rows,
            up_rows,
            mixed_rows,
            _,
            _,
        ) = front(
            res,
            q,
            kv_mine,
            table,
            grad_rows,
            (jnp.swapaxes(gate_weight, 1, 2), jnp.swapaxes(up_weight, 1, 2), down_weight),
            group,
            seqs,
            ranks,
            depth,
        )
        kv = kv.reshape(seqs * tokens, 2 * kv_width)

        def outer(a, b):
            a = a.reshape(local, seqs * ranks * depth, a.shape[3])
            b = b.reshape(local, seqs * ranks * depth, b.shape[3])
            return jnp.einsum("erm,ern->emn", a, b, preferred_element_type=F32).astype(BF)

        gate_share = outer(rows_cols, gate_rows)
        up_share = outer(rows_cols, up_rows)
        down_share = outer(mixed_rows, grads_cols)
    else:
        kv = lax.all_gather(kv_mine, "seq", axis=0, tiled=True)

        tables = lax.all_gather(table, both, axis=0, tiled=False)
        mine = lax.dynamic_slice_in_dim(tables, rank_index * local, local, axis=1)
        routed = mine >= 0.0
        before = jnp.triu(jnp.ones((tokens, tokens), BF), 1)
        rank = jnp.einsum("bet,tu->beu", routed.astype(BF), before, preferred_element_type=F32)
        slot = jnp.where(routed, rank.astype(jnp.int32), -1)
        slot = slot.reshape(seqs, ranks, local, tokens)
        mine = mine.reshape(seqs, ranks, local, tokens)

        grads_all = lax.all_gather(grad_rows, both, axis=0, tiled=True)
        grads_all = grads_all.reshape(seqs, ranks, tokens, width)

        att, log_total, inv_rms, normed_bf = attend(res, q, kv, group)
        grads_own = pick_rows(grads_all, slot, seq_array, 0, 1, depth)
        grads_far = pick_rows(grads_all, slot, seq_array, 1, seqs - 1, depth)
        if 2 * grads_all.size > GATHER_BYTES:
            normed_bf, grads_own, grads_far = lax.optimization_barrier(
                (normed_bf, grads_own, grads_far)
            )
        normed_all = lax.all_gather(normed_bf, both, axis=0, tiled=True)
        normed_all = normed_all.reshape(seqs, ranks, tokens, width)

        slot_turned = jnp.roll(slot, -seq_index, axis=0)
        mix_turned = jnp.roll(mine, -seq_index, axis=0)
        here = slot_turned[..., None, :] == jnp.arange(depth, dtype=jnp.int32)[:, None]
        mix_slot = jnp.sum(jnp.where(here, mix_turned[..., None, :], 0.0), axis=4)
        mix_slot = jnp.transpose(mix_slot, (2, 0, 1, 3)).reshape(local, seqs * ranks * depth)
        own = ranks * depth

        rows_own = pick_rows(normed_all, slot, seq_array, 0, 1, depth)
        rows_far = pick_rows(normed_all, slot, seq_array, 1, seqs - 1, depth)
        gate_own, up_own, mixed_own, act_own, raw_own = hidden_units(
            rows_own, grads_own, mix_slot[:, :own], *weights
        )
        input_grad = (
            jnp.einsum("erf,edf->erd", gate_own, gate_weight, preferred_element_type=F32)
            + jnp.einsum("erf,edf->erd", up_own, up_weight, preferred_element_type=F32)
        ).astype(BF)
        slot_own = slot_turned[0]
        input_part = spread_rows(input_grad, slot_own).reshape(ranks * tokens, width)
        normed_grad = lax.psum_scatter(input_part, "expert", scatter_dimension=0, tiled=True)

        expert_out = jnp.einsum(
            "erf,efd->erd", mixed_own, down_weight, preferred_element_type=F32
        ).astype(BF)
        out_part = spread_rows(expert_out, slot_own).reshape(ranks * tokens, width)
        routed_out = lax.psum_scatter(out_part, "expert", scatter_dimension=0, tiled=True)
        pair_dot = jnp.sum(act_own.astype(BF).astype(F32) * raw_own, axis=2)
        pair_dot = pair_dot.reshape(local, ranks, depth)
        token_dot = jnp.sum(
            jnp.where(here[0], jnp.transpose(pair_dot, (1, 0, 2))[..., None], 0.0), axis=2
        )
        gate_far, up_far, mixed_far, _, _ = hidden_units(
            rows_far, grads_far, mix_slot[:, own:], *weights
        )
        share = width // seqs

        def columns(array):
            return lax.dynamic_slice_in_dim(array, seq_index * share, share, axis=2)

        def outer(a_own, a_far, b_own, b_far):
            return (
                jnp.einsum("erm,ern->emn", a_own, b_own, preferred_element_type=F32)
                + jnp.einsum("erm,ern->emn", a_far, b_far, preferred_element_type=F32)
            ).astype(BF)

        cols_own, cols_far = columns(rows_own), columns(rows_far)
        gate_share = outer(cols_own, cols_far, gate_own, gate_far)
        up_share = outer(cols_own, cols_far, up_own, up_far)
        down_share = outer(mixed_own, mixed_far, columns(grads_own), columns(grads_far))
    hidden = res.astype(F32) + att.astype(F32)
    layer_out = (hidden + routed_out.astype(F32)).astype(BF)

    dots = lax.all_to_all(token_dot, "expert", split_axis=0, concat_axis=0, tiled=True)
    dots = dots.reshape(experts, tokens)
    mix_grad = jnp.sum(jnp.where(hit, dots[:, :, None], 0.0), axis=0)

    res_grad, q_grad, kv_part = attend_back(
        group, res, q, kv, att, log_total, inv_rms, grad_rows, normed_grad
    )
    kv_share = lax.psum_scatter(kv_part, "seq", scatter_dimension=0, tiled=True)
    return (
        layer_out.reshape(1, tokens, width),
        res_grad.reshape(1, tokens, width),
        q_grad.reshape(1, tokens, width),
        kv_share[:, :kv_width].reshape(1, tokens, kv_width),
        kv_share[:, kv_width:].reshape(1, tokens, kv_width),
        mix_grad.reshape(1, tokens, top_count),
        gate_share,
        up_share,
        down_share,
    )


def solution(mesh):
    rows = P("expert", "seq", None)
    weight = P("expert", None, None)
    return jax.shard_map(
        on_device,
        mesh=mesh,
        in_specs=(rows,) * 6 + (weight,) * 3 + (rows,),
        out_specs=(rows,) * 8 + (P("expert", None, "seq"),),
        check_vma=False,
    )
```

```python
import functools
import math

import jax
import jax.numpy as jnp
from jax import lax
from jax.experimental import pallas as pl
from jax.experimental.pallas import tpu as pltpu
from jax.sharding import PartitionSpec as P

DH = 128
neg_big = -1e30
norm_eps = 1e-06
BF = jnp.bfloat16
F32 = jnp.float32
GATHER_BYTES = 32 * 1024 * 1024
FRONT_LIMIT = 62 * 1024 * 1024
TASKS = 3
MESH = pl.DeviceIdType.MESH
VMEM_LIMIT = 56 * 1024 * 1024


def dot(a, b, ca, cb):
    return lax.dot_general(a, b, (((ca,), (cb,)), ((), ())), preferred_element_type=F32)


def vm():
    return pl.BlockSpec(memory_space=pltpu.VMEM)


def heads_of(ref, first, count):
    return jnp.concatenate(
        [ref[:, (first + g) * DH : (first + g + 1) * DH] for g in range(count)], axis=0
    )


def visible_mask(tokens, group, full, seq_index):
    shape = (group, tokens, full)
    pos = lax.broadcasted_iota(jnp.int32, shape, 1) + seq_index * tokens
    key = lax.broadcasted_iota(jnp.int32, shape, 2)
    return (key <= pos).reshape(group * tokens, full)


def attend_kernel(group, residual, q, kv, att, log_total, inv_rms, normed):
    tokens = q.shape[0]
    full = kv.shape[0]
    kv_heads = kv.shape[1] // (2 * DH)
    visible = visible_mask(tokens, group, full, lax.axis_index("seq"))
    scale = 1.0 / math.sqrt(DH)
    for k in range(kv_heads):
        qh = heads_of(q, k * group, group)
        kh = kv[:, k * DH : (k + 1) * DH]
        vh = kv[:, (kv_heads + k) * DH : (kv_heads + k + 1) * DH]
        scores = jnp.where(visible, dot(qh, kh, 1, 1) * scale, neg_big)
        top = jnp.max(scores, axis=1, keepdims=True)
        weights = jnp.exp(scores - top)
        total = jnp.sum(weights, axis=1, keepdims=True)
        out = (dot(weights.astype(BF), vh, 1, 0) / total).astype(BF)
        logs = top + jnp.log(total)
        for g in range(group):
            h = k * group + g
            att[:, h * DH : (h + 1) * DH] = out[g * tokens : (g + 1) * tokens]
            log_total[:, h : h + 1] = logs[g * tokens : (g + 1) * tokens]
    hidden = residual[...].astype(F32) + att[...].astype(F32)
    inv = lax.rsqrt(jnp.mean(hidden * hidden, axis=1, keepdims=True) + norm_eps)
    inv_rms[...] = inv
    normed[...] = (hidden * inv).astype(BF)


def attend(residual, q, kv, group):
    tokens, width = q.shape
    heads = width // DH
    return pl.pallas_call(
        functools.partial(attend_kernel, group),
        out_shape=(
            jax.ShapeDtypeStruct((tokens, width), BF),
            jax.ShapeDtypeStruct((tokens, heads), F32),
            jax.ShapeDtypeStruct((tokens, 1), F32),
            jax.ShapeDtypeStruct((tokens, width), BF),
        ),
        in_specs=[vm()] * 3,
        out_specs=(vm(),) * 4,
        compiler_params=pltpu.CompilerParams(vmem_limit_bytes=VMEM_LIMIT),
        cost_estimate=pl.CostEstimate(
            flops=4 * tokens * kv.shape[0] * width,
            bytes_accessed=8 * tokens * width + 2 * kv.size,
            transcendentals=heads * tokens * kv.shape[0],
        ),
        name="attend",
    )(residual, q, kv)


def attend_rows(group, residual, q, kv, att, log_total, inv_rms, normed):
    tokens = q.shape[0]
    full = kv.shape[0]
    kv_heads = kv.shape[1] // (2 * DH)
    visible = visible_mask(tokens, group, full, lax.axis_index("seq"))
    scale = 1.0 / math.sqrt(DH)
    for k in range(kv_heads):
        qh = heads_of(q, k * group, group)
        kh = kv[:, k * DH : (k + 1) * DH]
        vh = kv[:, (kv_heads + k) * DH : (kv_heads + k + 1) * DH]
        scores = jnp.where(visible, dot(qh, kh, 1, 1) * scale, neg_big)
        top = jnp.max(scores, axis=1, keepdims=True)
        weights = jnp.exp(scores - top)
        total = jnp.sum(weights, axis=1, keepdims=True)
        out = (dot(weights.astype(BF), vh, 1, 0) / total).astype(BF)
        logs = top + jnp.log(total)
        for g in range(group):
            h = k * group + g
            att[:, h * DH : (h + 1) * DH] = out[g * tokens : (g + 1) * tokens]
            log_total[:, h : h + 1] = logs[g * tokens : (g + 1) * tokens]
    hidden = residual[...].astype(F32) + att[...].astype(F32)
    inv = lax.rsqrt(jnp.mean(hidden * hidden, axis=1, keepdims=True) + norm_eps)
    inv_rms[...] = inv
    normed[...] = (hidden * inv).astype(BF)


def front_kernel(
    group,
    seqs,
    residual,
    q,
    kv_mine,
    table,
    grads,
    gate_weight,
    up_weight,
    down_weight,
    att,
    log_total,
    inv_rms,
    token_dot,
    input_sum,
    out_sum,
    kv_all,
    grads_all,
    normed_all,
    tables,
    rows_cols,
    pulls_cols,
    gate_all,
    up_all,
    mixed_all,
    input_part,
    out_part,
    kv,
    normed,
    gate_w,
    up_w,
    down_w,
    tabs,
    mix,
    slot,
    held,
    spare,
    pair_sum,
    line_sum,
    last_sum,
    rows,
    pulls,
    raw,
    gate_pre,
    up_pre,
    gate_grad,
    up_grad,
    mixed,
    local_sem,
    weight_sem,
    out_sem,
    part_sem,
    sum_sem,
    kv_sem,
    line_sem,
    plane_sem,
    table_line_sem,
    table_plane_sem,
):
    z = lax.axis_index("seq")
    e = lax.axis_index("expert")
    c, x, y = lax.rem(e, 2), lax.rem(e // 2, 2), e // 4
    tokens = q.shape[0]
    half = tokens // 2
    sibling = {"expert": e + 1 - 2 * c}
    across_x = {"expert": e + 2 - 4 * x}
    across_y = {"expert": e + 4 - 8 * y}
    above, below = {"seq": z + 1}, {"seq": z - 1}
    top = seqs - 1
    arrays = (grads_all, normed_all)
    sends = []

    def copy_of(view, sems, device):
        return pltpu.make_async_remote_copy(
            src_ref=view,
            dst_ref=view,
            send_sem=sems.at[0],
            recv_sem=sems.at[1],
            device_id=device,
            device_id_type=MESH,
        )

    def send(guard, view, sems, device):
        copy_of(view(), sems(), device).start()
        sends.append((guard, lambda: copy_of(view(), sems(), device).wait_send()))

    def arrived(view, sems):
        copy_of(view, sems, sibling).wait_recv()

    def under(guard, body):
        if guard is True:
            body()
        else:
            pl.when(guard)(body)

    def plane(k):
        d = (k + 1) // 2
        return z if k == 0 else (z - d if k % 2 else z + d)

    def present(k):
        d = (k + 1) // 2
        return True if k == 0 else (z >= d if k % 2 else z + d <= top)

    def forwarded(k):
        d = (k + 1) // 2
        return z + 1 <= top if k % 2 else z >= 1

    def both(a, b):
        return b if a is True else (a if b is True else jnp.logical_and(a, b))

    def line_start(ref, sems, k):
        guard = both(present(k - 2) if k > 2 else True, forwarded(k))

        def block():
            return ref.at[plane(k - 2) if k > 2 else z, y, x, c]

        under(guard, lambda: send(guard, block, lambda: sems(k), above if k % 2 else below))

    def first(a, k):
        ref = arrays[a]

        def sems(i):
            return plane_sem.at[a, k, i]

        if k:

            def take():
                arrived(ref.at[plane(k), y, x, c], line_sem.at[a, k])
                if a == 0:
                    arrived(tables.at[plane(k), y, x, c], table_line_sem.at[k])

            under(present(k), take)
            if k + 2 <= 2 * top:
                line_start(ref, lambda j: line_sem.at[a, j], k + 2)
                if a == 0:
                    line_start(tables, lambda j: table_line_sem.at[j], k + 2)

        def start():
            send(k, lambda: ref.at[plane(k), y, x, c, :half], lambda: sems(0), across_x)
            send(k, lambda: ref.at[plane(k), y, x, c, half:], lambda: sems(1), across_y)
            if a == 0:
                send(
                    k,
                    lambda: tables.at[plane(k), y, x, c],
                    lambda: table_plane_sem.at[k, 0],
                    across_x,
                )

        under(present(k), start)

    def second(a, k):
        ref = arrays[a]

        def sems(i):
            return plane_sem.at[a, k, i]

        def step():
            p = plane(k)
            arrived(ref.at[p, y, 1 - x, c, :half], sems(0))
            send(k, lambda: ref.at[plane(k), y, :, c, :half], lambda: sems(2), across_y)
            arrived(ref.at[p, 1 - y, x, c, half:], sems(1))
            send(k, lambda: ref.at[plane(k), :, x, c, half:], lambda: sems(3), across_x)
            if a == 0:
                arrived(tables.at[p, y, 1 - x, c], table_plane_sem.at[k, 0])
                send(
                    k,
                    lambda: tables.at[plane(k), y, :, c],
                    lambda: table_plane_sem.at[k, 1],
                    across_y,
                )

        under(present(k), step)

    def third(a, k):
        ref = arrays[a]

        def sems(i):
            return plane_sem.at[a, k, i]

        def step():
            p = plane(k)
            arrived(ref.at[p, 1 - y, :, c, :half], sems(2))
            arrived(ref.at[p, :, 1 - x, c, half:], sems(3))
            send(k, lambda: ref.at[plane(k), :, :, c], lambda: sems(4), sibling)
            if a == 0:
                arrived(tables.at[p, 1 - y, :, c], table_plane_sem.at[k, 1])
                send(
                    k,
                    lambda: tables.at[plane(k), :, :, c],
                    lambda: table_plane_sem.at[k, 2],
                    sibling,
                )

        under(present(k), step)

    def fourth(a, k):
        def step():
            p = plane(k)
            arrived(arrays[a].at[p, :, :, 1 - c], plane_sem.at[a, k, 4])
            if a == 0:
                arrived(tables.at[p, :, :, 1 - c], table_plane_sem.at[k, 2])

        under(present(k), step)

    copies = [
        pltpu.make_async_copy(grads, grads_all.at[z, y, x, c], local_sem.at[0]),
        pltpu.make_async_copy(table, tables.at[z, y, x, c], local_sem.at[1]),
        pltpu.make_async_copy(kv_mine, kv.at[z], local_sem.at[2]),
    ]
    for copy in copies:
        copy.start()
    weights = [
        pltpu.make_async_copy(down_weight, down_w, weight_sem.at[0]),
        pltpu.make_async_copy(gate_weight, gate_w, weight_sem.at[1]),
        pltpu.make_async_copy(up_weight, up_w, weight_sem.at[2]),
    ]
    for copy in weights:
        copy.start()
    for j in range(1, seqs):

        @pl.when(j > z)
        def _():
            kv[j] = jnp.zeros(kv.shape[1:], BF)

    barrier = pltpu.get_barrier_semaphore()
    for device in (sibling, across_x, across_y):
        pl.semaphore_signal(barrier, inc=1, device_id=device, device_id_type=MESH)

    @pl.when(z < top)
    def _():
        pl.semaphore_signal(barrier, inc=1, device_id=above, device_id_type=MESH)

    @pl.when(z > 0)
    def _():
        pl.semaphore_signal(barrier, inc=1, device_id=below, device_id_type=MESH)

    pl.semaphore_wait(barrier, 3 + (z < top).astype(jnp.int32) + (z > 0).astype(jnp.int32))
    for copy in copies:
        copy.wait()

    def kv_start(d):
        guard = both(z >= d if d else True, z < top)
        under(guard, lambda: send(guard, lambda: kv.at[z - d], lambda: kv_sem.at[d + 1], above))

    def kv_take(d):
        @pl.when(z >= d)
        def _():
            arrived(kv.at[z - d], kv_sem.at[d])

    kv_start(0)
    line_start(grads_all, lambda j: line_sem.at[0, j], 2)
    line_start(tables, lambda j: table_line_sem.at[j], 2)
    line_start(tables, lambda j: table_line_sem.at[j], 1)
    first(0, 0)
    for d in range(1, seqs):
        kv_take(d)
        if d < top:
            kv_start(d)
        if d == 1:
            second(0, 0)
        if d == 2:
            third(0, 0)
    line_start(grads_all, lambda j: line_sem.at[0, j], 1)
    keys = kv[...].reshape(seqs * tokens, kv.shape[2])
    attend_rows(group, residual, q, keys, att, log_total, inv_rms, normed)
    keep = [
        pltpu.make_async_copy(normed, normed_all.at[z, y, x, c], local_sem.at[3]),
        pltpu.make_async_copy(kv, kv_all, local_sem.at[4]),
    ]
    for copy in keep:
        copy.start()
    keep[0].wait()
    line_start(normed_all, lambda j: line_sem.at[1, j], 1)
    line_start(normed_all, lambda j: line_sem.at[1, j], 2)
    first(1, 0)

    local = slot.shape[0]
    ranks = slot.shape[1]
    depth = rows.shape[1] // ranks

    def chosen(i, r):
        row = lax.broadcasted_iota(jnp.int32, (depth, tokens), 0)
        return slot[i, pl.ds(r, 1), :] == row

    def all_chosen(r):
        return jnp.concatenate(
            [chosen(i, r).astype(F32) for i in range(local)], axis=0
        ).astype(BF)

    def span(r):
        return pl.ds(pl.multiple_of(r * depth, depth), depth)

    def each_rank(body):
        lax.fori_loop(0, ranks, lambda r, carry: (body(r), carry)[1], 0)

    def place(r):
        return (r // 4, lax.rem(r // 2, 2), lax.rem(r, 2))

    def find_slots():
        before = (
            lax.broadcasted_iota(jnp.int32, (tokens, tokens), 0)
            < lax.broadcasted_iota(jnp.int32, (tokens, tokens), 1)
        ).astype(F32).astype(BF)
        for i in range(local):
            mine = jnp.concatenate(
                [tabs[r // 4, r // 2 % 2, r % 2, pl.ds(e * local + i, 1), :] for r in range(ranks)],
                axis=0,
            )
            routed = mine >= 0.0
            rank = dot(routed.astype(F32).astype(BF), before, 1, 0)
            mix[i] = mine
            slot[i] = jnp.where(routed, rank.astype(jnp.int32), -1)

    def pick_into(target, source):
        def body(r):
            found = dot(all_chosen(r), source[place(r)], 1, 0).astype(BF)
            for i in range(local):
                target[i, span(r), :] = found[i * depth : (i + 1) * depth]

        each_rank(body)

    def blend(i, dots):
        def body(r):
            at = span(r)
            hit = chosen(i, r)
            share = jnp.sum(jnp.where(hit, mix[i, pl.ds(r, 1), :], 0.0), axis=1, keepdims=True)
            g, u, w = gate_pre[at, :], up_pre[at, :], raw[i, at, :]
            sigmoid = jax.nn.sigmoid(g)
            silu = g * sigmoid
            act = silu * u
            act_grad = w * share
            gate_grad[i, at, :] = (act_grad * u * sigmoid * (1.0 + g * (1.0 - sigmoid))).astype(BF)
            up_grad[i, at, :] = (act_grad * silu).astype(BF)
            mixed[i, at, :] = (act * share).astype(BF)
            if dots:
                total = jnp.sum(act.astype(BF).astype(F32) * w, axis=1, keepdims=True)
                token_dot[r, i : i + 1, :] = jnp.sum(
                    jnp.where(hit, total, 0.0), axis=0, keepdims=True
                )

        each_rank(body)

    def spread(source, target):
        def body(r):
            stacked = jnp.concatenate([source[i, span(r), :] for i in range(local)], axis=0)
            target[place(r)] = dot(all_chosen(r), stacked, 0, 0).astype(BF)

        each_rank(body)

    share = rows_cols.shape[3]

    def kept(j):
        cols = pl.ds(pl.multiple_of(z * share, share), share)
        return [
            pltpu.make_async_copy(pulls.at[:, :, cols], pulls_cols.at[:, j], out_sem.at[j, 0]),
            pltpu.make_async_copy(rows.at[:, :, cols], rows_cols.at[:, j], out_sem.at[j, 1]),
            pltpu.make_async_copy(gate_grad, gate_all.at[:, j], out_sem.at[j, 2]),
            pltpu.make_async_copy(up_grad, up_all.at[:, j], out_sem.at[j, 3]),
            pltpu.make_async_copy(mixed, mixed_all.at[:, j], out_sem.at[j, 4]),
        ]

    part_outs = [
        pltpu.make_async_copy(held, input_part, part_sem.at[0]),
        pltpu.make_async_copy(spare, out_part, part_sem.at[1]),
    ]

    def hold(ref, target, sem):
        copy = pltpu.make_async_copy(ref, target, sem)
        copy.start()
        return copy

    def task_grads():
        fourth(0, 0)
        hold(tables.at[z], tabs, local_sem.at[1]).wait()
        copy = hold(grads_all.at[z], held, local_sem.at[0])
        find_slots()
        copy.wait()
        pick_into(pulls, held)
        kept(0)[0].start()

    def task_raw(i, ready):
        if ready:
            weights[0].wait()
        raw[i] = dot(pulls[i], down_w[i], 1, 1)

    def task_rows():
        fourth(1, 0)
        hold(normed_all.at[z], held, local_sem.at[0]).wait()
        pick_into(rows, held)
        kept(0)[1].start()
        weights[1].wait()
        weights[2].wait()

    def task_gate(i):
        gate_pre[...] = dot(rows[i], gate_w[i], 1, 1)

    def task_up(i):
        up_pre[...] = dot(rows[i], up_w[i], 1, 1)

    def task_input(i):
        if i == 0:
            kept(0)[0].wait()
            kept(0)[1].wait()
        rows[i] = (dot(gate_grad[i], gate_w[i], 1, 0) + dot(up_grad[i], up_w[i], 1, 0)).astype(BF)

    def task_out(i):
        pulls[i] = dot(mixed[i], down_w[i], 1, 0).astype(BF)

    def task_spread_input():
        for copy in kept(0)[2:]:
            copy.start()
        spread(rows, held)
        part_outs[0].start()

    def task_spread_out():
        spread(pulls, spare)
        part_outs[1].start()

    parts = ((held, input_part, input_sum), (spare, out_part, out_sum))
    pieces = 4

    def in_pieces(body):
        step = half // pieces

        def run(j, carry):
            body(pl.ds(pl.multiple_of(j * step, step), step), step)
            return carry

        lax.fori_loop(0, pieces, run, 0)

    def sum_pair_send(a):
        part_outs[a].wait()
        view = parts[a][1]
        pltpu.make_async_remote_copy(
            src_ref=view.at[:, :, 1 - c],
            dst_ref=pair_sum.at[a],
            send_sem=sum_sem.at[a, 0, 0],
            recv_sem=sum_sem.at[a, 0, 1],
            device_id=sibling,
            device_id_type=MESH,
        ).start()

    def sum_pair_take(a):
        arrived(pair_sum.at[a], sum_sem.at[a, 0])
        for yy in range(2):
            for xx in range(2):

                def body(at, step):
                    mine = parts[a][0][yy, xx, c, at, :].astype(F32)
                    pair_sum[a, yy, xx, at, :] = (
                        mine + pair_sum[a, yy, xx, at, :].astype(F32)
                    ).astype(BF)

                def both_halves(at, step):
                    body(at, step)
                    low = pl.ds(pl.multiple_of(half + at.start, step), step)
                    body(low, step)

                in_pieces(both_halves)

    def half_copies(a):
        return (
            pltpu.make_async_remote_copy(
                src_ref=pair_sum.at[a, :, 1 - x, :half],
                dst_ref=line_sum.at[a, 0],
                send_sem=sum_sem.at[a, 1, 0],
                recv_sem=sum_sem.at[a, 1, 1],
                device_id=across_x,
                device_id_type=MESH,
            ),
            pltpu.make_async_remote_copy(
                src_ref=pair_sum.at[a, 1 - y, :, half:],
                dst_ref=line_sum.at[a, 1],
                send_sem=sum_sem.at[a, 2, 0],
                recv_sem=sum_sem.at[a, 2, 1],
                device_id=across_y,
                device_id_type=MESH,
            ),
        )

    def last_copies(a):
        return tuple(
            pltpu.make_async_remote_copy(
                src_ref=line_sum.at[a, i, 1 - (y, x)[i]],
                dst_ref=last_sum.at[a, i],
                send_sem=sum_sem.at[a, 3 + i, 0],
                recv_sem=sum_sem.at[a, 3 + i, 1],
                device_id=(across_y, across_x)[i],
                device_id_type=MESH,
            )
            for i in range(2)
        )

    def sum_line_send(a):
        for copy in half_copies(a):
            copy.start()

    def sum_line_take(a):
        for copy in half_copies(a):
            copy.wait_recv()
        for j in range(2):

            def body(at, step):
                low = pl.ds(pl.multiple_of(half + at.start, step), step)
                line_sum[a, 0, j, at, :] = (
                    line_sum[a, 0, j, at, :].astype(F32) + pair_sum[a, j, x, at, :].astype(F32)
                ).astype(BF)
                line_sum[a, 1, j, at, :] = (
                    line_sum[a, 1, j, at, :].astype(F32) + pair_sum[a, y, j, low, :].astype(F32)
                ).astype(BF)

            in_pieces(body)

    def sum_last_send(a):
        for copy in last_copies(a):
            copy.start()

    def sum_last_take(a):
        for copy in last_copies(a):
            copy.wait_recv()

        def body(at, step):
            low = pl.ds(pl.multiple_of(half + at.start, step), step)
            total = parts[a][2]
            total[at, :] = (
                line_sum[a, 0, y, at, :].astype(F32) + last_sum[a, 0, at, :].astype(F32)
            ).astype(BF)
            total[low, :] = (
                line_sum[a, 1, x, at, :].astype(F32) + last_sum[a, 1, at, :].astype(F32)
            ).astype(BF)

        in_pieces(body)

    def sum_end(a):
        view = parts[a][1].at[:, :, 1 - c]
        copy_of(view, sum_sem.at[a, 0], sibling).wait_send()
        for copy in half_copies(a) + last_copies(a):
            copy.wait_send()

    far = []
    for j in range(1, seqs):
        at, seen = 0, 0
        for k in range(1, 2 * seqs - 1):
            here = present(k).astype(jnp.int32)
            at = at + k * here * jnp.equal(seen, j - 1).astype(jnp.int32)
            seen = seen + here
        far.append(at)

    def far_plane(j):
        k = far[j - 1]
        return k, z + (k + 1) // 2 * (1 - 2 * lax.rem(k, 2))

    def task_far(j):
        k, p = far_plane(j)
        arrived(arrays[0].at[p, :, :, 1 - c], plane_sem.at[0, k, 4])
        arrived(tables.at[p, :, :, 1 - c], table_plane_sem.at[k, 2])
        loads = [
            hold(tables.at[p], tabs, local_sem.at[1]),
            hold(grads_all.at[p], held, local_sem.at[0]),
        ]
        arrived(arrays[1].at[p, :, :, 1 - c], plane_sem.at[1, k, 4])
        loads.append(hold(normed_all.at[p], spare, local_sem.at[3]))
        loads[0].wait()
        find_slots()
        for copy in kept(j - 1)[2:] if j == 1 else kept(j - 1):
            copy.wait()
        loads[1].wait()
        pick_into(pulls, held)
        kept(j)[0].start()
        loads[2].wait()
        pick_into(rows, spare)
        kept(j)[1].start()

    def task_far_units(j, i):
        task_raw(i, False)
        task_gate(i)
        task_up(i)
        blend(i, False)
        if i == local - 1:
            for copy in kept(j)[2:]:
                copy.start()

    task_grads()
    task_raw(0, True)
    second(1, 0)
    order = []
    for d in range(1, seqs):
        for a in range(2):
            order += [(a, 2 * d - 1), (a, 2 * d)]
    tasks = [(0, functools.partial(task_raw, i, False)) for i in range(1, local)]
    tasks += [(0, lambda: third(1, 0)), (0, task_rows)]
    for i in range(local):
        tasks += [
            (0, functools.partial(task_gate, i)),
            (0, functools.partial(task_up, i)),
            (0, functools.partial(blend, i, True)),
            (0, functools.partial(task_input, i)),
            (0, functools.partial(task_out, i)),
        ]
    tasks += [(0, task_spread_input), (0, task_spread_out)]
    sums = []
    for group_of in (
        (sum_pair_send,),
        (sum_pair_take, sum_line_send),
        (sum_line_take, sum_last_send),
        (sum_last_take,),
    ):
        for a in range(2):
            sums.append([(0, functools.partial(step, a)) for step in group_of])
    tasks += sums[0] + sums[1] + sums[2] + sums[3]
    sums = sums[4:]
    for j in range(1, seqs):
        least = 4 * (2 * j) // 2 + 3
        tasks.append((least, functools.partial(task_far, j)))
        for i in range(local):
            tasks.append((least, functools.partial(task_far_units, j, i)))
            if sums:
                tasks += sums.pop(0)
    for rest in sums:
        tasks += rest
    i = 0
    while i < len(order) + 4 or tasks:
        if i < len(order):
            first(*order[i])
        if 0 <= i - 2 < len(order):
            second(*order[i - 2])
        if 0 <= i - 4 < len(order):
            third(*order[i - 4])
        for _ in range(TASKS):
            if tasks and tasks[0][0] <= i:
                tasks.pop(0)[1]()
        i += 1
    for copy in kept(seqs - 1):
        copy.wait()
    for a in range(2):
        sum_end(a)
    keep[1].wait()
    for guard, finish in sends:
        under(present(guard) if isinstance(guard, int) else guard, finish)


def front(residual, q, kv_mine, table, grads, weights, group, seqs, ranks, depth):
    tokens, width = q.shape
    heads = width // DH
    slots = 2 * seqs - 1
    local, hidden, _ = weights[0].shape
    any_space = pl.BlockSpec(memory_space=pl.ANY)
    dma = pltpu.SemaphoreType.DMA
    picked = (local, ranks * depth, width)
    units = (local, ranks * depth, hidden)
    plane = (2, 2, 2, tokens, width)
    return pl.pallas_call(
        functools.partial(front_kernel, group, seqs),
        out_shape=(
            jax.ShapeDtypeStruct((tokens, width), BF),
            jax.ShapeDtypeStruct((tokens, heads), F32),
            jax.ShapeDtypeStruct((tokens, 1), F32),
            jax.ShapeDtypeStruct((ranks, local, tokens), F32),
            jax.ShapeDtypeStruct((tokens, width), BF),
            jax.ShapeDtypeStruct((tokens, width), BF),
            jax.ShapeDtypeStruct((seqs,) + kv_mine.shape, BF),
            jax.ShapeDtypeStruct((seqs,) + plane, BF),
            jax.ShapeDtypeStruct((seqs,) + plane, BF),
            jax.ShapeDtypeStruct((seqs, 2, 2, 2) + table.shape, F32),
            jax.ShapeDtypeStruct((local, seqs, ranks * depth, width // seqs), BF),
            jax.ShapeDtypeStruct((local, seqs, ranks * depth, width // seqs), BF),
            jax.ShapeDtypeStruct((local, seqs) + units[1:], BF),
            jax.ShapeDtypeStruct((local, seqs) + units[1:], BF),
            jax.ShapeDtypeStruct((local, seqs) + units[1:], BF),
            jax.ShapeDtypeStruct(plane, BF),
            jax.ShapeDtypeStruct(plane, BF),
        ),
        in_specs=[vm()] * 5 + [any_space] * 3,
        out_specs=(vm(),) * 6 + (any_space,) * 11,
        scratch_shapes=[
            pltpu.VMEM((seqs,) + kv_mine.shape, BF),
            pltpu.VMEM((tokens, width), BF),
            pltpu.VMEM(weights[0].shape, BF),
            pltpu.VMEM(weights[1].shape, BF),
            pltpu.VMEM(weights[2].shape, BF),
            pltpu.VMEM((2, 2, 2) + table.shape, F32),
            pltpu.VMEM((local, ranks, tokens), F32),
            pltpu.VMEM((local, ranks, tokens), jnp.int32),
            pltpu.VMEM(plane, BF),
            pltpu.VMEM(plane, BF),
            pltpu.VMEM((2, 2, 2, tokens, width), BF),
            pltpu.VMEM((2, 2, 2, tokens // 2, width), BF),
            pltpu.VMEM((2, 2, tokens // 2, width), BF),
            pltpu.VMEM(picked, BF),
            pltpu.VMEM(picked, BF),
            pltpu.VMEM(units, F32),
            pltpu.VMEM(units[1:], F32),
            pltpu.VMEM(units[1:], F32),
            pltpu.VMEM(units, BF),
            pltpu.VMEM(units, BF),
            pltpu.VMEM(units, BF),
            dma((5,)),
            dma((3,)),
            dma((seqs, 5)),
            dma((2,)),
            dma((2, 5, 2)),
            dma((seqs, 2)),
            dma((2, slots, 2)),
            dma((2, slots, 5, 2)),
            dma((slots, 2)),
            dma((slots, 3, 2)),
        ],
        compiler_params=pltpu.CompilerParams(
            collective_id=0, has_side_effects=True, vmem_limit_bytes=FRONT_LIMIT
        ),
        cost_estimate=pl.CostEstimate(
            flops=4 * tokens * seqs * tokens * width + (6 * seqs + 6) * local * ranks * depth * width * hidden,
            bytes_accessed=32 * seqs * tokens * width,
            transcendentals=heads * tokens * seqs * tokens,
        ),
        name="front",
    )(residual, q, kv_mine, table, grads, *weights)


def attend_back_kernel(
    group, residual, q, kv, att, log_total, inv_rms, grad_out, normed_grad, res_grad, q_grad, kv_part
):
    tokens = q.shape[0]
    full = kv.shape[0]
    kv_heads = kv.shape[1] // (2 * DH)
    scale = 1.0 / math.sqrt(DH)
    inv = inv_rms[...]
    normed = (residual[...].astype(F32) + att[...].astype(F32)) * inv
    ngrad = normed_grad[...].astype(F32)
    dot_mean = jnp.mean(ngrad * normed, axis=1, keepdims=True)
    res_grad[...] = (grad_out[...].astype(F32) + inv * (ngrad - normed * dot_mean)).astype(BF)
    visible = visible_mask(tokens, group, full, lax.axis_index("seq"))
    for k in range(kv_heads):
        qh = heads_of(q, k * group, group)
        oh = heads_of(att, k * group, group)
        gh = heads_of(res_grad, k * group, group)
        logs = jnp.concatenate(
            [log_total[:, k * group + g : k * group + g + 1] for g in range(group)], axis=0
        )
        kh = kv[:, k * DH : (k + 1) * DH]
        vh = kv[:, (kv_heads + k) * DH : (kv_heads + k + 1) * DH]
        scores = jnp.where(visible, dot(qh, kh, 1, 1) * scale, neg_big)
        probs = jnp.exp(scores - logs)
        delta = jnp.sum(gh.astype(F32) * oh.astype(F32), axis=1, keepdims=True)
        pgrad = dot(gh, vh, 1, 1)
        sgrad = (probs * (pgrad - delta)).astype(BF)
        dq = (dot(sgrad, kh, 1, 0) * scale).astype(BF)
        for g in range(group):
            h = k * group + g
            q_grad[:, h * DH : (h + 1) * DH] = dq[g * tokens : (g + 1) * tokens]
        kv_part[:, k * DH : (k + 1) * DH] = (dot(sgrad, qh, 0, 0) * scale).astype(BF)
        kv_part[:, (kv_heads + k) * DH : (kv_heads + k + 1) * DH] = dot(
            probs.astype(BF), gh, 0, 0
        ).astype(BF)


def attend_back(group, residual, q, kv, att, log_total, inv_rms, grad_out, normed_grad):
    tokens, width = q.shape
    return pl.pallas_call(
        functools.partial(attend_back_kernel, group),
        out_shape=(
            jax.ShapeDtypeStruct((tokens, width), BF),
            jax.ShapeDtypeStruct((tokens, width), BF),
            jax.ShapeDtypeStruct(kv.shape, BF),
        ),
        in_specs=[vm()] * 8,
        out_specs=(vm(),) * 3,
        compiler_params=pltpu.CompilerParams(vmem_limit_bytes=VMEM_LIMIT),
        cost_estimate=pl.CostEstimate(
            flops=10 * tokens * kv.shape[0] * width,
            bytes_accessed=14 * tokens * width + 4 * kv.size,
            transcendentals=tokens * kv.shape[0] * (width // DH),
        ),
        name="attend_back",
    )(residual, q, kv, att, log_total, inv_rms, grad_out, normed_grad)


def pick_kernel(seq_index, slot, rows, picked):
    local = slot.shape[2]
    depth = picked.shape[1]
    tokens = rows.shape[2]
    row = lax.broadcasted_iota(jnp.int32, (depth, tokens), 0)
    for e in range(local):
        chosen = (slot[0, 0, e : e + 1, :] == row).astype(F32).astype(BF)
        picked[e] = dot(chosen, rows[0, 0], 1, 0).astype(BF)


def pick_rows(gathered, slot, seq_index, first, planes, depth):
    seqs, ranks, tokens, width = gathered.shape
    local = slot.shape[2]
    count = planes * ranks

    def source(i, s):
        return (lax.rem(s[0] + first + i // ranks, seqs), lax.rem(i, ranks), 0, 0)

    return pl.pallas_call(
        pick_kernel,
        out_shape=jax.ShapeDtypeStruct((local, count * depth, width), BF),
        grid_spec=pltpu.PrefetchScalarGridSpec(
            num_scalar_prefetch=1,
            grid=(count,),
            in_specs=[
                pl.BlockSpec((1, 1, local, tokens), source),
                pl.BlockSpec((1, 1, tokens, width), source),
            ],
            out_specs=pl.BlockSpec((local, depth, width), lambda i, s: (0, i, 0)),
        ),
        compiler_params=pltpu.CompilerParams(vmem_limit_bytes=16 * 1024 * 1024),
        cost_estimate=pl.CostEstimate(
            flops=2 * local * count * depth * tokens * width,
            bytes_accessed=2 * count * (tokens + local * depth) * width,
            transcendentals=0,
        ),
        name="pick_rows",
    )(seq_index, slot, gathered)


def spread_kernel(slot, rows, out):
    ranks, local, tokens = slot.shape
    depth = rows.shape[1]
    row = lax.broadcasted_iota(jnp.int32, (depth, tokens), 0)
    total = None
    for e in range(local):
        chosen = (slot[0, e : e + 1, :] == row).astype(F32).astype(BF)
        part = dot(chosen, rows[e], 0, 0)
        total = part if total is None else total + part
    out[0] = total.astype(BF)


def spread_rows(rows, slot):
    ranks, local, tokens = slot.shape
    width = rows.shape[2]
    depth = rows.shape[1] // ranks
    return pl.pallas_call(
        spread_kernel,
        out_shape=jax.ShapeDtypeStruct((ranks, tokens, width), BF),
        grid=(ranks,),
        in_specs=[
            pl.BlockSpec((1, local, tokens), lambda i: (i, 0, 0)),
            pl.BlockSpec((local, depth, width), lambda i: (0, i, 0)),
        ],
        out_specs=pl.BlockSpec((1, tokens, width), lambda i: (i, 0, 0)),
        compiler_params=pltpu.CompilerParams(vmem_limit_bytes=16 * 1024 * 1024),
        cost_estimate=pl.CostEstimate(
            flops=2 * local * ranks * depth * tokens * width,
            bytes_accessed=2 * ranks * (tokens + local * depth) * width,
            transcendentals=0,
        ),
        name="spread_rows",
    )(slot, rows)


def hidden_units(rows, grads, mix, gate_weight, up_weight, down_weight):
    gate_pre = jnp.einsum("erd,edf->erf", rows, gate_weight, preferred_element_type=F32)
    up_pre = jnp.einsum("erd,edf->erf", rows, up_weight, preferred_element_type=F32)
    raw = jnp.einsum("erd,efd->erf", grads, down_weight, preferred_element_type=F32)
    sigmoid = jax.nn.sigmoid(gate_pre)
    silu = gate_pre * sigmoid
    act = silu * up_pre
    act_grad = raw * mix[:, :, None]
    gate_grad = (act_grad * up_pre * sigmoid * (1.0 + gate_pre * (1.0 - sigmoid))).astype(BF)
    up_grad = (act_grad * silu).astype(BF)
    mixed = (act * mix[:, :, None]).astype(BF)
    return (gate_grad, up_grad, mixed, act, raw)


def on_device(
    residual,
    queries,
    key_input,
    value_input,
    routes,
    mix_weights,
    gate_weight,
    up_weight,
    down_weight,
    grad_out,
):
    tokens = residual.shape[1]
    width = residual.shape[2]
    kv_width = key_input.shape[2]
    group = queries.shape[2] // kv_width
    local = gate_weight.shape[0]
    ranks = lax.axis_size("expert")
    seqs = lax.axis_size("seq")
    experts = local * ranks
    top_count = routes.shape[2]
    capacity = tokens * top_count * 5 // (4 * experts)
    depth = -(-capacity // 16) * 16
    both = ("seq", "expert")
    both_size = seqs * ranks
    seq_index = lax.axis_index("seq")
    rank_index = lax.axis_index("expert")
    seq_array = seq_index.astype(jnp.int32).reshape(1)

    kv_mine = jnp.concatenate(
        [key_input.reshape(tokens, kv_width), value_input.reshape(tokens, kv_width)], axis=1
    )
    expert_ids = jnp.arange(experts, dtype=jnp.int32)
    picked = routes.reshape(tokens, top_count)
    mix_rows = mix_weights.reshape(tokens, top_count)
    hit = picked[None, :, :] == expert_ids[:, None, None]
    table = jnp.sum(jnp.where(hit, mix_rows[None], 0.0), axis=2) - (
        1.0 - jnp.sum(hit.astype(F32), axis=2)
    )
    grad_rows = grad_out.reshape(tokens, width)
    q = queries.reshape(tokens, width)
    res = residual.reshape(tokens, width)
    weights = (gate_weight, up_weight, down_weight)
    paired = ranks == 8 and 2 * both_size * grad_rows.size <= GATHER_BYTES
    if paired:
        (
            att,
            log_total,
            inv_rms,
            token_dot,
            normed_grad,
            routed_out,
            kv,
            _,
            _,
            _,
            rows_cols,
            grads_cols,
            gate_rows,
            up_rows,
            mixed_rows,
            _,
            _,
        ) = front(
            res,
            q,
            kv_mine,
            table,
            grad_rows,
            (jnp.swapaxes(gate_weight, 1, 2), jnp.swapaxes(up_weight, 1, 2), down_weight),
            group,
            seqs,
            ranks,
            depth,
        )
        kv = kv.reshape(seqs * tokens, 2 * kv_width)

        def outer(a, b):
            a = a.reshape(local, seqs * ranks * depth, a.shape[3])
            b = b.reshape(local, seqs * ranks * depth, b.shape[3])
            return jnp.einsum("erm,ern->emn", a, b, preferred_element_type=F32).astype(BF)

        gate_share = outer(rows_cols, gate_rows)
        up_share = outer(rows_cols, up_rows)
        down_share = outer(mixed_rows, grads_cols)
    else:
        kv = lax.all_gather(kv_mine, "seq", axis=0, tiled=True)

        tables = lax.all_gather(table, both, axis=0, tiled=False)
        mine = lax.dynamic_slice_in_dim(tables, rank_index * local, local, axis=1)
        routed = mine >= 0.0
        before = jnp.triu(jnp.ones((tokens, tokens), BF), 1)
        rank = jnp.einsum("bet,tu->beu", routed.astype(BF), before, preferred_element_type=F32)
        slot = jnp.where(routed, rank.astype(jnp.int32), -1)
        slot = slot.reshape(seqs, ranks, local, tokens)
        mine = mine.reshape(seqs, ranks, local, tokens)

        grads_all = lax.all_gather(grad_rows, both, axis=0, tiled=True)
        grads_all = grads_all.reshape(seqs, ranks, tokens, width)

        att, log_total, inv_rms, normed_bf = attend(res, q, kv, group)
        grads_own = pick_rows(grads_all, slot, seq_array, 0, 1, depth)
        grads_far = pick_rows(grads_all, slot, seq_array, 1, seqs - 1, depth)
        if 2 * grads_all.size > GATHER_BYTES:
            normed_bf, grads_own, grads_far = lax.optimization_barrier(
                (normed_bf, grads_own, grads_far)
            )
        normed_all = lax.all_gather(normed_bf, both, axis=0, tiled=True)
        normed_all = normed_all.reshape(seqs, ranks, tokens, width)

        slot_turned = jnp.roll(slot, -seq_index, axis=0)
        mix_turned = jnp.roll(mine, -seq_index, axis=0)
        here = slot_turned[..., None, :] == jnp.arange(depth, dtype=jnp.int32)[:, None]
        mix_slot = jnp.sum(jnp.where(here, mix_turned[..., None, :], 0.0), axis=4)
        mix_slot = jnp.transpose(mix_slot, (2, 0, 1, 3)).reshape(local, seqs * ranks * depth)
        own = ranks * depth

        rows_own = pick_rows(normed_all, slot, seq_array, 0, 1, depth)
        rows_far = pick_rows(normed_all, slot, seq_array, 1, seqs - 1, depth)
        gate_own, up_own, mixed_own, act_own, raw_own = hidden_units(
            rows_own, grads_own, mix_slot[:, :own], *weights
        )
        input_grad = (
            jnp.einsum("erf,edf->erd", gate_own, gate_weight, preferred_element_type=F32)
            + jnp.einsum("erf,edf->erd", up_own, up_weight, preferred_element_type=F32)
        ).astype(BF)
        slot_own = slot_turned[0]
        input_part = spread_rows(input_grad, slot_own).reshape(ranks * tokens, width)
        normed_grad = lax.psum_scatter(input_part, "expert", scatter_dimension=0, tiled=True)

        expert_out = jnp.einsum(
            "erf,efd->erd", mixed_own, down_weight, preferred_element_type=F32
        ).astype(BF)
        out_part = spread_rows(expert_out, slot_own).reshape(ranks * tokens, width)
        routed_out = lax.psum_scatter(out_part, "expert", scatter_dimension=0, tiled=True)
        pair_dot = jnp.sum(act_own.astype(BF).astype(F32) * raw_own, axis=2)
        pair_dot = pair_dot.reshape(local, ranks, depth)
        token_dot = jnp.sum(
            jnp.where(here[0], jnp.transpose(pair_dot, (1, 0, 2))[..., None], 0.0), axis=2
        )
        gate_far, up_far, mixed_far, _, _ = hidden_units(
            rows_far, grads_far, mix_slot[:, own:], *weights
        )
        share = width // seqs

        def columns(array):
            return lax.dynamic_slice_in_dim(array, seq_index * share, share, axis=2)

        def outer(a_own, a_far, b_own, b_far):
            return (
                jnp.einsum("erm,ern->emn", a_own, b_own, preferred_element_type=F32)
                + jnp.einsum("erm,ern->emn", a_far, b_far, preferred_element_type=F32)
            ).astype(BF)

        cols_own, cols_far = columns(rows_own), columns(rows_far)
        gate_share = outer(cols_own, cols_far, gate_own, gate_far)
        up_share = outer(cols_own, cols_far, up_own, up_far)
        down_share = outer(mixed_own, mixed_far, columns(grads_own), columns(grads_far))
    hidden = res.astype(F32) + att.astype(F32)
    layer_out = (hidden + routed_out.astype(F32)).astype(BF)

    dots = lax.all_to_all(token_dot, "expert", split_axis=0, concat_axis=0, tiled=True)
    dots = dots.reshape(experts, tokens)
    mix_grad = jnp.sum(jnp.where(hit, dots[:, :, None], 0.0), axis=0)

    res_grad, q_grad, kv_part = attend_back(
        group, res, q, kv, att, log_total, inv_rms, grad_rows, normed_grad
    )
    kv_share = lax.psum_scatter(kv_part, "seq", scatter_dimension=0, tiled=True)
    return (
        layer_out.reshape(1, tokens, width),
        res_grad.reshape(1, tokens, width),
        q_grad.reshape(1, tokens, width),
        kv_share[:, :kv_width].reshape(1, tokens, kv_width),
        kv_share[:, kv_width:].reshape(1, tokens, kv_width),
        mix_grad.reshape(1, tokens, top_count),
        gate_share,
        up_share,
        down_share,
    )


def solution(mesh):
    rows = P("expert", "seq", None)
    weight = P("expert", None, None)
    return jax.shard_map(
        on_device,
        mesh=mesh,
        in_specs=(rows,) * 6 + (weight,) * 3 + (rows,),
        out_specs=(rows,) * 8 + (P("expert", None, "seq"),),
        check_vma=False,
    )
```

```python
import functools
import math

import jax
import jax.numpy as jnp
from jax import lax
from jax.experimental import pallas as pl
from jax.experimental.pallas import tpu as pltpu
from jax.sharding import PartitionSpec as P

DH = 128
neg_big = -1e30
norm_eps = 1e-06
BF = jnp.bfloat16
F32 = jnp.float32
GATHER_BYTES = 32 * 1024 * 1024
FRONT_LIMIT = 62 * 1024 * 1024
TASKS = 2
MESH = pl.DeviceIdType.MESH
VMEM_LIMIT = 56 * 1024 * 1024


def dot(a, b, ca, cb):
    return lax.dot_general(a, b, (((ca,), (cb,)), ((), ())), preferred_element_type=F32)


def vm():
    return pl.BlockSpec(memory_space=pltpu.VMEM)


def heads_of(ref, first, count):
    return jnp.concatenate(
        [ref[:, (first + g) * DH : (first + g + 1) * DH] for g in range(count)], axis=0
    )


def visible_mask(tokens, group, full, seq_index):
    shape = (group, tokens, full)
    pos = lax.broadcasted_iota(jnp.int32, shape, 1) + seq_index * tokens
    key = lax.broadcasted_iota(jnp.int32, shape, 2)
    return (key <= pos).reshape(group * tokens, full)


def attend_kernel(group, residual, q, kv, att, log_total, inv_rms, normed):
    tokens = q.shape[0]
    full = kv.shape[0]
    kv_heads = kv.shape[1] // (2 * DH)
    visible = visible_mask(tokens, group, full, lax.axis_index("seq"))
    scale = 1.0 / math.sqrt(DH)
    for k in range(kv_heads):
        qh = heads_of(q, k * group, group)
        kh = kv[:, k * DH : (k + 1) * DH]
        vh = kv[:, (kv_heads + k) * DH : (kv_heads + k + 1) * DH]
        scores = jnp.where(visible, dot(qh, kh, 1, 1) * scale, neg_big)
        top = jnp.max(scores, axis=1, keepdims=True)
        weights = jnp.exp(scores - top)
        total = jnp.sum(weights, axis=1, keepdims=True)
        out = (dot(weights.astype(BF), vh, 1, 0) / total).astype(BF)
        logs = top + jnp.log(total)
        for g in range(group):
            h = k * group + g
            att[:, h * DH : (h + 1) * DH] = out[g * tokens : (g + 1) * tokens]
            log_total[:, h : h + 1] = logs[g * tokens : (g + 1) * tokens]
    hidden = residual[...].astype(F32) + att[...].astype(F32)
    inv = lax.rsqrt(jnp.mean(hidden * hidden, axis=1, keepdims=True) + norm_eps)
    inv_rms[...] = inv
    normed[...] = (hidden * inv).astype(BF)


def attend(residual, q, kv, group):
    tokens, width = q.shape
    heads = width // DH
    return pl.pallas_call(
        functools.partial(attend_kernel, group),
        out_shape=(
            jax.ShapeDtypeStruct((tokens, width), BF),
            jax.ShapeDtypeStruct((tokens, heads), F32),
            jax.ShapeDtypeStruct((tokens, 1), F32),
            jax.ShapeDtypeStruct((tokens, width), BF),
        ),
        in_specs=[vm()] * 3,
        out_specs=(vm(),) * 4,
        compiler_params=pltpu.CompilerParams(vmem_limit_bytes=VMEM_LIMIT),
        cost_estimate=pl.CostEstimate(
            flops=4 * tokens * kv.shape[0] * width,
            bytes_accessed=8 * tokens * width + 2 * kv.size,
            transcendentals=heads * tokens * kv.shape[0],
        ),
        name="attend",
    )(residual, q, kv)


def attend_rows(group, residual, q, kv, att, log_total, inv_rms, normed):
    tokens = q.shape[0]
    full = kv.shape[0]
    kv_heads = kv.shape[1] // (2 * DH)
    visible = visible_mask(tokens, group, full, lax.axis_index("seq"))
    scale = 1.0 / math.sqrt(DH)
    for k in range(kv_heads):
        qh = heads_of(q, k * group, group)
        kh = kv[:, k * DH : (k + 1) * DH]
        vh = kv[:, (kv_heads + k) * DH : (kv_heads + k + 1) * DH]
        scores = jnp.where(visible, dot(qh, kh, 1, 1) * scale, neg_big)
        top = jnp.max(scores, axis=1, keepdims=True)
        weights = jnp.exp(scores - top)
        total = jnp.sum(weights, axis=1, keepdims=True)
        out = (dot(weights.astype(BF), vh, 1, 0) / total).astype(BF)
        logs = top + jnp.log(total)
        for g in range(group):
            h = k * group + g
            att[:, h * DH : (h + 1) * DH] = out[g * tokens : (g + 1) * tokens]
            log_total[:, h : h + 1] = logs[g * tokens : (g + 1) * tokens]
    hidden = residual[...].astype(F32) + att[...].astype(F32)
    inv = lax.rsqrt(jnp.mean(hidden * hidden, axis=1, keepdims=True) + norm_eps)
    inv_rms[...] = inv
    normed[...] = (hidden * inv).astype(BF)


def front_kernel(
    group,
    seqs,
    residual,
    q,
    kv_mine,
    table,
    grads,
    gate_weight,
    up_weight,
    down_weight,
    att,
    log_total,
    inv_rms,
    token_dot,
    input_sum,
    out_sum,
    kv_all,
    grads_all,
    normed_all,
    tables,
    rows_cols,
    pulls_cols,
    gate_all,
    up_all,
    mixed_all,
    input_part,
    out_part,
    kv,
    normed,
    gate_w,
    up_w,
    down_w,
    tabs,
    mix,
    slot,
    held,
    spare,
    pair_sum,
    line_sum,
    last_sum,
    rows,
    pulls,
    raw,
    gate_pre,
    up_pre,
    gate_grad,
    up_grad,
    mixed,
    local_sem,
    weight_sem,
    out_sem,
    part_sem,
    sum_sem,
    kv_sem,
    line_sem,
    plane_sem,
    table_line_sem,
    table_plane_sem,
):
    z = lax.axis_index("seq")
    e = lax.axis_index("expert")
    c, x, y = lax.rem(e, 2), lax.rem(e // 2, 2), e // 4
    tokens = q.shape[0]
    half = tokens // 2
    sibling = {"expert": e + 1 - 2 * c}
    across_x = {"expert": e + 2 - 4 * x}
    across_y = {"expert": e + 4 - 8 * y}
    above, below = {"seq": z + 1}, {"seq": z - 1}
    top = seqs - 1
    arrays = (grads_all, normed_all)
    sends = []

    def copy_of(view, sems, device):
        return pltpu.make_async_remote_copy(
            src_ref=view,
            dst_ref=view,
            send_sem=sems.at[0],
            recv_sem=sems.at[1],
            device_id=device,
            device_id_type=MESH,
        )

    def send(guard, view, sems, device):
        copy_of(view(), sems(), device).start()
        sends.append((guard, lambda: copy_of(view(), sems(), device).wait_send()))

    def arrived(view, sems):
        copy_of(view, sems, sibling).wait_recv()

    def under(guard, body):
        if guard is True:
            body()
        else:
            pl.when(guard)(body)

    def plane(k):
        d = (k + 1) // 2
        return z if k == 0 else (z - d if k % 2 else z + d)

    def present(k):
        d = (k + 1) // 2
        return True if k == 0 else (z >= d if k % 2 else z + d <= top)

    def forwarded(k):
        d = (k + 1) // 2
        return z + 1 <= top if k % 2 else z >= 1

    def both(a, b):
        return b if a is True else (a if b is True else jnp.logical_and(a, b))

    def line_start(ref, sems, k):
        guard = both(present(k - 2) if k > 2 else True, forwarded(k))

        def block():
            return ref.at[plane(k - 2) if k > 2 else z, y, x, c]

        under(guard, lambda: send(guard, block, lambda: sems(k), above if k % 2 else below))

    def first(a, k):
        ref = arrays[a]

        def sems(i):
            return plane_sem.at[a, k, i]

        if k:

            def take():
                arrived(ref.at[plane(k), y, x, c], line_sem.at[a, k])
                if a == 0:
                    arrived(tables.at[plane(k), y, x, c], table_line_sem.at[k])

            under(present(k), take)
            if k + 2 <= 2 * top:
                line_start(ref, lambda j: line_sem.at[a, j], k + 2)
                if a == 0:
                    line_start(tables, lambda j: table_line_sem.at[j], k + 2)

        def start():
            send(k, lambda: ref.at[plane(k), y, x, c, :half], lambda: sems(0), across_x)
            send(k, lambda: ref.at[plane(k), y, x, c, half:], lambda: sems(1), across_y)
            if a == 0:
                send(
                    k,
                    lambda: tables.at[plane(k), y, x, c],
                    lambda: table_plane_sem.at[k, 0],
                    across_x,
                )

        under(present(k), start)

    def second(a, k):
        ref = arrays[a]

        def sems(i):
            return plane_sem.at[a, k, i]

        def step():
            p = plane(k)
            arrived(ref.at[p, y, 1 - x, c, :half], sems(0))
            send(k, lambda: ref.at[plane(k), y, :, c, :half], lambda: sems(2), across_y)
            arrived(ref.at[p, 1 - y, x, c, half:], sems(1))
            send(k, lambda: ref.at[plane(k), :, x, c, half:], lambda: sems(3), across_x)
            if a == 0:
                arrived(tables.at[p, y, 1 - x, c], table_plane_sem.at[k, 0])
                send(
                    k,
                    lambda: tables.at[plane(k), y, :, c],
                    lambda: table_plane_sem.at[k, 1],
                    across_y,
                )

        under(present(k), step)

    def third(a, k):
        ref = arrays[a]

        def sems(i):
            return plane_sem.at[a, k, i]

        def step():
            p = plane(k)
            arrived(ref.at[p, 1 - y, :, c, :half], sems(2))
            arrived(ref.at[p, :, 1 - x, c, half:], sems(3))
            send(k, lambda: ref.at[plane(k), :, :, c], lambda: sems(4), sibling)
            if a == 0:
                arrived(tables.at[p, 1 - y, :, c], table_plane_sem.at[k, 1])
                send(
                    k,
                    lambda: tables.at[plane(k), :, :, c],
                    lambda: table_plane_sem.at[k, 2],
                    sibling,
                )

        under(present(k), step)

    def fourth(a, k):
        def step():
            p = plane(k)
            arrived(arrays[a].at[p, :, :, 1 - c], plane_sem.at[a, k, 4])
            if a == 0:
                arrived(tables.at[p, :, :, 1 - c], table_plane_sem.at[k, 2])

        under(present(k), step)

    copies = [
        pltpu.make_async_copy(grads, grads_all.at[z, y, x, c], local_sem.at[0]),
        pltpu.make_async_copy(table, tables.at[z, y, x, c], local_sem.at[1]),
        pltpu.make_async_copy(kv_mine, kv.at[z], local_sem.at[2]),
    ]
    for copy in copies:
        copy.start()
    weights = [
        pltpu.make_async_copy(down_weight, down_w, weight_sem.at[0]),
        pltpu.make_async_copy(gate_weight, gate_w, weight_sem.at[1]),
        pltpu.make_async_copy(up_weight, up_w, weight_sem.at[2]),
    ]
    for copy in weights:
        copy.start()
    for j in range(1, seqs):

        @pl.when(j > z)
        def _():
            kv[j] = jnp.zeros(kv.shape[1:], BF)

    barrier = pltpu.get_barrier_semaphore()
    for device in (sibling, across_x, across_y):
        pl.semaphore_signal(barrier, inc=1, device_id=device, device_id_type=MESH)

    @pl.when(z < top)
    def _():
        pl.semaphore_signal(barrier, inc=1, device_id=above, device_id_type=MESH)

    @pl.when(z > 0)
    def _():
        pl.semaphore_signal(barrier, inc=1, device_id=below, device_id_type=MESH)

    pl.semaphore_wait(barrier, 3 + (z < top).astype(jnp.int32) + (z > 0).astype(jnp.int32))
    for copy in copies:
        copy.wait()

    def kv_start(d):
        guard = both(z >= d if d else True, z < top)
        under(guard, lambda: send(guard, lambda: kv.at[z - d], lambda: kv_sem.at[d + 1], above))

    def kv_take(d):
        @pl.when(z >= d)
        def _():
            arrived(kv.at[z - d], kv_sem.at[d])

    kv_start(0)
    line_start(grads_all, lambda j: line_sem.at[0, j], 2)
    line_start(tables, lambda j: table_line_sem.at[j], 2)
    line_start(tables, lambda j: table_line_sem.at[j], 1)
    first(0, 0)
    for d in range(1, seqs):
        kv_take(d)
        if d < top:
            kv_start(d)
        if d == 1:
            second(0, 0)
        if d == 2:
            third(0, 0)
    line_start(grads_all, lambda j: line_sem.at[0, j], 1)
    keys = kv[...].reshape(seqs * tokens, kv.shape[2])
    attend_rows(group, residual, q, keys, att, log_total, inv_rms, normed)
    keep = [
        pltpu.make_async_copy(normed, normed_all.at[z, y, x, c], local_sem.at[3]),
        pltpu.make_async_copy(kv, kv_all, local_sem.at[4]),
    ]
    for copy in keep:
        copy.start()
    keep[0].wait()
    line_start(normed_all, lambda j: line_sem.at[1, j], 1)
    line_start(normed_all, lambda j: line_sem.at[1, j], 2)
    first(1, 0)

    local = slot.shape[0]
    ranks = slot.shape[1]
    depth = rows.shape[1] // ranks

    def chosen(i, r):
        row = lax.broadcasted_iota(jnp.int32, (depth, tokens), 0)
        return slot[i, pl.ds(r, 1), :] == row

    def all_chosen(r):
        return jnp.concatenate(
            [chosen(i, r).astype(F32) for i in range(local)], axis=0
        ).astype(BF)

    def span(r):
        return pl.ds(pl.multiple_of(r * depth, depth), depth)

    def each_rank(body):
        lax.fori_loop(0, ranks, lambda r, carry: (body(r), carry)[1], 0)

    def place(r):
        return (r // 4, lax.rem(r // 2, 2), lax.rem(r, 2))

    def find_slots():
        before = (
            lax.broadcasted_iota(jnp.int32, (tokens, tokens), 0)
            < lax.broadcasted_iota(jnp.int32, (tokens, tokens), 1)
        ).astype(F32).astype(BF)
        for i in range(local):
            mine = jnp.concatenate(
                [tabs[r // 4, r // 2 % 2, r % 2, pl.ds(e * local + i, 1), :] for r in range(ranks)],
                axis=0,
            )
            routed = mine >= 0.0
            rank = dot(routed.astype(F32).astype(BF), before, 1, 0)
            mix[i] = mine
            slot[i] = jnp.where(routed, rank.astype(jnp.int32), -1)

    def pick_into(target, source):
        def body(r):
            found = dot(all_chosen(r), source[place(r)], 1, 0).astype(BF)
            for i in range(local):
                target[i, span(r), :] = found[i * depth : (i + 1) * depth]

        each_rank(body)

    def blend(i, dots):
        def body(r):
            at = span(r)
            hit = chosen(i, r)
            share = jnp.sum(jnp.where(hit, mix[i, pl.ds(r, 1), :], 0.0), axis=1, keepdims=True)
            g, u, w = gate_pre[at, :], up_pre[at, :], raw[i, at, :]
            sigmoid = jax.nn.sigmoid(g)
            silu = g * sigmoid
            act = silu * u
            act_grad = w * share
            gate_grad[i, at, :] = (act_grad * u * sigmoid * (1.0 + g * (1.0 - sigmoid))).astype(BF)
            up_grad[i, at, :] = (act_grad * silu).astype(BF)
            mixed[i, at, :] = (act * share).astype(BF)
            if dots:
                total = jnp.sum(act.astype(BF).astype(F32) * w, axis=1, keepdims=True)
                token_dot[r, i : i + 1, :] = jnp.sum(
                    jnp.where(hit, total, 0.0), axis=0, keepdims=True
                )

        each_rank(body)

    def spread(source, target):
        def body(r):
            stacked = jnp.concatenate([source[i, span(r), :] for i in range(local)], axis=0)
            target[place(r)] = dot(all_chosen(r), stacked, 0, 0).astype(BF)

        each_rank(body)

    share = rows_cols.shape[3]

    def kept(j):
        cols = pl.ds(pl.multiple_of(z * share, share), share)
        return [
            pltpu.make_async_copy(pulls.at[:, :, cols], pulls_cols.at[:, j], out_sem.at[j, 0]),
            pltpu.make_async_copy(rows.at[:, :, cols], rows_cols.at[:, j], out_sem.at[j, 1]),
            pltpu.make_async_copy(gate_grad, gate_all.at[:, j], out_sem.at[j, 2]),
            pltpu.make_async_copy(up_grad, up_all.at[:, j], out_sem.at[j, 3]),
            pltpu.make_async_copy(mixed, mixed_all.at[:, j], out_sem.at[j, 4]),
        ]

    part_outs = [
        pltpu.make_async_copy(held, input_part, part_sem.at[0]),
        pltpu.make_async_copy(spare, out_part, part_sem.at[1]),
    ]

    def hold(ref, target, sem):
        copy = pltpu.make_async_copy(ref, target, sem)
        copy.start()
        return copy

    def task_grads():
        fourth(0, 0)
        hold(tables.at[z], tabs, local_sem.at[1]).wait()
        copy = hold(grads_all.at[z], held, local_sem.at[0])
        find_slots()
        copy.wait()
        pick_into(pulls, held)
        kept(0)[0].start()

    def task_raw(i, ready):
        if ready:
            weights[0].wait()
        raw[i] = dot(pulls[i], down_w[i], 1, 1)

    def task_rows():
        fourth(1, 0)
        hold(normed_all.at[z], held, local_sem.at[0]).wait()
        pick_into(rows, held)
        kept(0)[1].start()
        weights[1].wait()
        weights[2].wait()

    def task_gate(i):
        gate_pre[...] = dot(rows[i], gate_w[i], 1, 1)

    def task_up(i):
        up_pre[...] = dot(rows[i], up_w[i], 1, 1)

    def task_input(i):
        if i == 0:
            kept(0)[0].wait()
            kept(0)[1].wait()
        rows[i] = (dot(gate_grad[i], gate_w[i], 1, 0) + dot(up_grad[i], up_w[i], 1, 0)).astype(BF)

    def task_out(i):
        pulls[i] = dot(mixed[i], down_w[i], 1, 0).astype(BF)

    def task_spread_input():
        for copy in kept(0)[2:]:
            copy.start()
        spread(rows, held)
        part_outs[0].start()

    def task_spread_out():
        spread(pulls, spare)
        part_outs[1].start()

    parts = ((held, input_part, input_sum), (spare, out_part, out_sum))
    pieces = 4

    def in_pieces(body):
        step = half // pieces

        def run(j, carry):
            body(pl.ds(pl.multiple_of(j * step, step), step), step)
            return carry

        lax.fori_loop(0, pieces, run, 0)

    def sum_pair_send(a):
        part_outs[a].wait()
        view = parts[a][1]
        pltpu.make_async_remote_copy(
            src_ref=view.at[:, :, 1 - c],
            dst_ref=pair_sum.at[a],
            send_sem=sum_sem.at[a, 0, 0],
            recv_sem=sum_sem.at[a, 0, 1],
            device_id=sibling,
            device_id_type=MESH,
        ).start()

    def sum_pair_take(a):
        arrived(pair_sum.at[a], sum_sem.at[a, 0])
        for yy in range(2):
            for xx in range(2):

                def body(at, step):
                    mine = parts[a][0][yy, xx, c, at, :].astype(F32)
                    pair_sum[a, yy, xx, at, :] = (
                        mine + pair_sum[a, yy, xx, at, :].astype(F32)
                    ).astype(BF)

                def both_halves(at, step):
                    body(at, step)
                    low = pl.ds(pl.multiple_of(half + at.start, step), step)
                    body(low, step)

                in_pieces(both_halves)

    def half_copies(a):
        return (
            pltpu.make_async_remote_copy(
                src_ref=pair_sum.at[a, :, 1 - x, :half],
                dst_ref=line_sum.at[a, 0],
                send_sem=sum_sem.at[a, 1, 0],
                recv_sem=sum_sem.at[a, 1, 1],
                device_id=across_x,
                device_id_type=MESH,
            ),
            pltpu.make_async_remote_copy(
                src_ref=pair_sum.at[a, 1 - y, :, half:],
                dst_ref=line_sum.at[a, 1],
                send_sem=sum_sem.at[a, 2, 0],
                recv_sem=sum_sem.at[a, 2, 1],
                device_id=across_y,
                device_id_type=MESH,
            ),
        )

    def last_copies(a):
        return tuple(
            pltpu.make_async_remote_copy(
                src_ref=line_sum.at[a, i, 1 - (y, x)[i]],
                dst_ref=last_sum.at[a, i],
                send_sem=sum_sem.at[a, 3 + i, 0],
                recv_sem=sum_sem.at[a, 3 + i, 1],
                device_id=(across_y, across_x)[i],
                device_id_type=MESH,
            )
            for i in range(2)
        )

    def sum_line_send(a):
        for copy in half_copies(a):
            copy.start()

    def sum_line_take(a):
        for copy in half_copies(a):
            copy.wait_recv()
        for j in range(2):

            def body(at, step):
                low = pl.ds(pl.multiple_of(half + at.start, step), step)
                line_sum[a, 0, j, at, :] = (
                    line_sum[a, 0, j, at, :].astype(F32) + pair_sum[a, j, x, at, :].astype(F32)
                ).astype(BF)
                line_sum[a, 1, j, at, :] = (
                    line_sum[a, 1, j, at, :].astype(F32) + pair_sum[a, y, j, low, :].astype(F32)
                ).astype(BF)

            in_pieces(body)

    def sum_last_send(a):
        for copy in last_copies(a):
            copy.start()

    def sum_last_take(a):
        for copy in last_copies(a):
            copy.wait_recv()

        def body(at, step):
            low = pl.ds(pl.multiple_of(half + at.start, step), step)
            total = parts[a][2]
            total[at, :] = (
                line_sum[a, 0, y, at, :].astype(F32) + last_sum[a, 0, at, :].astype(F32)
            ).astype(BF)
            total[low, :] = (
                line_sum[a, 1, x, at, :].astype(F32) + last_sum[a, 1, at, :].astype(F32)
            ).astype(BF)

        in_pieces(body)

    def sum_end(a):
        view = parts[a][1].at[:, :, 1 - c]
        copy_of(view, sum_sem.at[a, 0], sibling).wait_send()
        for copy in half_copies(a) + last_copies(a):
            copy.wait_send()

    far = []
    for j in range(1, seqs):
        at, seen = 0, 0
        for k in range(1, 2 * seqs - 1):
            here = present(k).astype(jnp.int32)
            at = at + k * here * jnp.equal(seen, j - 1).astype(jnp.int32)
            seen = seen + here
        far.append(at)

    def far_plane(j):
        k = far[j - 1]
        return k, z + (k + 1) // 2 * (1 - 2 * lax.rem(k, 2))

    def task_far(j):
        k, p = far_plane(j)
        arrived(arrays[0].at[p, :, :, 1 - c], plane_sem.at[0, k, 4])
        arrived(tables.at[p, :, :, 1 - c], table_plane_sem.at[k, 2])
        loads = [
            hold(tables.at[p], tabs, local_sem.at[1]),
            hold(grads_all.at[p], held, local_sem.at[0]),
        ]
        arrived(arrays[1].at[p, :, :, 1 - c], plane_sem.at[1, k, 4])
        loads.append(hold(normed_all.at[p], spare, local_sem.at[3]))
        loads[0].wait()
        find_slots()
        for copy in kept(j - 1)[2:] if j == 1 else kept(j - 1):
            copy.wait()
        loads[1].wait()
        pick_into(pulls, held)
        kept(j)[0].start()
        loads[2].wait()
        pick_into(rows, spare)
        kept(j)[1].start()

    def task_far_units(j, i):
        task_raw(i, False)
        task_gate(i)
        task_up(i)
        blend(i, False)
        if i == local - 1:
            for copy in kept(j)[2:]:
                copy.start()

    task_grads()
    task_raw(0, True)
    second(1, 0)
    order = []
    for d in range(1, seqs):
        for a in range(2):
            order += [(a, 2 * d - 1), (a, 2 * d)]
    tasks = [(0, functools.partial(task_raw, i, False)) for i in range(1, local)]
    tasks += [(0, lambda: third(1, 0)), (0, task_rows)]
    for i in range(local):
        tasks += [
            (0, functools.partial(task_gate, i)),
            (0, functools.partial(task_up, i)),
            (0, functools.partial(blend, i, True)),
            (0, functools.partial(task_input, i)),
            (0, functools.partial(task_out, i)),
        ]
    tasks += [(0, task_spread_input), (0, task_spread_out)]
    sums = []
    for group_of in (
        (sum_pair_send,),
        (sum_pair_take, sum_line_send),
        (sum_line_take, sum_last_send),
        (sum_last_take,),
    ):
        for a in range(2):
            sums.append([(0, functools.partial(step, a)) for step in group_of])
    tasks += sums[0] + sums[1] + sums[2] + sums[3]
    sums = sums[4:]
    for j in range(1, seqs):
        least = 4 * (2 * j) // 2 + 3
        tasks.append((least, functools.partial(task_far, j)))
        for i in range(local):
            tasks.append((least, functools.partial(task_far_units, j, i)))
            if sums:
                tasks += sums.pop(0)
    for rest in sums:
        tasks += rest
    i = 0
    while i < len(order) + 4 or tasks:
        if i < len(order):
            first(*order[i])
        if 0 <= i - 2 < len(order):
            second(*order[i - 2])
        if 0 <= i - 4 < len(order):
            third(*order[i - 4])
        for _ in range(TASKS):
            if tasks and tasks[0][0] <= i:
                tasks.pop(0)[1]()
        i += 1
    for copy in kept(seqs - 1):
        copy.wait()
    for a in range(2):
        sum_end(a)
    keep[1].wait()
    for guard, finish in sends:
        under(present(guard) if isinstance(guard, int) else guard, finish)


def front(residual, q, kv_mine, table, grads, weights, group, seqs, ranks, depth):
    tokens, width = q.shape
    heads = width // DH
    slots = 2 * seqs - 1
    local, hidden, _ = weights[0].shape
    any_space = pl.BlockSpec(memory_space=pl.ANY)
    dma = pltpu.SemaphoreType.DMA
    picked = (local, ranks * depth, width)
    units = (local, ranks * depth, hidden)
    plane = (2, 2, 2, tokens, width)
    return pl.pallas_call(
        functools.partial(front_kernel, group, seqs),
        out_shape=(
            jax.ShapeDtypeStruct((tokens, width), BF),
            jax.ShapeDtypeStruct((tokens, heads), F32),
            jax.ShapeDtypeStruct((tokens, 1), F32),
            jax.ShapeDtypeStruct((ranks, local, tokens), F32),
            jax.ShapeDtypeStruct((tokens, width), BF),
            jax.ShapeDtypeStruct((tokens, width), BF),
            jax.ShapeDtypeStruct((seqs,) + kv_mine.shape, BF),
            jax.ShapeDtypeStruct((seqs,) + plane, BF),
            jax.ShapeDtypeStruct((seqs,) + plane, BF),
            jax.ShapeDtypeStruct((seqs, 2, 2, 2) + table.shape, F32),
            jax.ShapeDtypeStruct((local, seqs, ranks * depth, width // seqs), BF),
            jax.ShapeDtypeStruct((local, seqs, ranks * depth, width // seqs), BF),
            jax.ShapeDtypeStruct((local, seqs) + units[1:], BF),
            jax.ShapeDtypeStruct((local, seqs) + units[1:], BF),
            jax.ShapeDtypeStruct((local, seqs) + units[1:], BF),
            jax.ShapeDtypeStruct(plane, BF),
            jax.ShapeDtypeStruct(plane, BF),
        ),
        in_specs=[vm()] * 5 + [any_space] * 3,
        out_specs=(vm(),) * 6 + (any_space,) * 11,
        scratch_shapes=[
            pltpu.VMEM((seqs,) + kv_mine.shape, BF),
            pltpu.VMEM((tokens, width), BF),
            pltpu.VMEM(weights[0].shape, BF),
            pltpu.VMEM(weights[1].shape, BF),
            pltpu.VMEM(weights[2].shape, BF),
            pltpu.VMEM((2, 2, 2) + table.shape, F32),
            pltpu.VMEM((local, ranks, tokens), F32),
            pltpu.VMEM((local, ranks, tokens), jnp.int32),
            pltpu.VMEM(plane, BF),
            pltpu.VMEM(plane, BF),
            pltpu.VMEM((2, 2, 2, tokens, width), BF),
            pltpu.VMEM((2, 2, 2, tokens // 2, width), BF),
            pltpu.VMEM((2, 2, tokens // 2, width), BF),
            pltpu.VMEM(picked, BF),
            pltpu.VMEM(picked, BF),
            pltpu.VMEM(units, F32),
            pltpu.VMEM(units[1:], F32),
            pltpu.VMEM(units[1:], F32),
            pltpu.VMEM(units, BF),
            pltpu.VMEM(units, BF),
            pltpu.VMEM(units, BF),
            dma((5,)),
            dma((3,)),
            dma((seqs, 5)),
            dma((2,)),
            dma((2, 5, 2)),
            dma((seqs, 2)),
            dma((2, slots, 2)),
            dma((2, slots, 5, 2)),
            dma((slots, 2)),
            dma((slots, 3, 2)),
        ],
        compiler_params=pltpu.CompilerParams(
            collective_id=0, has_side_effects=True, vmem_limit_bytes=FRONT_LIMIT
        ),
        cost_estimate=pl.CostEstimate(
            flops=4 * tokens * seqs * tokens * width + (6 * seqs + 6) * local * ranks * depth * width * hidden,
            bytes_accessed=32 * seqs * tokens * width,
            transcendentals=heads * tokens * seqs * tokens,
        ),
        name="front",
    )(residual, q, kv_mine, table, grads, *weights)


def attend_back_kernel(
    group, residual, q, kv, att, log_total, inv_rms, grad_out, normed_grad, res_grad, q_grad, kv_part
):
    tokens = q.shape[0]
    full = kv.shape[0]
    kv_heads = kv.shape[1] // (2 * DH)
    scale = 1.0 / math.sqrt(DH)
    inv = inv_rms[...]
    normed = (residual[...].astype(F32) + att[...].astype(F32)) * inv
    ngrad = normed_grad[...].astype(F32)
    dot_mean = jnp.mean(ngrad * normed, axis=1, keepdims=True)
    res_grad[...] = (grad_out[...].astype(F32) + inv * (ngrad - normed * dot_mean)).astype(BF)
    visible = visible_mask(tokens, group, full, lax.axis_index("seq"))
    for k in range(kv_heads):
        qh = heads_of(q, k * group, group)
        oh = heads_of(att, k * group, group)
        gh = heads_of(res_grad, k * group, group)
        logs = jnp.concatenate(
            [log_total[:, k * group + g : k * group + g + 1] for g in range(group)], axis=0
        )
        kh = kv[:, k * DH : (k + 1) * DH]
        vh = kv[:, (kv_heads + k) * DH : (kv_heads + k + 1) * DH]
        scores = jnp.where(visible, dot(qh, kh, 1, 1) * scale, neg_big)
        probs = jnp.exp(scores - logs)
        delta = jnp.sum(gh.astype(F32) * oh.astype(F32), axis=1, keepdims=True)
        pgrad = dot(gh, vh, 1, 1)
        sgrad = (probs * (pgrad - delta)).astype(BF)
        dq = (dot(sgrad, kh, 1, 0) * scale).astype(BF)
        for g in range(group):
            h = k * group + g
            q_grad[:, h * DH : (h + 1) * DH] = dq[g * tokens : (g + 1) * tokens]
        kv_part[:, k * DH : (k + 1) * DH] = (dot(sgrad, qh, 0, 0) * scale).astype(BF)
        kv_part[:, (kv_heads + k) * DH : (kv_heads + k + 1) * DH] = dot(
            probs.astype(BF), gh, 0, 0
        ).astype(BF)


def attend_back(group, residual, q, kv, att, log_total, inv_rms, grad_out, normed_grad):
    tokens, width = q.shape
    return pl.pallas_call(
        functools.partial(attend_back_kernel, group),
        out_shape=(
            jax.ShapeDtypeStruct((tokens, width), BF),
            jax.ShapeDtypeStruct((tokens, width), BF),
            jax.ShapeDtypeStruct(kv.shape, BF),
        ),
        in_specs=[vm()] * 8,
        out_specs=(vm(),) * 3,
        compiler_params=pltpu.CompilerParams(vmem_limit_bytes=VMEM_LIMIT),
        cost_estimate=pl.CostEstimate(
            flops=10 * tokens * kv.shape[0] * width,
            bytes_accessed=14 * tokens * width + 4 * kv.size,
            transcendentals=tokens * kv.shape[0] * (width // DH),
        ),
        name="attend_back",
    )(residual, q, kv, att, log_total, inv_rms, grad_out, normed_grad)


def pick_kernel(seq_index, slot, rows, picked):
    local = slot.shape[2]
    depth = picked.shape[1]
    tokens = rows.shape[2]
    row = lax.broadcasted_iota(jnp.int32, (depth, tokens), 0)
    for e in range(local):
        chosen = (slot[0, 0, e : e + 1, :] == row).astype(F32).astype(BF)
        picked[e] = dot(chosen, rows[0, 0], 1, 0).astype(BF)


def pick_rows(gathered, slot, seq_index, first, planes, depth):
    seqs, ranks, tokens, width = gathered.shape
    local = slot.shape[2]
    count = planes * ranks

    def source(i, s):
        return (lax.rem(s[0] + first + i // ranks, seqs), lax.rem(i, ranks), 0, 0)

    return pl.pallas_call(
        pick_kernel,
        out_shape=jax.ShapeDtypeStruct((local, count * depth, width), BF),
        grid_spec=pltpu.PrefetchScalarGridSpec(
            num_scalar_prefetch=1,
            grid=(count,),
            in_specs=[
                pl.BlockSpec((1, 1, local, tokens), source),
                pl.BlockSpec((1, 1, tokens, width), source),
            ],
            out_specs=pl.BlockSpec((local, depth, width), lambda i, s: (0, i, 0)),
        ),
        compiler_params=pltpu.CompilerParams(vmem_limit_bytes=16 * 1024 * 1024),
        cost_estimate=pl.CostEstimate(
            flops=2 * local * count * depth * tokens * width,
            bytes_accessed=2 * count * (tokens + local * depth) * width,
            transcendentals=0,
        ),
        name="pick_rows",
    )(seq_index, slot, gathered)


def spread_kernel(slot, rows, out):
    ranks, local, tokens = slot.shape
    depth = rows.shape[1]
    row = lax.broadcasted_iota(jnp.int32, (depth, tokens), 0)
    total = None
    for e in range(local):
        chosen = (slot[0, e : e + 1, :] == row).astype(F32).astype(BF)
        part = dot(chosen, rows[e], 0, 0)
        total = part if total is None else total + part
    out[0] = total.astype(BF)


def spread_rows(rows, slot):
    ranks, local, tokens = slot.shape
    width = rows.shape[2]
    depth = rows.shape[1] // ranks
    return pl.pallas_call(
        spread_kernel,
        out_shape=jax.ShapeDtypeStruct((ranks, tokens, width), BF),
        grid=(ranks,),
        in_specs=[
            pl.BlockSpec((1, local, tokens), lambda i: (i, 0, 0)),
            pl.BlockSpec((local, depth, width), lambda i: (0, i, 0)),
        ],
        out_specs=pl.BlockSpec((1, tokens, width), lambda i: (i, 0, 0)),
        compiler_params=pltpu.CompilerParams(vmem_limit_bytes=16 * 1024 * 1024),
        cost_estimate=pl.CostEstimate(
            flops=2 * local * ranks * depth * tokens * width,
            bytes_accessed=2 * ranks * (tokens + local * depth) * width,
            transcendentals=0,
        ),
        name="spread_rows",
    )(slot, rows)


def hidden_units(rows, grads, mix, gate_weight, up_weight, down_weight):
    gate_pre = jnp.einsum("erd,edf->erf", rows, gate_weight, preferred_element_type=F32)
    up_pre = jnp.einsum("erd,edf->erf", rows, up_weight, preferred_element_type=F32)
    raw = jnp.einsum("erd,efd->erf", grads, down_weight, preferred_element_type=F32)
    sigmoid = jax.nn.sigmoid(gate_pre)
    silu = gate_pre * sigmoid
    act = silu * up_pre
    act_grad = raw * mix[:, :, None]
    gate_grad = (act_grad * up_pre * sigmoid * (1.0 + gate_pre * (1.0 - sigmoid))).astype(BF)
    up_grad = (act_grad * silu).astype(BF)
    mixed = (act * mix[:, :, None]).astype(BF)
    return (gate_grad, up_grad, mixed, act, raw)


def on_device(
    residual,
    queries,
    key_input,
    value_input,
    routes,
    mix_weights,
    gate_weight,
    up_weight,
    down_weight,
    grad_out,
):
    tokens = residual.shape[1]
    width = residual.shape[2]
    kv_width = key_input.shape[2]
    group = queries.shape[2] // kv_width
    local = gate_weight.shape[0]
    ranks = lax.axis_size("expert")
    seqs = lax.axis_size("seq")
    experts = local * ranks
    top_count = routes.shape[2]
    capacity = tokens * top_count * 5 // (4 * experts)
    depth = -(-capacity // 16) * 16
    both = ("seq", "expert")
    both_size = seqs * ranks
    seq_index = lax.axis_index("seq")
    rank_index = lax.axis_index("expert")
    seq_array = seq_index.astype(jnp.int32).reshape(1)

    kv_mine = jnp.concatenate(
        [key_input.reshape(tokens, kv_width), value_input.reshape(tokens, kv_width)], axis=1
    )
    expert_ids = jnp.arange(experts, dtype=jnp.int32)
    picked = routes.reshape(tokens, top_count)
    mix_rows = mix_weights.reshape(tokens, top_count)
    hit = picked[None, :, :] == expert_ids[:, None, None]
    table = jnp.sum(jnp.where(hit, mix_rows[None], 0.0), axis=2) - (
        1.0 - jnp.sum(hit.astype(F32), axis=2)
    )
    grad_rows = grad_out.reshape(tokens, width)
    q = queries.reshape(tokens, width)
    res = residual.reshape(tokens, width)
    weights = (gate_weight, up_weight, down_weight)
    paired = ranks == 8 and 2 * both_size * grad_rows.size <= GATHER_BYTES
    if paired:
        (
            att,
            log_total,
            inv_rms,
            token_dot,
            normed_grad,
            routed_out,
            kv,
            _,
            _,
            _,
            rows_cols,
            grads_cols,
            gate_rows,
            up_rows,
            mixed_rows,
            _,
            _,
        ) = front(
            res,
            q,
            kv_mine,
            table,
            grad_rows,
            (jnp.swapaxes(gate_weight, 1, 2), jnp.swapaxes(up_weight, 1, 2), down_weight),
            group,
            seqs,
            ranks,
            depth,
        )
        kv = kv.reshape(seqs * tokens, 2 * kv_width)

        def outer(a, b):
            a = a.reshape(local, seqs * ranks * depth, a.shape[3])
            b = b.reshape(local, seqs * ranks * depth, b.shape[3])
            return jnp.einsum("erm,ern->emn", a, b, preferred_element_type=F32).astype(BF)

        gate_share = outer(rows_cols, gate_rows)
        up_share = outer(rows_cols, up_rows)
        down_share = outer(mixed_rows, grads_cols)
    else:
        kv = lax.all_gather(kv_mine, "seq", axis=0, tiled=True)

        tables = lax.all_gather(table, both, axis=0, tiled=False)
        mine = lax.dynamic_slice_in_dim(tables, rank_index * local, local, axis=1)
        routed = mine >= 0.0
        before = jnp.triu(jnp.ones((tokens, tokens), BF), 1)
        rank = jnp.einsum("bet,tu->beu", routed.astype(BF), before, preferred_element_type=F32)
        slot = jnp.where(routed, rank.astype(jnp.int32), -1)
        slot = slot.reshape(seqs, ranks, local, tokens)
        mine = mine.reshape(seqs, ranks, local, tokens)

        grads_all = lax.all_gather(grad_rows, both, axis=0, tiled=True)
        grads_all = grads_all.reshape(seqs, ranks, tokens, width)

        att, log_total, inv_rms, normed_bf = attend(res, q, kv, group)
        grads_own = pick_rows(grads_all, slot, seq_array, 0, 1, depth)
        grads_far = pick_rows(grads_all, slot, seq_array, 1, seqs - 1, depth)
        if 2 * grads_all.size > GATHER_BYTES:
            normed_bf, grads_own, grads_far = lax.optimization_barrier(
                (normed_bf, grads_own, grads_far)
            )
        normed_all = lax.all_gather(normed_bf, both, axis=0, tiled=True)
        normed_all = normed_all.reshape(seqs, ranks, tokens, width)

        slot_turned = jnp.roll(slot, -seq_index, axis=0)
        mix_turned = jnp.roll(mine, -seq_index, axis=0)
        here = slot_turned[..., None, :] == jnp.arange(depth, dtype=jnp.int32)[:, None]
        mix_slot = jnp.sum(jnp.where(here, mix_turned[..., None, :], 0.0), axis=4)
        mix_slot = jnp.transpose(mix_slot, (2, 0, 1, 3)).reshape(local, seqs * ranks * depth)
        own = ranks * depth

        rows_own = pick_rows(normed_all, slot, seq_array, 0, 1, depth)
        rows_far = pick_rows(normed_all, slot, seq_array, 1, seqs - 1, depth)
        gate_own, up_own, mixed_own, act_own, raw_own = hidden_units(
            rows_own, grads_own, mix_slot[:, :own], *weights
        )
        input_grad = (
            jnp.einsum("erf,edf->erd", gate_own, gate_weight, preferred_element_type=F32)
            + jnp.einsum("erf,edf->erd", up_own, up_weight, preferred_element_type=F32)
        ).astype(BF)
        slot_own = slot_turned[0]
        input_part = spread_rows(input_grad, slot_own).reshape(ranks * tokens, width)
        normed_grad = lax.psum_scatter(input_part, "expert", scatter_dimension=0, tiled=True)

        expert_out = jnp.einsum(
            "erf,efd->erd", mixed_own, down_weight, preferred_element_type=F32
        ).astype(BF)
        out_part = spread_rows(expert_out, slot_own).reshape(ranks * tokens, width)
        routed_out = lax.psum_scatter(out_part, "expert", scatter_dimension=0, tiled=True)
        pair_dot = jnp.sum(act_own.astype(BF).astype(F32) * raw_own, axis=2)
        pair_dot = pair_dot.reshape(local, ranks, depth)
        token_dot = jnp.sum(
            jnp.where(here[0], jnp.transpose(pair_dot, (1, 0, 2))[..., None], 0.0), axis=2
        )
        gate_far, up_far, mixed_far, _, _ = hidden_units(
            rows_far, grads_far, mix_slot[:, own:], *weights
        )
        share = width // seqs

        def columns(array):
            return lax.dynamic_slice_in_dim(array, seq_index * share, share, axis=2)

        def outer(a_own, a_far, b_own, b_far):
            return (
                jnp.einsum("erm,ern->emn", a_own, b_own, preferred_element_type=F32)
                + jnp.einsum("erm,ern->emn", a_far, b_far, preferred_element_type=F32)
            ).astype(BF)

        cols_own, cols_far = columns(rows_own), columns(rows_far)
        gate_share = outer(cols_own, cols_far, gate_own, gate_far)
        up_share = outer(cols_own, cols_far, up_own, up_far)
        down_share = outer(mixed_own, mixed_far, columns(grads_own), columns(grads_far))
    hidden = res.astype(F32) + att.astype(F32)
    layer_out = (hidden + routed_out.astype(F32)).astype(BF)

    dots = lax.all_to_all(token_dot, "expert", split_axis=0, concat_axis=0, tiled=True)
    dots = dots.reshape(experts, tokens)
    mix_grad = jnp.sum(jnp.where(hit, dots[:, :, None], 0.0), axis=0)

    res_grad, q_grad, kv_part = attend_back(
        group, res, q, kv, att, log_total, inv_rms, grad_rows, normed_grad
    )
    kv_share = lax.psum_scatter(kv_part, "seq", scatter_dimension=0, tiled=True)
    return (
        layer_out.reshape(1, tokens, width),
        res_grad.reshape(1, tokens, width),
        q_grad.reshape(1, tokens, width),
        kv_share[:, :kv_width].reshape(1, tokens, kv_width),
        kv_share[:, kv_width:].reshape(1, tokens, kv_width),
        mix_grad.reshape(1, tokens, top_count),
        gate_share,
        up_share,
        down_share,
    )


def solution(mesh):
    rows = P("expert", "seq", None)
    weight = P("expert", None, None)
    return jax.shard_map(
        on_device,
        mesh=mesh,
        in_specs=(rows,) * 6 + (weight,) * 3 + (rows,),
        out_specs=(rows,) * 8 + (P("expert", None, "seq"),),
        check_vma=False,
    )
```
